32 devices in a mesh: batch: 16 (over z, y, core), head: 2 (over x).
Axes of the slice: x: 2, y: 2, z: 4, core: 2. Of those that a mesh axis runs over, the one named last changes fastest.
Arguments:
- layer_in: bfloat16 [16384, 1024], P('batch'), may hold values from -6 to 6
- slot_stretch: int32 [32], replicated, may hold values from 0 to 31, each once
- seq_stretches: int32 [8], replicated, may hold values from 1 to 6, 32 in all
- w_qkv: bfloat16 [1024, 3, 1024], P(None, None, 'head'), may hold values from -0.1875 to 0.1875
- qv_bias: bfloat16 [2, 1024], P(None, 'head'), may hold values from -0.29882812 to 0.29882812
- w_out: bfloat16 [1024, 1024], P('head'), may hold values from -3 to 3
- out_bias: bfloat16 [1024], replicated, may hold values from -3 to 3
- norm1_gain: bfloat16 [1024], replicated, may hold values from 0.099609375 to 1.8984375
- norm1_shift: bfloat16 [1024], replicated, may hold values from -2 to 2
- w_up: bfloat16 [1024, 4096], P(None, 'head'), may hold values from -0.1875 to 0.1875
- up_bias: bfloat16 [4096], P('head'), may hold values from -3 to 3
- w_down: bfloat16 [4096, 1024], P('head'), may hold values from -0.09375 to 0.09375
- down_bias: bfloat16 [1024], replicated, may hold values from -3 to 3
- norm2_gain: bfloat16 [1024], replicated, may hold values from 0.099609375 to 1.8984375
- norm2_shift: bfloat16 [1024], replicated, may hold values from -2 to 2
- cotangent: bfloat16 [16384, 1024], P('batch'), may hold values from -6 to 6
Outputs:
- layer_out: bfloat16 [16384, 1024], P('batch')
- grad_in: float32 [16384, 1024], P('batch', 'head')
- grad_w_qkv: float32 [1024, 3, 1024], P(None, None, 'head')
- grad_qv_bias: float32 [2, 1024], P(None, 'head')
- grad_w_out: float32 [1024, 1024], P('head')
- grad_out_bias: float32 [1024], replicated
- grad_norm1_gain: float32 [1024], replicated
- grad_norm1_shift: float32 [1024], replicated
- grad_w_up: float32 [1024, 4096], P(None, 'head')
- grad_up_bias: float32 [4096], P('head')
- grad_w_down: float32 [4096, 1024], P('head')
- grad_down_bias: float32 [1024], replicated
- grad_norm2_gain: float32 [1024], replicated
- grad_norm2_shift: float32 [1024], replicated
The draws below stay inside these ranges and needn't reach their ends.
Inputs may be any that keep to these rules, and one draw needn't show every extreme that they name: `seq_stretches`: lengths in stretches of 512 tokens, in the order in which stretches are numbered; they sum to 32 and the largest is exactly 6. Slot s, rows s * 512 to s * 512 + 511, holds stretch slot_stretch[s]; every stretch is in exactly one slot.
All inputs are finite; a program needn't handle non-finite values.
Results may differ from the reference program's by a relative error of at most 0.02.
Values may be sent and summed in bfloat16 or wider, within the bound.
No kernel may reach another device: no remote copies, remote signals or barrier semaphores. Data moves between devices by JAX's collectives and lax.ppermute only.
A program may use at most 320 MiB of HBM per device.

```python
import math
import jax
import jax.numpy as jnp
import numpy as np
from jax import lax

D = 1024
H = 16
HD = 64
FF = 4096
CH = 512
MAXCH = 6
STRETCHES = 32
NSEQ = 8
TOKENS = 16384


def block_scale(key, dims, cuts, smallest, largest):
    level = 1.0
    for dim, shards_of in cuts:
        steps = jax.random.uniform(jax.random.fold_in(jax.random.fold_in(key, 6), dim), (shards_of,), jnp.float32, smallest / len(cuts), largest / len(cuts))
        level = level * jnp.repeat(jnp.exp(steps), dims[dim] // shards_of).reshape((-1,) + (1,) * (len(dims) - 1 - dim))
    return level


def profile(amount, total, most, skew):
    weights = [(1 << 20) // math.isqrt(grade ** skew) + 1 for grade in range(2, amount + 1)]
    rest, holding = total - most - (amount - 1), [1] * (amount - 1)
    while rest > 0:
        candidates = [i for i in range(amount - 1) if holding[i] < most]
        whole, left = sum([weights[i] for i in candidates]), rest
        for i in candidates:
            addition = min(most - holding[i], max(1, left * weights[i] // whole), rest)
            holding[i] = holding[i] + addition
            rest = rest - addition
    return np.array([most] + holding)


def ragged_sizes(stream_key, count, total, reach, lean):
    if count == 2:
        one = jax.random.randint(stream_key, (), max(1, total - reach), min(reach, total - 1) + 1)
        return jnp.stack([one, total - one])
    sizes = jnp.asarray(profile(count, total, reach, lean), jnp.int32)
    pairs = (count - 1) // 2
    source_of, sink = sizes[1:1 + 2 * pairs:2], sizes[2:2 + 2 * pairs:2]
    slack = jnp.minimum(source_of - 1, reach - sink)
    shifted = jax.random.randint(jax.random.fold_in(stream_key, 1), (pairs,), 0, 1 << 20) % (slack + 1)
    sizes = sizes.at[1:1 + 2 * pairs:2].set(source_of - shifted).at[2:2 + 2 * pairs:2].set(sink + shifted)
    return sizes[jax.random.permutation(jax.random.fold_in(stream_key, 2), count)]


def noise(key, dims, deviation, most, shards=(), held_as=jnp.bfloat16):
    level = block_scale(key, dims, shards, -0.22, 0.18) if shards else 1.0
    array = jax.random.normal(key, dims, jnp.float32) * deviation * level
    return jnp.minimum(jnp.maximum(array, -most), most).astype(held_as)


def setup_inputs(seed: int = 0) -> dict:
    key_list = jax.random.split(jax.random.key(seed), 17)
    layer_in = noise(key_list[0], (TOKENS, D), 1.0, 6.0, ((0, 16),))
    slot_stretch = jax.random.permutation(key_list[1], STRETCHES).astype(jnp.int32)
    seq_stretches = ragged_sizes(key_list[2], NSEQ, STRETCHES, MAXCH, 2).astype(jnp.int32)
    w_qkv = noise(key_list[3], (D, 3, D), D ** -0.5, 0.1875, ((2, 2),))
    qv_bias = noise(key_list[4], (2, D), 0.05, 0.29882812, ((1, 2),))
    w_out = noise(key_list[5], (D, D), (max(D // 256, 1)) ** -0.5, 3.0, ((0, 2),))
    out_bias = noise(key_list[6], (D,), 0.5, 3.0)
    norm1_gain = jnp.clip(1.0 + 0.18 * jax.random.normal(key_list[7], (D,), jnp.float32), 0.099609375, 1.8984375).astype(jnp.bfloat16)
    norm1_shift = noise(key_list[8], (D,), 0.3, 2.0)
    w_up = noise(key_list[9], (D, FF), D ** -0.5, 0.1875, ((1, 2),))
    up_bias = noise(key_list[10], (FF,), 0.5, 3.0, ((0, 2),))
    w_down = noise(key_list[11], (FF, D), FF ** -0.5, 0.09375, ((0, 2),))
    down_bias = noise(key_list[12], (D,), 0.5, 3.0)
    norm2_gain = jnp.clip(1.0 + 0.18 * jax.random.normal(key_list[13], (D,), jnp.float32), 0.099609375, 1.8984375).astype(jnp.bfloat16)
    norm2_shift = noise(key_list[14], (D,), 0.3, 2.0)
    cotangent = noise(key_list[15], (TOKENS, D), 1.0, 6.0, ((0, 16),))
    return dict(layer_in=layer_in, slot_stretch=slot_stretch, seq_stretches=seq_stretches, w_qkv=w_qkv, qv_bias=qv_bias, w_out=w_out, out_bias=out_bias, norm1_gain=norm1_gain, norm1_shift=norm1_shift, w_up=w_up, up_bias=up_bias, w_down=w_down, down_bias=down_bias, norm2_gain=norm2_gain, norm2_shift=norm2_shift, cotangent=cotangent)


@jax.custom_vjp
def low(v):
    return lax.optimization_barrier(v.astype(jnp.bfloat16)).astype(jnp.float32)

@jax.custom_vjp
def low_back(v):
    return v

def low_keep(v):
    return (low(v), None)

def low_pass(kept, grad):
    return (grad,)

def back_keep(v):
    return (v, None)

def back_low(kept, grad):
    return (low(grad),)
low.defvjp(low_keep, low_pass)
low_back.defvjp(back_keep, back_low)
EPSILON = 1e-05

def matmul(left, right):
    return jnp.dot(left, right, precision=lax.Precision.HIGHEST, preferred_element_type=jnp.float32)

def layer_norm(values, gain_vec, shift_vec):
    centre = lax.optimization_barrier(jnp.mean(values, axis=-1, keepdims=True))
    centred = values - centre
    spread = lax.optimization_barrier(jnp.mean(centred * centred, axis=-1, keepdims=True))
    return centred * lax.rsqrt(spread + EPSILON) * gain_vec + shift_vec

def attend(queries, key_rows, value_rows, seq_of, first_stretch):
    padding = jnp.zeros((MAXCH * CH, D), jnp.float32)
    key_padded = jnp.concatenate([key_rows, padding], axis=0)
    value_padded = jnp.concatenate([value_rows, padding], axis=0)
    token_seq = jnp.repeat(seq_of, CH)
    seq_padded = jnp.concatenate([token_seq, jnp.full((MAXCH * CH,), -1, jnp.int32)], axis=0)
    query_stretches = queries.reshape(STRETCHES, CH, H, HD)

    def attend_stretch(inputs):
        query_block, seq_id, begin_stretch = inputs
        offset = (begin_stretch * CH).astype(jnp.int32)
        key_window = lax.dynamic_slice_in_dim(key_padded, offset, MAXCH * CH, 0).reshape(MAXCH * CH, H, HD)
        value_window = lax.dynamic_slice_in_dim(value_padded, offset, MAXCH * CH, 0).reshape(MAXCH * CH, H, HD)
        seq_window = lax.dynamic_slice_in_dim(seq_padded, offset, MAXCH * CH, 0)
        score_block = jnp.einsum('qhd,khd->hqk', query_block, key_window, precision=lax.Precision.HIGHEST) * HD ** (-0.5)
        score_block = low_back(score_block)
        score_block = jnp.where((seq_window == seq_id)[None, None, :], score_block, -1e+30)
        weights = low(jax.nn.softmax(score_block, axis=-1))
        context = jnp.einsum('hqk,khd->qhd', weights, value_window, precision=lax.Precision.HIGHEST)
        return context.reshape(CH, D)
    context = lax.map(jax.checkpoint(attend_stretch), (query_stretches, seq_of, first_stretch))
    return context.reshape(TOKENS, D)

def reference(layer_in, slot_stretch, seq_stretches, w_qkv, qv_bias, w_out, out_bias, norm1_gain, norm1_shift, w_up, up_bias, w_down, down_bias, norm2_gain, norm2_shift, cotangent):
    seq_ends = jnp.cumsum(seq_stretches).astype(jnp.int32)
    seq_starts = (seq_ends - seq_stretches).astype(jnp.int32)
    stretch_index = jnp.arange(STRETCHES, dtype=jnp.int32)
    seq_of = lax.optimization_barrier(jnp.sum((stretch_index[:, None] >= seq_ends[None, :]).astype(jnp.int32), axis=1)).astype(jnp.int32)
    first_stretch = seq_starts[seq_of].astype(jnp.int32)
    stretch_slot = jnp.argsort(slot_stretch).astype(jnp.int32)

    def to_stretches(rows):
        return rows.reshape(STRETCHES, CH, D)[stretch_slot].reshape(TOKENS, D)

    def to_slots(rows):
        return rows.reshape(STRETCHES, CH, D)[slot_stretch].reshape(TOKENS, D)

    def forward(inputs, wqkv, bqv, wout, bout, gain_one, shift_one, wup, bup, wdown, bdown, gain_two, shift_two):
        queries = low_back(low(matmul(inputs, wqkv[:, 0, :]) + bqv[0]))
        key_rows = low_back(low(matmul(inputs, wqkv[:, 1, :])))
        value_rows = low_back(low(matmul(inputs, wqkv[:, 2, :]) + bqv[1]))
        context = attend(queries, key_rows, value_rows, seq_of, first_stretch)
        context = low_back(low(context))
        hidden = inputs + low_back(matmul(context, wout)) + bout
        first = layer_norm(hidden, gain_one, shift_one)
        pre_act = low_back(matmul(low(first), wup) + bup)
        activation = low(jax.nn.gelu(pre_act, approximate=False))
        second = first + low_back(matmul(activation, wdown)) + bdown
        return layer_norm(second, gain_two, shift_two)
    primals = (to_stretches(layer_in.astype(jnp.float32)), w_qkv.astype(jnp.float32), qv_bias.astype(jnp.float32), w_out.astype(jnp.float32), out_bias.astype(jnp.float32), norm1_gain.astype(jnp.float32), norm1_shift.astype(jnp.float32), w_up.astype(jnp.float32), up_bias.astype(jnp.float32), w_down.astype(jnp.float32), down_bias.astype(jnp.float32), norm2_gain.astype(jnp.float32), norm2_shift.astype(jnp.float32))
    result, pullback = jax.vjp(forward, *primals)
    gradients = pullback(to_stretches(cotangent.astype(jnp.float32)))
    layer_out = to_slots(result).astype(jnp.bfloat16)
    grad_in = to_slots(gradients[0])
    return (layer_out, grad_in, gradients[1], gradients[2], gradients[3], gradients[4], gradients[5], gradients[6], gradients[7], gradients[8], gradients[9], gradients[10], gradients[11], gradients[12])
```

```python
import math

import jax
import jax.numpy as jnp
from jax import lax
from jax.experimental import pallas as pl
from jax.experimental.pallas import tpu as pltpu
from jax.sharding import Mesh
from jax.sharding import PartitionSpec as P

HD = 64
CH = 512
ATTEND_PARTS = 2
BACK_PARTS = 2

EPSILON = 1e-05


def norm_forward(values, gain_vec, shift_vec):
    centre = jnp.mean(values, axis=-1, keepdims=True)
    centred = values - centre
    spread = jnp.mean(centred * centred, axis=-1, keepdims=True)
    inv_std = lax.rsqrt(spread + EPSILON)
    normed = centred * inv_std
    return (normed * gain_vec + shift_vec, normed, inv_std)


def norm_backward(gradient, normed, inv_std, gain_vec):
    scaled = gradient * gain_vec
    mean_one = jnp.mean(scaled, axis=-1, keepdims=True)
    mean_two = jnp.mean(scaled * normed, axis=-1, keepdims=True)
    back_grad = inv_std * (scaled - mean_one - normed * mean_two)
    return (back_grad, jnp.sum(gradient * normed, axis=0), jnp.sum(gradient, axis=0))


def gelu_exact(values):
    return jax.nn.gelu(values, approximate=False)


def lookup(table_vec, index_vec):
    table_width = table_vec.shape[0]
    is_match = index_vec[:, None] == jnp.arange(table_width, dtype=jnp.int32)[None, :]
    return jnp.sum(jnp.where(is_match, table_vec[None, :], 0), axis=1)


def pick_one(table_vec, position):
    return lax.dynamic_index_in_dim(table_vec, position, 0, keepdims=False)


def split_heads(block, head_count):
    return block.reshape(block.shape[0], head_count, HD)


def head_scores(query_block, key_block, head_count):
    return jnp.einsum(
        "qhd,khd->hqk",
        split_heads(query_block, head_count),
        split_heads(key_block, head_count),
        preferred_element_type=jnp.float32,
    ) * HD ** (-0.5)


def score_grads(
    query_block, key_block, value_block, grad_block, log_total, delta_block, head_count
):
    weights = jnp.exp(head_scores(query_block, key_block, head_count) - log_total[..., None])
    grad_weights = jnp.einsum(
        "qhd,khd->hqk",
        split_heads(grad_block, head_count),
        split_heads(value_block, head_count),
        preferred_element_type=jnp.float32,
    )
    grad_score = (weights * (grad_weights - delta_block[..., None])).astype(jnp.bfloat16)
    return (weights.astype(jnp.bfloat16), grad_score)


def stretch_tables(slot_stretch, seq_stretches):
    stretch_count = slot_stretch.shape[0]
    seq_ends = jnp.cumsum(seq_stretches)
    seq_starts = seq_ends - seq_stretches
    stretch_index = jnp.arange(stretch_count, dtype=jnp.int32)
    seq_of = jnp.sum((stretch_index[:, None] >= seq_ends[None, :]).astype(jnp.int32), axis=1)
    first_stretch = lookup(seq_starts, seq_of)
    stretch_span = lookup(seq_stretches, seq_of)
    is_match = slot_stretch[None, :] == stretch_index[:, None]
    stretch_slot = jnp.sum(jnp.where(is_match, stretch_index[None, :], 0), axis=1)
    return (first_stretch, stretch_span, stretch_slot)


def local(
    layer_in,
    slot_stretch,
    seq_stretches,
    w_qkv,
    qv_bias,
    w_out,
    out_bias,
    norm1_gain,
    norm1_shift,
    w_up,
    up_bias,
    w_down,
    down_bias,
    norm2_gain,
    norm2_shift,
    cotangent,
):
    tok_rows = layer_in.shape[0]
    model_width = layer_in.shape[1]
    slot_count = tok_rows // CH
    col_count = w_qkv.shape[2]
    head_count = col_count // HD
    score_scale = HD ** (-0.5)
    first_stretch, stretch_span, stretch_slot = stretch_tables(slot_stretch, seq_stretches)
    group_index = lax.axis_index("batch")
    local_stretches = lax.dynamic_slice_in_dim(slot_stretch, group_index * slot_count, slot_count)
    local_first = lookup(first_stretch, local_stretches)
    local_span = lookup(stretch_span, local_stretches)
    proj_weight = w_qkv.reshape(model_width, 3 * col_count)
    projected = jnp.dot(layer_in, proj_weight, preferred_element_type=jnp.float32)
    queries = (projected[:, :col_count] + qv_bias[0]).astype(jnp.bfloat16)
    key_rows = projected[:, col_count : 2 * col_count].astype(jnp.bfloat16)
    value_rows = (projected[:, 2 * col_count :] + qv_bias[1]).astype(jnp.bfloat16)
    query_slots = queries.reshape(slot_count, CH, col_count)
    own_keys = key_rows.reshape(slot_count, CH, col_count)
    own_values = value_rows.reshape(slot_count, CH, col_count)
    key_all, value_all = (
        lax.all_gather(own_keys, "batch", axis=0, tiled=True),
        lax.all_gather(own_values, "batch", axis=0, tiled=True),
    )

    def attend(inputs):
        query_block, begin_stretch, length = inputs

        def norm_step(offset, running):
            row_max, row_total = running
            key_slot = pick_one(stretch_slot, begin_stretch + offset)
            score_block = head_scores(query_block, pick_one(key_all, key_slot), head_count)
            new_max = jnp.maximum(row_max, jnp.max(score_block, axis=-1))
            row_total = row_total * jnp.exp(row_max - new_max) + jnp.sum(
                jnp.exp(score_block - new_max[..., None]), axis=-1
            )
            return (new_max, row_total)

        initial = (
            jnp.full((head_count, CH), -1e30, jnp.float32),
            jnp.zeros((head_count, CH), jnp.float32),
        )
        row_max, row_total = lax.fori_loop(0, length, norm_step, initial)
        log_total = row_max + jnp.log(row_total)

        def value_step(offset, summed):
            key_slot = pick_one(stretch_slot, begin_stretch + offset)
            score_block = head_scores(query_block, pick_one(key_all, key_slot), head_count)
            weights = jnp.exp(score_block - log_total[..., None]).astype(jnp.bfloat16)
            value_heads = split_heads(pick_one(value_all, key_slot), head_count)
            return summed + jnp.einsum(
                "hqk,khd->qhd", weights, value_heads, preferred_element_type=jnp.float32
            )

        summed = lax.fori_loop(0, length, value_step, jnp.zeros((CH, head_count, HD), jnp.float32))
        return (summed.reshape(CH, col_count), log_total)

    context, log_totals = lax.map(attend, (query_slots, local_first, local_span))
    context = context.reshape(tok_rows, col_count)
    context_low = context.astype(jnp.bfloat16)
    attn_part = jnp.dot(context_low, w_out, preferred_element_type=jnp.float32)
    hidden = (
        layer_in.astype(jnp.float32)
        + lax.psum(attn_part.astype(jnp.bfloat16), "head").astype(jnp.float32)
        + out_bias
    )
    first_norm, normed_one, inv_one = norm_forward(hidden, norm1_gain, norm1_shift)
    first_low = first_norm.astype(jnp.bfloat16)
    pre_act = jnp.dot(first_low, w_up, preferred_element_type=jnp.float32) + up_bias
    activation, gelu_back = jax.vjp(gelu_exact, pre_act)
    act_low = activation.astype(jnp.bfloat16)
    down_part = jnp.dot(act_low, w_down, preferred_element_type=jnp.float32)
    second_in = (
        first_norm
        + lax.psum(down_part.astype(jnp.bfloat16), "head").astype(jnp.float32)
        + down_bias
    )
    normed_out, normed_two, inv_two = norm_forward(second_in, norm2_gain, norm2_shift)
    grad_second, grad_gain_two, grad_shift_two = norm_backward(
        cotangent.astype(jnp.float32), normed_two, inv_two, norm2_gain
    )
    layer_out = normed_out.astype(jnp.bfloat16)
    second_low = grad_second.astype(jnp.bfloat16)
    grad_down = jnp.einsum("tf,td->fd", act_low, second_low, preferred_element_type=jnp.float32)
    grad_down_bias = jnp.sum(grad_second, axis=0)
    grad_act = jnp.einsum("td,fd->tf", second_low, w_down, preferred_element_type=jnp.float32)
    grad_pre_low = gelu_back(grad_act)[0].astype(jnp.bfloat16)
    grad_up = jnp.einsum("td,tf->df", first_low, grad_pre_low, preferred_element_type=jnp.float32)
    grad_up_bias = jnp.sum(grad_pre_low.astype(jnp.float32), axis=0)
    ffn_back = jnp.einsum("tf,df->td", grad_pre_low, w_up, preferred_element_type=jnp.float32)
    grad_first = lax.psum(ffn_back.astype(jnp.bfloat16), "head").astype(jnp.float32) + grad_second
    grad_hidden, grad_gain_one, grad_shift_one = norm_backward(
        grad_first, normed_one, inv_one, norm1_gain
    )
    grad_out_bias = jnp.sum(grad_hidden, axis=0)
    hidden_low = grad_hidden.astype(jnp.bfloat16)
    grad_out = jnp.einsum("tc,td->cd", context_low, hidden_low, preferred_element_type=jnp.float32)
    grad_context = jnp.einsum(
        "td,cd->tc", hidden_low, w_out, preferred_element_type=jnp.float32
    ).astype(jnp.bfloat16)
    delta_rows = jnp.sum(
        (grad_context.astype(jnp.float32) * context).reshape(tok_rows, head_count, HD), axis=-1
    )
    delta_slots = jnp.swapaxes(delta_rows.reshape(slot_count, CH, head_count), 1, 2)
    grad_slots = grad_context.reshape(slot_count, CH, col_count)

    def back_slot(key_total, inputs):
        query_block, grad_block, log_total, delta_block, begin_stretch, length = inputs

        def key_step(offset, running):
            grad_query, key_sum = running
            key_slot = pick_one(stretch_slot, begin_stretch + offset)
            key_block = pick_one(key_all, key_slot)
            value_block = pick_one(value_all, key_slot)
            weights_low, grad_score = score_grads(
                query_block, key_block, value_block, grad_block, log_total, delta_block, head_count
            )
            grad_query = (
                grad_query
                + jnp.einsum(
                    "hqk,khd->qhd",
                    grad_score,
                    split_heads(key_block, head_count),
                    preferred_element_type=jnp.float32,
                )
                * score_scale
            )
            grad_key = (
                jnp.einsum(
                    "hqk,qhd->khd",
                    grad_score,
                    split_heads(query_block, head_count),
                    preferred_element_type=jnp.float32,
                )
                * score_scale
            )
            grad_value = jnp.einsum(
                "hqk,qhd->khd",
                weights_low,
                split_heads(grad_block, head_count),
                preferred_element_type=jnp.float32,
            )
            update = jnp.concatenate(
                [grad_key.reshape(CH, col_count), grad_value.reshape(CH, col_count)], axis=1
            )
            key_sum = lax.dynamic_update_index_in_dim(
                key_sum, pick_one(key_sum, key_slot) + update, key_slot, 0
            )
            return (grad_query, key_sum)

        start_state = (jnp.zeros((CH, head_count, HD), jnp.float32), key_total)
        grad_query, key_total = lax.fori_loop(0, length, key_step, start_state)
        return (key_total, grad_query.reshape(CH, col_count))

    key_start = jnp.zeros((key_all.shape[0], CH, 2 * col_count), jnp.float32)
    key_total, grad_query_slots = lax.scan(
        back_slot,
        key_start,
        (query_slots, grad_slots, log_totals, delta_slots, local_first, local_span),
    )
    key_grads = lax.psum_scatter(
        key_total.astype(jnp.bfloat16), "batch", scatter_dimension=0, tiled=True
    ).astype(jnp.float32)
    grad_keys = key_grads[:, :, :col_count].astype(jnp.bfloat16)
    grad_values = key_grads[:, :, col_count:].astype(jnp.bfloat16)
    grad_queries = grad_query_slots.reshape(tok_rows, col_count).astype(jnp.bfloat16)
    grad_keys = grad_keys.reshape(tok_rows, col_count)
    grad_values = grad_values.reshape(tok_rows, col_count)
    grad_proj = jnp.concatenate([grad_queries, grad_keys, grad_values], axis=1)
    grad_qkv = jnp.einsum(
        "td,tc->dc", layer_in, grad_proj, preferred_element_type=jnp.float32
    ).reshape(model_width, 3, col_count)
    grad_qv = jnp.stack(
        [
            jnp.sum(grad_queries.astype(jnp.float32), axis=0),
            jnp.sum(grad_values.astype(jnp.float32), axis=0),
        ]
    )
    input_part = jnp.einsum("tc,dc->td", grad_proj, proj_weight, preferred_element_type=jnp.float32)
    own_width = model_width // lax.axis_size("head")
    own_grad = lax.dynamic_slice_in_dim(
        grad_hidden, lax.axis_index("head") * own_width, own_width, 1
    )
    grad_in = (
        lax.psum_scatter(
            input_part.astype(jnp.bfloat16), "head", scatter_dimension=1, tiled=True
        ).astype(jnp.float32)
        + own_grad
    )
    totals = (
        lax.psum(grad_qkv.astype(jnp.bfloat16), "batch").astype(jnp.float32),
        lax.psum(grad_qv.astype(jnp.bfloat16), "batch").astype(jnp.float32),
        lax.psum(grad_out.astype(jnp.bfloat16), "batch").astype(jnp.float32),
        lax.psum(grad_out_bias.astype(jnp.bfloat16), "batch").astype(jnp.float32),
        lax.psum(grad_gain_one.astype(jnp.bfloat16), "batch").astype(jnp.float32),
        lax.psum(grad_shift_one.astype(jnp.bfloat16), "batch").astype(jnp.float32),
        lax.psum(grad_up.astype(jnp.bfloat16), "batch").astype(jnp.float32),
        lax.psum(grad_up_bias.astype(jnp.bfloat16), "batch").astype(jnp.float32),
        lax.psum(grad_down.astype(jnp.bfloat16), "batch").astype(jnp.float32),
        lax.psum(grad_down_bias.astype(jnp.bfloat16), "batch").astype(jnp.float32),
        lax.psum(grad_gain_two.astype(jnp.bfloat16), "batch").astype(jnp.float32),
        lax.psum(grad_shift_two.astype(jnp.bfloat16), "batch").astype(jnp.float32),
    )
    return (
        layer_out,
        grad_in,
        totals[0],
        totals[1],
        totals[2],
        totals[3],
        totals[4],
        totals[5],
        totals[6],
        totals[7],
        totals[8],
        totals[9],
        totals[10],
        totals[11],
    )


LOG2E = 1.4426950408889634
SCORE = HD ** (-0.5)
SWAP = [(0, 1), (1, 0)]
VMEM_LIMIT = 56 * 1024 * 1024


def nt(left, right):
    return lax.dot_general(
        left, right, (((1,), (1,)), ((), ())), preferred_element_type=jnp.float32
    )


def mm(left, right):
    return jnp.dot(left, right, preferred_element_type=jnp.float32)


def low_half(block):
    lane = lax.broadcasted_iota(jnp.int32, block.shape, 1)
    return lane < HD


def project_kernel(x_ref, wq_ref, wk_ref, wv_ref, bias_ref, kv_ref, q_ref):
    slot = pl.program_id(1)
    rows = x_ref[...]
    q_all = mm(rows, wq_ref[...]) + bias_ref[0:1, :].astype(jnp.float32)
    k_all = mm(rows, wk_ref[...])
    v_all = mm(rows, wv_ref[...]) + bias_ref[1:2, :].astype(jnp.float32)
    for pair in range(q_all.shape[1] // 128):
        cols = slice(pair * 128, pair * 128 + 128)
        q_pair, k_pair, v_pair = q_all[:, cols], k_all[:, cols], v_all[:, cols]
        low = low_half(q_pair)
        kv_ref[2 * pair] = jnp.where(low, k_pair, pltpu.roll(v_pair, HD, 1)).astype(jnp.bfloat16)
        kv_ref[2 * pair + 1] = jnp.where(low, pltpu.roll(k_pair, HD, 1), v_pair).astype(
            jnp.bfloat16
        )
        q_low = q_pair.astype(jnp.bfloat16)
        q_roll = pltpu.roll(q_pair, HD, 1).astype(jnp.bfloat16)

        @pl.when(slot == 0)
        def _():
            q_ref[2 * pair, :, 0:HD] = q_low[:, 0:HD]
            q_ref[2 * pair + 1, :, 0:HD] = q_roll[:, 0:HD]

        @pl.when(slot == 1)
        def _():
            q_ref[2 * pair, :, HD:128] = q_roll[:, HD:128]
            q_ref[2 * pair + 1, :, HD:128] = q_low[:, HD:128]


def project(layer_in, weight, bias):
    width = layer_in.shape[1]
    heads = weight.shape[1] // 3 // HD
    step = 4
    groups = heads // step
    cols = step * HD
    return pl.pallas_call(
        project_kernel,
        grid=(groups, 2),
        in_specs=[
            pl.BlockSpec((CH, width), lambda g, s: (s, 0)),
            pl.BlockSpec((width, cols), lambda g, s: (0, g)),
            pl.BlockSpec((width, cols), lambda g, s: (0, groups + g)),
            pl.BlockSpec((width, cols), lambda g, s: (0, 2 * groups + g)),
            pl.BlockSpec((2, cols), lambda g, s: (0, g)),
        ],
        out_specs=[
            pl.BlockSpec((step, CH, 128), lambda g, s: (g, s, 0)),
            pl.BlockSpec((step, CH, 128), lambda g, s: (g, 0, 0)),
        ],
        out_shape=[
            jax.ShapeDtypeStruct((heads, 2 * CH, 128), jnp.bfloat16),
            jax.ShapeDtypeStruct((heads, CH, 128), jnp.bfloat16),
        ],
        compiler_params=pltpu.CompilerParams(vmem_limit_bytes=VMEM_LIMIT),
        cost_estimate=pl.CostEstimate(
            flops=2 * layer_in.size * weight.shape[1],
            bytes_accessed=2 * (layer_in.size + weight.size) + 6 * layer_in.size,
            transcendentals=0,
        ),
        name="project",
    )(layer_in, weight, weight, weight, bias)


def fill_tables(slot_ref, seq_ref, stretch_slot, seq_first, seq_length):
    def place(slot, carry):
        stretch_slot[slot_ref[slot]] = slot
        return carry

    lax.fori_loop(0, slot_ref.shape[0], place, 0)

    def one_sequence(seq, start):
        length = seq_ref[seq]

        def one_stretch(offset, carry):
            seq_first[start + offset] = start
            seq_length[start + offset] = length
            return carry

        lax.fori_loop(0, length, one_stretch, 0)
        return start + length

    lax.fori_loop(0, seq_ref.shape[0], one_sequence, jnp.int32(0))


def key_index(slot, core, half):
    own = ((slot >> 1) & 1) == core
    return jnp.where(own, 0, half) + ((slot >> 2) << 1) + (slot & 1)


def load_keys(own_hbm, other_hbm, keys, sem):
    half = own_hbm.shape[0]
    first = pltpu.make_async_copy(own_hbm, keys.at[pl.ds(0, half)], sem.at[0])
    second = pltpu.make_async_copy(other_hbm, keys.at[pl.ds(half, half)], sem.at[1])
    first.start()
    second.start()
    first.wait()
    second.wait()


def pick_slot(packed, slot_bit):
    wide = packed.astype(jnp.float32)
    return jnp.where(slot_bit == 0, wide, pltpu.roll(wide, HD, 1))


def attend_kernel(
    slot_ref,
    seq_ref,
    core_ref,
    q_ref,
    own_hbm,
    other_hbm,
    ctx_ref,
    ctx_t_ref,
    lse_ref,
    keys,
    values_t,
    stretch_slot,
    seq_first,
    seq_length,
    sem,
):
    chip, bit = pl.program_id(0), pl.program_id(1)
    half = own_hbm.shape[0]

    @pl.when((chip == 0) & (bit == 0))
    def _():
        load_keys(own_hbm, other_hbm, keys, sem)
        fill_tables(slot_ref, seq_ref, stretch_slot, seq_first, seq_length)

        def turn(index, carry):
            values_t[index] = keys[index].T[HD:128, :]
            return carry

        lax.fori_loop(0, 2 * half, turn, 0)

    core = core_ref[0]
    stretch = slot_ref[4 * chip + 2 * core + bit]
    begin, length = seq_first[stretch], seq_length[stretch]
    query = pick_slot(q_ref[0], bit)
    query = jnp.where(low_half(query), query, 0.0).astype(jnp.bfloat16)
    parts = ATTEND_PARTS
    part = CH // parts

    def step(offset, state):
        index = key_index(stretch_slot[begin + offset], core, half)
        block = keys[index]
        block_t = values_t[index]
        fresh = []
        for n in range(parts):
            top, total, acc = state[n]
            score = nt(block, query[n * part : (n + 1) * part, :]) * (SCORE * LOG2E)
            new_top = jnp.maximum(top, jnp.max(score, axis=0, keepdims=True))
            weight = jnp.exp2(score - new_top)
            scale = jnp.exp2(top - new_top)
            total = total * scale + jnp.sum(weight, axis=0, keepdims=True)
            acc = acc * scale + mm(block_t, weight.astype(jnp.bfloat16))
            fresh.append((new_top, total, acc))
        return tuple(fresh)

    start = tuple(
        (
            jnp.full((1, part), -1e30, jnp.float32),
            jnp.zeros((1, part), jnp.float32),
            jnp.zeros((HD, part), jnp.float32),
        )
        for _ in range(parts)
    )
    final = lax.fori_loop(0, length, step, start)
    for n in range(parts):
        top, total, acc = final[n]
        cols = slice(n * part, (n + 1) * part)
        context_t = acc / total
        ctx_t_ref[0, :, cols] = context_t
        lse_ref[0, :, cols] = top + jnp.log2(total)
        turned = context_t.T.astype(jnp.bfloat16)

        @pl.when(bit == 0)
        def _():
            ctx_ref[0, cols, 0:HD] = turned

        @pl.when(bit == 1)
        def _():
            ctx_ref[0, cols, HD:128] = turned


def table_scratch(stretches):
    return [pltpu.SMEM((stretches,), jnp.int32) for _ in range(3)] + [
        pltpu.SemaphoreType.DMA((2,))
    ]


def attend(slot_stretch, seq_stretches, core, q_pack, own_keys, other_keys):
    chips = q_pack.shape[0]
    slots = 2 * chips
    stretches = slot_stretch.shape[0]
    pairs = slots * 5 * CH * CH
    return pl.pallas_call(
        attend_kernel,
        grid_spec=pltpu.PrefetchScalarGridSpec(
            num_scalar_prefetch=3,
            grid=(chips, 2),
            in_specs=[
                pl.BlockSpec((1, CH, 128), lambda z, s, *_: (z, 0, 0)),
                pl.BlockSpec(memory_space=pl.ANY),
                pl.BlockSpec(memory_space=pl.ANY),
            ],
            out_specs=[
                pl.BlockSpec((1, CH, 128), lambda z, s, *_: (z, 0, 0)),
                pl.BlockSpec((1, HD, CH), lambda z, s, *_: (2 * z + s, 0, 0)),
                pl.BlockSpec((1, 1, CH), lambda z, s, *_: (2 * z + s, 0, 0)),
            ],
            scratch_shapes=[
                pltpu.VMEM((2 * slots, CH, 128), jnp.bfloat16),
                pltpu.VMEM((2 * slots, HD, CH), jnp.bfloat16),
            ]
            + table_scratch(stretches),
        ),
        out_shape=[
            jax.ShapeDtypeStruct((chips, CH, 128), jnp.bfloat16),
            jax.ShapeDtypeStruct((slots, HD, CH), jnp.float32),
            jax.ShapeDtypeStruct((slots, 1, CH), jnp.float32),
        ],
        compiler_params=pltpu.CompilerParams(vmem_limit_bytes=VMEM_LIMIT),
        cost_estimate=pl.CostEstimate(
            flops=4 * HD * pairs, bytes_accessed=16 * q_pack.size, transcendentals=pairs
        ),
        name="attend",
    )(slot_stretch, seq_stretches, core, q_pack, own_keys, other_keys)


def attend_back_kernel(
    slot_ref,
    seq_ref,
    core_ref,
    q_ref,
    g_ref,
    ctx_t_ref,
    lse_ref,
    own_hbm,
    other_hbm,
    dq_ref,
    own_grad_ref,
    other_grad_ref,
    keys,
    keys_t,
    grads,
    stretch_slot,
    seq_first,
    seq_length,
    sem,
):
    chip, bit = pl.program_id(0), pl.program_id(1)
    half = own_hbm.shape[0]

    @pl.when((chip == 0) & (bit == 0))
    def _():
        load_keys(own_hbm, other_hbm, keys, sem)
        fill_tables(slot_ref, seq_ref, stretch_slot, seq_first, seq_length)

        def turn(index, carry):
            keys_t[index] = keys[index].T[0:HD, :]
            grads[index] = jnp.zeros((CH, 128), jnp.float32)
            return carry

        lax.fori_loop(0, 2 * half, turn, 0)

    core = core_ref[0]
    stretch = slot_ref[4 * chip + 2 * core + bit]
    begin, length = seq_first[stretch], seq_length[stretch]
    query = pick_slot(q_ref[0], bit)
    low = low_half(query)
    query = jnp.where(low, query, 0.0).astype(jnp.bfloat16)
    grad = pick_slot(g_ref[0], 1 - bit)
    grad = jnp.where(low, 0.0, grad)
    delta = jnp.sum(grad.T[HD:128, :] * ctx_t_ref[0], axis=0, keepdims=True)
    grad = grad.astype(jnp.bfloat16)
    lse = lse_ref[0]
    parts = BACK_PARTS
    part = CH // parts

    def step(offset, state):
        index = key_index(stretch_slot[begin + offset], core, half)
        block = keys[index]
        block_t = keys_t[index]
        fresh = []
        total = None
        for n in range(parts):
            cols = slice(n * part, (n + 1) * part)
            q_part, g_part = query[cols, :], grad[cols, :]
            score = nt(block, q_part) * (SCORE * LOG2E)
            weight = jnp.exp2(score - lse[:, cols])
            slope = weight * (nt(block, g_part) - delta[:, cols])
            slope = slope.astype(jnp.bfloat16)
            weight = weight.astype(jnp.bfloat16)
            fresh.append(state[n] + mm(block_t, slope))
            update = mm(slope, q_part) + mm(weight, g_part)
            total = update if total is None else total + update
        grads[index] += total
        return tuple(fresh)

    start = tuple(jnp.zeros((HD, part), jnp.float32) for _ in range(parts))
    final = lax.fori_loop(0, length, step, start)
    for n in range(parts):
        cols = slice(n * part, (n + 1) * part)
        turned = (final[n] * SCORE).T.astype(jnp.bfloat16)

        @pl.when(bit == 0)
        def _():
            dq_ref[0, cols, 0:HD] = turned

        @pl.when(bit == 1)
        def _():
            dq_ref[0, cols, HD:128] = turned

    @pl.when((chip == pl.num_programs(0) - 1) & (bit == 1))
    def _():
        scale = jnp.where(low, SCORE, 1.0)

        def leave(index, carry):
            own_grad_ref[index] = grads[index] * scale
            other_grad_ref[index] = (grads[half + index] * scale).astype(jnp.bfloat16)
            return carry

        lax.fori_loop(0, half, leave, 0)


def attend_back(
    slot_stretch, seq_stretches, core, q_pack, g_pack, ctx_t, lse, own_keys, other_keys
):
    chips = q_pack.shape[0]
    slots = 2 * chips
    stretches = slot_stretch.shape[0]
    pairs = slots * 5 * CH * CH
    return pl.pallas_call(
        attend_back_kernel,
        grid_spec=pltpu.PrefetchScalarGridSpec(
            num_scalar_prefetch=3,
            grid=(chips, 2),
            in_specs=[
                pl.BlockSpec((1, CH, 128), lambda z, s, *_: (z, 0, 0)),
                pl.BlockSpec((1, CH, 128), lambda z, s, *_: (z, 0, 0)),
                pl.BlockSpec((1, HD, CH), lambda z, s, *_: (2 * z + s, 0, 0)),
                pl.BlockSpec((1, 1, CH), lambda z, s, *_: (2 * z + s, 0, 0)),
                pl.BlockSpec(memory_space=pl.ANY),
                pl.BlockSpec(memory_space=pl.ANY),
            ],
            out_specs=[
                pl.BlockSpec((1, CH, 128), lambda z, s, *_: (z, 0, 0)),
                pl.BlockSpec((slots, CH, 128), lambda z, s, *_: (0, 0, 0)),
                pl.BlockSpec((slots, CH, 128), lambda z, s, *_: (0, 0, 0)),
            ],
            scratch_shapes=[
                pltpu.VMEM((2 * slots, CH, 128), jnp.bfloat16),
                pltpu.VMEM((2 * slots, HD, CH), jnp.bfloat16),
                pltpu.VMEM((2 * slots, CH, 128), jnp.float32),
            ]
            + table_scratch(stretches),
        ),
        out_shape=[
            jax.ShapeDtypeStruct((chips, CH, 128), jnp.bfloat16),
            jax.ShapeDtypeStruct((slots, CH, 128), jnp.float32),
            jax.ShapeDtypeStruct((slots, CH, 128), jnp.bfloat16),
        ],
        compiler_params=pltpu.CompilerParams(vmem_limit_bytes=VMEM_LIMIT),
        cost_estimate=pl.CostEstimate(
            flops=10 * HD * pairs, bytes_accessed=24 * q_pack.size, transcendentals=pairs
        ),
        name="attend_back",
    )(slot_stretch, seq_stretches, core, q_pack, g_pack, ctx_t, lse, own_keys, other_keys)


def swap_across(block, axis_name):
    return lax.ppermute(block, axis_name, SWAP)


def spread(block):
    return lax.all_to_all(block, "chip", 0, 0, tiled=True)


def gelu_both(pre):
    phi = 0.5 + 0.5 * lax.erf(pre * (2.0**-0.5))
    density = jnp.exp(-0.5 * pre * pre) * ((2.0 * math.pi) ** -0.5)
    return ((pre * phi).astype(jnp.bfloat16), phi + pre * density)


def tn(left, right):
    return lax.dot_general(
        left, right, (((0,), (0,)), ((), ())), preferred_element_type=jnp.float32
    )


def fast_local(
    layer_in,
    slot_stretch,
    seq_stretches,
    w_qkv,
    qv_bias,
    w_out,
    out_bias,
    norm1_gain,
    norm1_shift,
    w_up,
    up_bias,
    w_down,
    down_bias,
    norm2_gain,
    norm2_shift,
    cotangent,
):
    width = layer_in.shape[1]
    cols = w_qkv.shape[2]
    heads = cols // HD
    units = w_up.shape[1]
    half = units // 2
    side = lax.axis_index("head")
    core = lax.axis_index("core")
    core_vec = core.reshape(1).astype(jnp.int32)
    low = jnp.bfloat16

    def both_halves(array, axis):
        mine = lax.dynamic_slice_in_dim(array, core * half, half, axis)
        rest = lax.dynamic_slice_in_dim(array, (1 - core) * half, half, axis)
        far_mine = swap_across(mine, "head")
        return [mine, rest, far_mine, swap_across(far_mine, "core")]

    proj_weight = w_qkv.reshape(width, 3 * cols)
    send_kv, send_q = project(layer_in, proj_weight, qv_bias)
    own_kv = spread(send_kv)
    q_pack = spread(send_q)
    other_kv = swap_across(own_kv, "core")
    own_keys = own_kv.reshape(2 * heads, CH, 128)
    other_keys = other_kv.reshape(2 * heads, CH, 128)

    up_parts = both_halves(w_up, 1)
    down_parts = both_halves(w_down, 0)
    up_biases = both_halves(up_bias, 0)
    w_out_far = swap_across(w_out, "head")

    ctx, ctx_t, lse = attend(slot_stretch, seq_stretches, core_vec, q_pack, own_keys, other_keys)
    ctx_in = spread(ctx).reshape(heads, CH, 2, HD)
    ctx_in = ctx_in.transpose(2, 1, 0, 3).reshape(2, CH, cols)
    ctx_own = lax.dynamic_index_in_dim(ctx_in, side, 0, keepdims=False)
    ctx_far = swap_across(lax.dynamic_index_in_dim(ctx_in, 1 - side, 0, keepdims=False), "head")

    row0 = side * CH
    rows_in = lax.dynamic_slice_in_dim(layer_in, row0, CH, 0).astype(jnp.float32)
    cot = lax.dynamic_slice_in_dim(cotangent, row0, CH, 0).astype(jnp.float32)
    hidden = rows_in + (mm(ctx_own, w_out) + mm(ctx_far, w_out_far)) + out_bias
    first_norm, normed_one, inv_one = norm_forward(hidden, norm1_gain, norm1_shift)
    first_low = first_norm.astype(low)
    acts, slopes = [], []
    down_sum = None
    for up, bias, down in zip(up_parts, up_biases, down_parts):
        act, slope = gelu_both(mm(first_low, up) + bias)
        acts.append(act)
        slopes.append(slope)
        term = mm(act, down)
        down_sum = term if down_sum is None else down_sum + term
    second_in = first_norm + down_sum + down_bias
    normed_out, normed_two, inv_two = norm_forward(second_in, norm2_gain, norm2_shift)
    grad_second, grad_gain_two, grad_shift_two = norm_backward(
        cot, normed_two, inv_two, norm2_gain
    )
    out_rows = normed_out.astype(low)
    second_low = grad_second.astype(low)
    grad_pres = []
    back_sum = None
    for up, down, slope in zip(up_parts, down_parts, slopes):
        grad_pre = (nt(second_low, down) * slope).astype(low)
        grad_pres.append(grad_pre)
        term = nt(grad_pre, up)
        back_sum = term if back_sum is None else back_sum + term
    grad_first = back_sum + grad_second
    grad_hidden, grad_gain_one, grad_shift_one = norm_backward(
        grad_first, normed_one, inv_one, norm1_gain
    )
    hidden_low = grad_hidden.astype(low)
    gc_far = nt(hidden_low, w_out_far).astype(low)
    gc_own = nt(hidden_low, w_out).astype(low)
    gc_in = swap_across(gc_far, "head")

    def head_major(first, second):
        pair = jnp.stack([first, second]).reshape(2, CH, heads, HD)
        return pair.transpose(2, 1, 0, 3).reshape(heads, CH, 128)

    is_low = side == 0
    g_pack = spread(
        head_major(jnp.where(is_low, gc_own, gc_in), jnp.where(is_low, gc_in, gc_own))
    )

    def reduce_far(own, far):
        kept = own[0] + swap_across(own[1].astype(low), "core").astype(jnp.float32)
        gone = far[0] + swap_across(far[1].astype(low), "core").astype(jnp.float32)
        return kept + swap_across(gone.astype(low), "head").astype(jnp.float32)

    up_grads = [tn(first_low, part) for part in grad_pres]
    down_grads = [tn(act, second_low) for act in acts]
    half_rows = cols // 2

    def rows_of(block, which):
        return lax.dynamic_slice_in_dim(block, which * half_rows, half_rows, 1)

    out_grads = [
        tn(rows_of(block, which), hidden_low)
        for block in (ctx_own, ctx_far)
        for which in (core, 1 - core)
    ]
    sums = [
        reduce_far(part[:2], part[2:]).astype(low) for part in (up_grads, down_grads, out_grads)
    ]
    sums = lax.psum(tuple(sums), "chip")

    def join(mine, axis):
        rest = swap_across(mine, "core")
        is_first = core == 0
        return jnp.concatenate(
            [jnp.where(is_first, mine, rest), jnp.where(is_first, rest, mine)], axis=axis
        ).astype(jnp.float32)

    grad_up, grad_down, grad_out = join(sums[0], 1), join(sums[1], 0), join(sums[2], 0)

    bias_grads = [jnp.sum(part.astype(jnp.float32), axis=0) for part in grad_pres]
    is_first = core == 0

    def ordered(first, second):
        return jnp.concatenate(
            [jnp.where(is_first, first, second), jnp.where(is_first, second, first)]
        )

    bias_own, bias_far = ordered(*bias_grads[:2]), ordered(*bias_grads[2:])
    small = jnp.concatenate(
        [
            jnp.where(is_low, bias_own, bias_far),
            jnp.where(is_low, bias_far, bias_own),
            jnp.sum(grad_hidden, axis=0),
            grad_gain_one,
            grad_shift_one,
            jnp.sum(grad_second, axis=0),
            grad_gain_two,
            grad_shift_two,
        ]
    )
    small = lax.psum(small, ("chip", "core", "head"))
    grad_up_bias = lax.dynamic_slice_in_dim(small, side * units, units)
    vectors = small[2 * units :].reshape(6, width)

    layer_out_pair = jnp.stack([out_rows, swap_across(out_rows, "head")])
    layer_out = jnp.where(is_low, layer_out_pair, layer_out_pair[::-1]).reshape(2 * CH, width)

    dq_pack, own_grad, other_grad = attend_back(
        slot_stretch, seq_stretches, core_vec, q_pack, g_pack, ctx_t, lse, own_keys, other_keys
    )
    kv_grad = (own_grad + swap_across(other_grad, "core").astype(jnp.float32)).astype(low)
    kv_grad = spread(kv_grad.reshape(heads, 2 * CH, 128))
    dq_in = spread(dq_pack)

    grad_q = dq_in.reshape(heads, CH, 2, HD).transpose(2, 1, 0, 3).reshape(2 * CH, cols)
    kv_rows = kv_grad.reshape(heads, 2 * CH, 2, HD).transpose(1, 2, 0, 3)
    grad_proj = jnp.concatenate([grad_q, kv_rows.reshape(2 * CH, 2 * cols)], axis=1)
    grad_qkv = tn(layer_in, grad_proj).astype(low)
    row_sums = jnp.sum(grad_proj.astype(jnp.float32), axis=0)
    grad_qv = jnp.stack([row_sums[:cols], row_sums[2 * cols :]])
    input_part = nt(grad_proj, proj_weight)
    own_width = width // 2
    far_part = lax.dynamic_slice_in_dim(input_part, (1 - side) * own_width, own_width, 1)
    own_part = lax.dynamic_slice_in_dim(input_part, side * own_width, own_width, 1)
    rows_pair = jnp.where(
        jnp.arange(2)[:, None, None] == side, grad_hidden[None].astype(jnp.float32), 0.0
    ).reshape(2 * CH, width)
    far_hidden = lax.dynamic_slice_in_dim(rows_pair, (1 - side) * own_width, own_width, 1)
    own_hidden = lax.dynamic_slice_in_dim(rows_pair, side * own_width, own_width, 1)
    arrived = swap_across((far_part + far_hidden).astype(low), "head")
    grad_in = own_part + own_hidden + arrived.astype(jnp.float32)
    grad_qkv, grad_qv = lax.psum((grad_qkv, grad_qv.astype(low)), ("chip", "core"))
    return (
        layer_out,
        grad_in,
        grad_qkv.astype(jnp.float32).reshape(width, 3, cols),
        grad_qv.astype(jnp.float32),
        grad_out,
        vectors[0],
        vectors[1],
        vectors[2],
        grad_up,
        grad_up_bias,
        grad_down,
        vectors[3],
        vectors[4],
        vectors[5],
    )


def solution(mesh):
    batch, head = mesh.shape["batch"], mesh.shape["head"]

    def whole(*arrays):
        tokens, width = arrays[0].shape
        heads = arrays[3].shape[2] // head // HD
        fits = (
            head == 2
            and batch == 2 * heads
            and tokens == batch * 2 * CH
            and arrays[9].shape[1] % (4 * 128) == 0
        )
        if fits:
            split = Mesh(mesh.devices.reshape(batch // 2, 2, head), ("chip", "core", "head"))
            return run(fast_local, split, ("chip", "core"))(*arrays)
        return run(local, mesh, "batch")(*arrays)

    return whole


def run(body, mesh, rows):
    in_specs = (
        P(rows, None),
        P(),
        P(),
        P(None, None, "head"),
        P(None, "head"),
        P("head", None),
        P(),
        P(),
        P(),
        P(None, "head"),
        P("head"),
        P("head", None),
        P(),
        P(),
        P(),
        P(rows, None),
    )
    out_specs = (
        P(rows, None),
        P(rows, "head"),
        P(None, None, "head"),
        P(None, "head"),
        P("head", None),
        P(),
        P(),
        P(),
        P(None, "head"),
        P("head"),
        P("head", None),
        P(),
        P(),
        P(),
    )
    return jax.shard_map(body, mesh=mesh, in_specs=in_specs, out_specs=out_specs, check_vma=False)
```

```python
import functools
import math

import jax
import jax.numpy as jnp
from jax import lax
from jax.experimental import pallas as pl
from jax.experimental.pallas import tpu as pltpu
from jax.sharding import Mesh
from jax.sharding import PartitionSpec as P

HD = 64
CH = 512

EPSILON = 1e-05


def norm_forward(values, gain_vec, shift_vec):
    centre = jnp.mean(values, axis=-1, keepdims=True)
    centred = values - centre
    spread = jnp.mean(centred * centred, axis=-1, keepdims=True)
    inv_std = lax.rsqrt(spread + EPSILON)
    normed = centred * inv_std
    return (normed * gain_vec + shift_vec, normed, inv_std)


def norm_backward(gradient, normed, inv_std, gain_vec):
    scaled = gradient * gain_vec
    mean_one = jnp.mean(scaled, axis=-1, keepdims=True)
    mean_two = jnp.mean(scaled * normed, axis=-1, keepdims=True)
    back_grad = inv_std * (scaled - mean_one - normed * mean_two)
    return (back_grad, jnp.sum(gradient * normed, axis=0), jnp.sum(gradient, axis=0))


def gelu_exact(values):
    return jax.nn.gelu(values, approximate=False)


def lookup(table_vec, index_vec):
    table_width = table_vec.shape[0]
    is_match = index_vec[:, None] == jnp.arange(table_width, dtype=jnp.int32)[None, :]
    return jnp.sum(jnp.where(is_match, table_vec[None, :], 0), axis=1)


def pick_one(table_vec, position):
    return lax.dynamic_index_in_dim(table_vec, position, 0, keepdims=False)


def split_heads(block, head_count):
    return block.reshape(block.shape[0], head_count, HD)


def head_scores(query_block, key_block, head_count):
    return jnp.einsum(
        "qhd,khd->hqk",
        split_heads(query_block, head_count),
        split_heads(key_block, head_count),
        preferred_element_type=jnp.float32,
    ) * HD ** (-0.5)


def score_grads(
    query_block, key_block, value_block, grad_block, log_total, delta_block, head_count
):
    weights = jnp.exp(head_scores(query_block, key_block, head_count) - log_total[..., None])
    grad_weights = jnp.einsum(
        "qhd,khd->hqk",
        split_heads(grad_block, head_count),
        split_heads(value_block, head_count),
        preferred_element_type=jnp.float32,
    )
    grad_score = (weights * (grad_weights - delta_block[..., None])).astype(jnp.bfloat16)
    return (weights.astype(jnp.bfloat16), grad_score)


def stretch_tables(slot_stretch, seq_stretches):
    stretch_count = slot_stretch.shape[0]
    seq_ends = jnp.cumsum(seq_stretches)
    seq_starts = seq_ends - seq_stretches
    stretch_index = jnp.arange(stretch_count, dtype=jnp.int32)
    seq_of = jnp.sum((stretch_index[:, None] >= seq_ends[None, :]).astype(jnp.int32), axis=1)
    first_stretch = lookup(seq_starts, seq_of)
    stretch_span = lookup(seq_stretches, seq_of)
    is_match = slot_stretch[None, :] == stretch_index[:, None]
    stretch_slot = jnp.sum(jnp.where(is_match, stretch_index[None, :], 0), axis=1)
    return (first_stretch, stretch_span, stretch_slot)


def local(
    layer_in,
    slot_stretch,
    seq_stretches,
    w_qkv,
    qv_bias,
    w_out,
    out_bias,
    norm1_gain,
    norm1_shift,
    w_up,
    up_bias,
    w_down,
    down_bias,
    norm2_gain,
    norm2_shift,
    cotangent,
):
    tok_rows = layer_in.shape[0]
    model_width = layer_in.shape[1]
    slot_count = tok_rows // CH
    col_count = w_qkv.shape[2]
    head_count = col_count // HD
    score_scale = HD ** (-0.5)
    first_stretch, stretch_span, stretch_slot = stretch_tables(slot_stretch, seq_stretches)
    group_index = lax.axis_index("batch")
    local_stretches = lax.dynamic_slice_in_dim(slot_stretch, group_index * slot_count, slot_count)
    local_first = lookup(first_stretch, local_stretches)
    local_span = lookup(stretch_span, local_stretches)
    proj_weight = w_qkv.reshape(model_width, 3 * col_count)
    projected = jnp.dot(layer_in, proj_weight, preferred_element_type=jnp.float32)
    queries = (projected[:, :col_count] + qv_bias[0]).astype(jnp.bfloat16)
    key_rows = projected[:, col_count : 2 * col_count].astype(jnp.bfloat16)
    value_rows = (projected[:, 2 * col_count :] + qv_bias[1]).astype(jnp.bfloat16)
    query_slots = queries.reshape(slot_count, CH, col_count)
    own_keys = key_rows.reshape(slot_count, CH, col_count)
    own_values = value_rows.reshape(slot_count, CH, col_count)
    key_all, value_all = (
        lax.all_gather(own_keys, "batch", axis=0, tiled=True),
        lax.all_gather(own_values, "batch", axis=0, tiled=True),
    )

    def attend(inputs):
        query_block, begin_stretch, length = inputs

        def norm_step(offset, running):
            row_max, row_total = running
            key_slot = pick_one(stretch_slot, begin_stretch + offset)
            score_block = head_scores(query_block, pick_one(key_all, key_slot), head_count)
            new_max = jnp.maximum(row_max, jnp.max(score_block, axis=-1))
            row_total = row_total * jnp.exp(row_max - new_max) + jnp.sum(
                jnp.exp(score_block - new_max[..., None]), axis=-1
            )
            return (new_max, row_total)

        initial = (
            jnp.full((head_count, CH), -1e30, jnp.float32),
            jnp.zeros((head_count, CH), jnp.float32),
        )
        row_max, row_total = lax.fori_loop(0, length, norm_step, initial)
        log_total = row_max + jnp.log(row_total)

        def value_step(offset, summed):
            key_slot = pick_one(stretch_slot, begin_stretch + offset)
            score_block = head_scores(query_block, pick_one(key_all, key_slot), head_count)
            weights = jnp.exp(score_block - log_total[..., None]).astype(jnp.bfloat16)
            value_heads = split_heads(pick_one(value_all, key_slot), head_count)
            return summed + jnp.einsum(
                "hqk,khd->qhd", weights, value_heads, preferred_element_type=jnp.float32
            )

        summed = lax.fori_loop(0, length, value_step, jnp.zeros((CH, head_count, HD), jnp.float32))
        return (summed.reshape(CH, col_count), log_total)

    context, log_totals = lax.map(attend, (query_slots, local_first, local_span))
    context = context.reshape(tok_rows, col_count)
    context_low = context.astype(jnp.bfloat16)
    attn_part = jnp.dot(context_low, w_out, preferred_element_type=jnp.float32)
    hidden = (
        layer_in.astype(jnp.float32)
        + lax.psum(attn_part.astype(jnp.bfloat16), "head").astype(jnp.float32)
        + out_bias
    )
    first_norm, normed_one, inv_one = norm_forward(hidden, norm1_gain, norm1_shift)
    first_low = first_norm.astype(jnp.bfloat16)
    pre_act = jnp.dot(first_low, w_up, preferred_element_type=jnp.float32) + up_bias
    activation, gelu_back = jax.vjp(gelu_exact, pre_act)
    act_low = activation.astype(jnp.bfloat16)
    down_part = jnp.dot(act_low, w_down, preferred_element_type=jnp.float32)
    second_in = (
        first_norm
        + lax.psum(down_part.astype(jnp.bfloat16), "head").astype(jnp.float32)
        + down_bias
    )
    normed_out, normed_two, inv_two = norm_forward(second_in, norm2_gain, norm2_shift)
    grad_second, grad_gain_two, grad_shift_two = norm_backward(
        cotangent.astype(jnp.float32), normed_two, inv_two, norm2_gain
    )
    layer_out = normed_out.astype(jnp.bfloat16)
    second_low = grad_second.astype(jnp.bfloat16)
    grad_down = jnp.einsum("tf,td->fd", act_low, second_low, preferred_element_type=jnp.float32)
    grad_down_bias = jnp.sum(grad_second, axis=0)
    grad_act = jnp.einsum("td,fd->tf", second_low, w_down, preferred_element_type=jnp.float32)
    grad_pre_low = gelu_back(grad_act)[0].astype(jnp.bfloat16)
    grad_up = jnp.einsum("td,tf->df", first_low, grad_pre_low, preferred_element_type=jnp.float32)
    grad_up_bias = jnp.sum(grad_pre_low.astype(jnp.float32), axis=0)
    ffn_back = jnp.einsum("tf,df->td", grad_pre_low, w_up, preferred_element_type=jnp.float32)
    grad_first = lax.psum(ffn_back.astype(jnp.bfloat16), "head").astype(jnp.float32) + grad_second
    grad_hidden, grad_gain_one, grad_shift_one = norm_backward(
        grad_first, normed_one, inv_one, norm1_gain
    )
    grad_out_bias = jnp.sum(grad_hidden, axis=0)
    hidden_low = grad_hidden.astype(jnp.bfloat16)
    grad_out = jnp.einsum("tc,td->cd", context_low, hidden_low, preferred_element_type=jnp.float32)
    grad_context = jnp.einsum(
        "td,cd->tc", hidden_low, w_out, preferred_element_type=jnp.float32
    ).astype(jnp.bfloat16)
    delta_rows = jnp.sum(
        (grad_context.astype(jnp.float32) * context).reshape(tok_rows, head_count, HD), axis=-1
    )
    delta_slots = jnp.swapaxes(delta_rows.reshape(slot_count, CH, head_count), 1, 2)
    grad_slots = grad_context.reshape(slot_count, CH, col_count)

    def back_slot(key_total, inputs):
        query_block, grad_block, log_total, delta_block, begin_stretch, length = inputs

        def key_step(offset, running):
            grad_query, key_sum = running
            key_slot = pick_one(stretch_slot, begin_stretch + offset)
            key_block = pick_one(key_all, key_slot)
            value_block = pick_one(value_all, key_slot)
            weights_low, grad_score = score_grads(
                query_block, key_block, value_block, grad_block, log_total, delta_block, head_count
            )
            grad_query = (
                grad_query
                + jnp.einsum(
                    "hqk,khd->qhd",
                    grad_score,
                    split_heads(key_block, head_count),
                    preferred_element_type=jnp.float32,
                )
                * score_scale
            )
            grad_key = (
                jnp.einsum(
                    "hqk,qhd->khd",
                    grad_score,
                    split_heads(query_block, head_count),
                    preferred_element_type=jnp.float32,
                )
                * score_scale
            )
            grad_value = jnp.einsum(
                "hqk,qhd->khd",
                weights_low,
                split_heads(grad_block, head_count),
                preferred_element_type=jnp.float32,
            )
            update = jnp.concatenate(
                [grad_key.reshape(CH, col_count), grad_value.reshape(CH, col_count)], axis=1
            )
            key_sum = lax.dynamic_update_index_in_dim(
                key_sum, pick_one(key_sum, key_slot) + update, key_slot, 0
            )
            return (grad_query, key_sum)

        start_state = (jnp.zeros((CH, head_count, HD), jnp.float32), key_total)
        grad_query, key_total = lax.fori_loop(0, length, key_step, start_state)
        return (key_total, grad_query.reshape(CH, col_count))

    key_start = jnp.zeros((key_all.shape[0], CH, 2 * col_count), jnp.float32)
    key_total, grad_query_slots = lax.scan(
        back_slot,
        key_start,
        (query_slots, grad_slots, log_totals, delta_slots, local_first, local_span),
    )
    key_grads = lax.psum_scatter(
        key_total.astype(jnp.bfloat16), "batch", scatter_dimension=0, tiled=True
    ).astype(jnp.float32)
    grad_keys = key_grads[:, :, :col_count].astype(jnp.bfloat16)
    grad_values = key_grads[:, :, col_count:].astype(jnp.bfloat16)
    grad_queries = grad_query_slots.reshape(tok_rows, col_count).astype(jnp.bfloat16)
    grad_keys = grad_keys.reshape(tok_rows, col_count)
    grad_values = grad_values.reshape(tok_rows, col_count)
    grad_proj = jnp.concatenate([grad_queries, grad_keys, grad_values], axis=1)
    grad_qkv = jnp.einsum(
        "td,tc->dc", layer_in, grad_proj, preferred_element_type=jnp.float32
    ).reshape(model_width, 3, col_count)
    grad_qv = jnp.stack(
        [
            jnp.sum(grad_queries.astype(jnp.float32), axis=0),
            jnp.sum(grad_values.astype(jnp.float32), axis=0),
        ]
    )
    input_part = jnp.einsum("tc,dc->td", grad_proj, proj_weight, preferred_element_type=jnp.float32)
    own_width = model_width // lax.axis_size("head")
    own_grad = lax.dynamic_slice_in_dim(
        grad_hidden, lax.axis_index("head") * own_width, own_width, 1
    )
    grad_in = (
        lax.psum_scatter(
            input_part.astype(jnp.bfloat16), "head", scatter_dimension=1, tiled=True
        ).astype(jnp.float32)
        + own_grad
    )
    totals = (
        lax.psum(grad_qkv.astype(jnp.bfloat16), "batch").astype(jnp.float32),
        lax.psum(grad_qv.astype(jnp.bfloat16), "batch").astype(jnp.float32),
        lax.psum(grad_out.astype(jnp.bfloat16), "batch").astype(jnp.float32),
        lax.psum(grad_out_bias.astype(jnp.bfloat16), "batch").astype(jnp.float32),
        lax.psum(grad_gain_one.astype(jnp.bfloat16), "batch").astype(jnp.float32),
        lax.psum(grad_shift_one.astype(jnp.bfloat16), "batch").astype(jnp.float32),
        lax.psum(grad_up.astype(jnp.bfloat16), "batch").astype(jnp.float32),
        lax.psum(grad_up_bias.astype(jnp.bfloat16), "batch").astype(jnp.float32),
        lax.psum(grad_down.astype(jnp.bfloat16), "batch").astype(jnp.float32),
        lax.psum(grad_down_bias.astype(jnp.bfloat16), "batch").astype(jnp.float32),
        lax.psum(grad_gain_two.astype(jnp.bfloat16), "batch").astype(jnp.float32),
        lax.psum(grad_shift_two.astype(jnp.bfloat16), "batch").astype(jnp.float32),
    )
    return (
        layer_out,
        grad_in,
        totals[0],
        totals[1],
        totals[2],
        totals[3],
        totals[4],
        totals[5],
        totals[6],
        totals[7],
        totals[8],
        totals[9],
        totals[10],
        totals[11],
    )


MAXCH = 6
LOG2E = 1.4426950408889634
SCORE = HD ** (-0.5)
SWAP = [(0, 1), (1, 0)]
VMEM_LIMIT = 56 * 1024 * 1024


def nt(left, right):
    return lax.dot_general(
        left, right, (((1,), (1,)), ((), ())), preferred_element_type=jnp.float32
    )


def mm(left, right):
    return jnp.dot(left, right, preferred_element_type=jnp.float32)


def low_half(block):
    lane = lax.broadcasted_iota(jnp.int32, block.shape, 1)
    return lane < HD


def unfold(packed):
    wide = packed.astype(jnp.float32)
    return wide, pltpu.roll(wide, HD, 1)


def project_kernel(side_ref, x_ref, wq_ref, wk_ref, wv_ref, bias_ref, kv_ref, far_ref, near_ref):
    order = pl.program_id(1)
    rows = x_ref[...]
    q_all = mm(rows, wq_ref[0]) + bias_ref[0:1, :].astype(jnp.float32)
    k_all = mm(rows, wk_ref[0])
    v_all = mm(rows, wv_ref[0]) + bias_ref[1:2, :].astype(jnp.float32)
    packs = []
    for pair in range(q_all.shape[1] // 128):
        cols = slice(pair * 128, pair * 128 + 128)
        q_pair, k_pair, v_pair = q_all[:, cols], k_all[:, cols], v_all[:, cols]
        low = low_half(q_pair)
        kv_ref[2 * pair] = jnp.where(low, k_pair, pltpu.roll(v_pair, HD, 1)).astype(jnp.bfloat16)
        kv_ref[2 * pair + 1] = jnp.where(low, pltpu.roll(k_pair, HD, 1), v_pair).astype(
            jnp.bfloat16
        )
        top, bottom = q_pair[: CH // 2], q_pair[CH // 2 :]
        low = low[: CH // 2]
        packs.append(jnp.where(low, top, pltpu.roll(bottom, HD, 1)).astype(jnp.bfloat16))
        packs.append(jnp.where(low, pltpu.roll(top, HD, 1), bottom).astype(jnp.bfloat16))

    @pl.when(order == 0)
    def _():
        for head, pack in enumerate(packs):
            far_ref[head] = pack

    @pl.when(order == 1)
    def _():
        for head, pack in enumerate(packs):
            near_ref[head] = pack


def project(side, layer_in, weight, bias):
    width = layer_in.shape[1]
    heads = weight.shape[2] // HD
    step = 4
    groups = heads // step
    cols = step * HD

    def slot_of(order, side_ref):
        return (order + side_ref[0] + 1) % 2

    return pl.pallas_call(
        project_kernel,
        grid_spec=pltpu.PrefetchScalarGridSpec(
            num_scalar_prefetch=1,
            grid=(groups, 2),
            in_specs=[
                pl.BlockSpec((CH, width), lambda g, o, side: (slot_of(o, side), 0)),
                pl.BlockSpec((1, width, cols), lambda g, o, side: (0, 0, g)),
                pl.BlockSpec((1, width, cols), lambda g, o, side: (1, 0, g)),
                pl.BlockSpec((1, width, cols), lambda g, o, side: (2, 0, g)),
                pl.BlockSpec((2, cols), lambda g, o, side: (0, g)),
            ],
            out_specs=[
                pl.BlockSpec((step, CH, 128), lambda g, o, side: (g, slot_of(o, side), 0)),
                pl.BlockSpec((step, CH // 2, 128), lambda g, o, side: (g, 0, 0)),
                pl.BlockSpec((step, CH // 2, 128), lambda g, o, side: (g, 0, 0)),
            ],
        ),
        out_shape=[
            jax.ShapeDtypeStruct((heads, 2 * CH, 128), jnp.bfloat16),
            jax.ShapeDtypeStruct((heads, CH // 2, 128), jnp.bfloat16),
            jax.ShapeDtypeStruct((heads, CH // 2, 128), jnp.bfloat16),
        ],
        compiler_params=pltpu.CompilerParams(vmem_limit_bytes=VMEM_LIMIT),
        cost_estimate=pl.CostEstimate(
            flops=6 * layer_in.size * weight.shape[2],
            bytes_accessed=2 * (layer_in.size + weight.size) + 6 * layer_in.size,
            transcendentals=0,
        ),
        name="project",
    )(side, layer_in, weight, weight, weight, bias)


def fill_tables(slot_ref, seq_ref, stretch_slot, seq_first, seq_length):
    def place(slot, carry):
        stretch_slot[slot_ref[slot]] = slot
        return carry

    lax.fori_loop(0, slot_ref.shape[0], place, 0)

    def one_sequence(seq, start):
        length = seq_ref[seq]

        def one_stretch(offset, carry):
            seq_first[start + offset] = start
            seq_length[start + offset] = length
            return carry

        lax.fori_loop(0, length, one_stretch, 0)
        return start + length

    lax.fori_loop(0, seq_ref.shape[0], one_sequence, jnp.int32(0))


def key_index(slot, core, half):
    own = ((slot >> 1) & 1) == core
    return jnp.where(own, 0, half) + ((slot >> 2) << 1) + (slot & 1)


def load_keys(own_hbm, other_hbm, keys, sem):
    half = own_hbm.shape[0]
    first = pltpu.make_async_copy(own_hbm, keys.at[pl.ds(0, half)], sem.at[0])
    second = pltpu.make_async_copy(other_hbm, keys.at[pl.ds(half, half)], sem.at[1])
    first.start()
    second.start()
    first.wait()
    second.wait()


def my_slot(place_ref, chip):
    return 4 * chip + 2 * place_ref[0] + place_ref[1]


def attend_kernel(
    slot_ref,
    seq_ref,
    place_ref,
    q_ref,
    own_hbm,
    other_hbm,
    ctx_ref,
    ctx_t_ref,
    lse_ref,
    keys,
    values_t,
    held,
    stretch_slot,
    seq_first,
    seq_length,
    sem,
):
    chip = pl.program_id(0)
    half = own_hbm.shape[0]

    @pl.when(chip == 0)
    def _():
        load_keys(own_hbm, other_hbm, keys, sem)
        fill_tables(slot_ref, seq_ref, stretch_slot, seq_first, seq_length)

        def turn(index, carry):
            values_t[index] = keys[index].T[HD:128, :]
            return carry

        lax.fori_loop(0, 2 * half, turn, 0)

    core = place_ref[0]
    stretch = slot_ref[my_slot(place_ref, chip)]
    begin, length = seq_first[stretch], seq_length[stretch]
    part = CH // 2
    low = low_half(q_ref[0])
    queries = [jnp.where(low, q, 0.0).astype(jnp.bfloat16) for q in unfold(q_ref[0])]

    def scores(offset, tops):
        index = key_index(stretch_slot[begin + offset], core, half)
        block = keys[index]
        fresh = []
        for n in range(2):
            score = nt(block, queries[n]) * (SCORE * LOG2E)
            held[offset, :, n * part : (n + 1) * part] = score
            fresh.append(jnp.maximum(tops[n], jnp.max(score.reshape(CH // 8, 8, part), axis=0)))
        return tuple(fresh)

    lowest = jnp.full((8, part), -3e38, jnp.float32)
    tops = lax.fori_loop(0, length, scores, (lowest, lowest))
    tops = [jnp.max(top, axis=0, keepdims=True) for top in tops]

    def step(offset, state):
        index = key_index(stretch_slot[begin + offset], core, half)
        block_t = values_t[index]
        fresh = []
        for n in range(2):
            total, acc = state[n]
            weight = jnp.exp2(held[offset, :, n * part : (n + 1) * part] - tops[n])
            total = total + jnp.sum(weight.reshape(CH // 8, 8, part), axis=0)
            acc = acc + mm(block_t, weight.astype(jnp.bfloat16))
            fresh.append((total, acc))
        return tuple(fresh)

    start = (jnp.zeros((8, part), jnp.float32), jnp.zeros((HD, part), jnp.float32))
    final = lax.fori_loop(0, length, step, (start, start))
    final = [(tops[n], jnp.sum(final[n][0], axis=0, keepdims=True), final[n][1]) for n in range(2)]
    for n in range(2):
        top, total, acc = final[n]
        cols = slice(n * part, (n + 1) * part)
        context_t = acc / total
        ctx_t_ref[0, :, cols] = context_t
        lse_ref[0, :, cols] = top + jnp.log2(total)
        ctx_ref[0, :, n * HD : (n + 1) * HD] = context_t.T.astype(jnp.bfloat16)


def table_scratch(stretches):
    return [pltpu.SMEM((stretches,), jnp.int32) for _ in range(3)] + [
        pltpu.SemaphoreType.DMA((2,))
    ]


def attend(slot_stretch, seq_stretches, place, q_pack, own_keys, other_keys):
    chips = q_pack.shape[0]
    keys = 2 * own_keys.shape[0]
    stretches = slot_stretch.shape[0]
    pairs = chips * 5 * CH * CH
    return pl.pallas_call(
        attend_kernel,
        grid_spec=pltpu.PrefetchScalarGridSpec(
            num_scalar_prefetch=3,
            grid=(chips,),
            in_specs=[
                pl.BlockSpec((1, CH // 2, 128), lambda z, *_: (z, 0, 0)),
                pl.BlockSpec(memory_space=pl.ANY),
                pl.BlockSpec(memory_space=pl.ANY),
            ],
            out_specs=[
                pl.BlockSpec((1, CH // 2, 128), lambda z, *_: (z, 0, 0)),
                pl.BlockSpec((1, HD, CH), lambda z, *_: (z, 0, 0)),
                pl.BlockSpec((1, 1, CH), lambda z, *_: (z, 0, 0)),
            ],
            scratch_shapes=[
                pltpu.VMEM((keys, CH, 128), jnp.bfloat16),
                pltpu.VMEM((keys, HD, CH), jnp.bfloat16),
                pltpu.VMEM((MAXCH, CH, CH), jnp.float32),
            ]
            + table_scratch(stretches),
        ),
        out_shape=[
            jax.ShapeDtypeStruct((chips, CH // 2, 128), jnp.bfloat16),
            jax.ShapeDtypeStruct((chips, HD, CH), jnp.float32),
            jax.ShapeDtypeStruct((chips, 1, CH), jnp.float32),
        ],
        compiler_params=pltpu.CompilerParams(vmem_limit_bytes=24 * 1024 * 1024),
        cost_estimate=pl.CostEstimate(
            flops=HD * pairs, bytes_accessed=16 * q_pack.size, transcendentals=0
        ),
        name="attend",
    )(slot_stretch, seq_stretches, place, q_pack, own_keys, other_keys)


def attend_back_kernel(first, slot_ref, seq_ref, place_ref, *refs):
    q_ref, g_ref, ctx_t_ref, lse_ref, own_hbm, other_hbm = refs[:6]
    if first:
        dq_ref, total_ref = refs[6:8]
    else:
        total_hbm, dq_ref, own_grad_ref, other_grad_ref = refs[6:10]
    keys, keys_t, grads, stretch_slot, seq_first, seq_length, sem = refs[-7:]
    chip = pl.program_id(0)
    half = own_hbm.shape[0]

    @pl.when(chip == 0)
    def _():
        if not first:
            copy = pltpu.make_async_copy(total_hbm, grads, sem.at[2])
            copy.start()
        load_keys(own_hbm, other_hbm, keys, sem)
        fill_tables(slot_ref, seq_ref, stretch_slot, seq_first, seq_length)

        def turn(index, carry):
            keys_t[index] = keys[index].T[0:HD, :]
            if first:
                grads[index] = jnp.zeros((CH, 128), jnp.float32)
            return carry

        lax.fori_loop(0, 2 * half, turn, 0)
        if not first:
            copy.wait()

    core = place_ref[0]
    stretch = slot_ref[my_slot(place_ref, chip)]
    begin, length = seq_first[stretch], seq_length[stretch]
    part = CH // 2
    low = low_half(q_ref[0])
    queries = [jnp.where(low, q, 0.0).astype(jnp.bfloat16) for q in unfold(q_ref[0])]
    wide, rolled = unfold(g_ref[0])
    slopes = [jnp.where(low, 0.0, g) for g in (rolled, wide)]
    delta = [
        jnp.sum(slopes[n].T[HD:128, :] * ctx_t_ref[0, :, n * part : (n + 1) * part], axis=0)[None]
        for n in range(2)
    ]
    slopes = [g.astype(jnp.bfloat16) for g in slopes]
    lse = [lse_ref[0, :, n * part : (n + 1) * part] for n in range(2)]

    def step(offset, state):
        index = key_index(stretch_slot[begin + offset], core, half)
        block = keys[index]
        block_t = keys_t[index]
        fresh = []
        total = None
        for n in range(2):
            score = nt(block, queries[n]) * (SCORE * LOG2E)
            weight = jnp.exp2(score - lse[n])
            slope = weight * (nt(block, slopes[n]) - delta[n])
            slope = slope.astype(jnp.bfloat16)
            weight = weight.astype(jnp.bfloat16)
            fresh.append(state[n] + mm(block_t, slope))
            update = mm(slope, queries[n]) + mm(weight, slopes[n])
            total = update if total is None else total + update
        grads[index] += total
        return tuple(fresh)

    start = tuple(jnp.zeros((HD, part), jnp.float32) for _ in range(2))
    final = lax.fori_loop(0, length, step, start)
    for n in range(2):
        dq_ref[0, :, n * HD : (n + 1) * HD] = (final[n] * SCORE).T.astype(jnp.bfloat16)

    @pl.when(chip == pl.num_programs(0) - 1)
    def _():
        if first:
            copy = pltpu.make_async_copy(grads, total_ref, sem.at[2])
            copy.start()
            copy.wait()
        else:
            scale = jnp.where(low_half(keys[0]), SCORE, 1.0)

            def leave(index, carry):
                own_grad_ref[index] = (grads[index] * scale).astype(jnp.bfloat16)
                other_grad_ref[index] = (grads[half + index] * scale).astype(jnp.bfloat16)
                return carry

            lax.fori_loop(0, half, leave, 0)


def attend_back(tables, place, q_pack, g_pack, ctx_t, lse, own_keys, other_keys, total=None):
    first = total is None
    chips = q_pack.shape[0]
    slots = own_keys.shape[0]
    stretches = tables[0].shape[0]
    pairs = chips * 5 * CH * CH
    pack = pl.BlockSpec((1, CH // 2, 128), lambda z, *_: (z, 0, 0))
    anywhere = pl.BlockSpec(memory_space=pl.ANY)
    in_specs = [
        pack,
        pack,
        pl.BlockSpec((1, HD, CH), lambda z, *_: (z, 0, 0)),
        pl.BlockSpec((1, 1, CH), lambda z, *_: (z, 0, 0)),
        anywhere,
        anywhere,
    ]
    pack_shape = jax.ShapeDtypeStruct((chips, CH // 2, 128), jnp.bfloat16)
    if first:
        out_specs = [pack, anywhere]
        out_shape = [pack_shape, jax.ShapeDtypeStruct((2 * slots, CH, 128), jnp.float32)]
    else:
        in_specs = in_specs + [anywhere]
        whole = pl.BlockSpec((slots, CH, 128), lambda z, *_: (0, 0, 0))
        out_specs = [pack, whole, whole]
        out_shape = [
            pack_shape,
            jax.ShapeDtypeStruct((slots, CH, 128), jnp.bfloat16),
            jax.ShapeDtypeStruct((slots, CH, 128), jnp.bfloat16),
        ]
    operands = (q_pack, g_pack, ctx_t, lse, own_keys, other_keys) + (() if first else (total,))
    return pl.pallas_call(
        functools.partial(attend_back_kernel, first),
        grid_spec=pltpu.PrefetchScalarGridSpec(
            num_scalar_prefetch=3,
            grid=(chips,),
            in_specs=in_specs,
            out_specs=out_specs,
            scratch_shapes=[
                pltpu.VMEM((2 * slots, CH, 128), jnp.bfloat16),
                pltpu.VMEM((2 * slots, HD, CH), jnp.bfloat16),
                pltpu.VMEM((2 * slots, CH, 128), jnp.float32),
            ]
            + table_scratch(stretches)[:3]
            + [pltpu.SemaphoreType.DMA((3,))],
        ),
        out_shape=out_shape,
        compiler_params=pltpu.CompilerParams(vmem_limit_bytes=36 * 1024 * 1024),
        cost_estimate=pl.CostEstimate(
            flops=HD * pairs, bytes_accessed=24 * q_pack.size, transcendentals=0
        ),
        name="attend_back",
    )(*tables, place, *operands)


def swap_across(block, axis_name):
    return lax.ppermute(block, axis_name, SWAP)


def spread(block):
    return lax.all_to_all(block, ("z", "y"), 0, 0, tiled=True)


def gelu_both(pre):
    phi = 0.5 + 0.5 * lax.erf(pre * (2.0**-0.5))
    density = jnp.exp(-0.5 * pre * pre) * ((2.0 * math.pi) ** -0.5)
    return ((pre * phi).astype(jnp.bfloat16), phi + pre * density)


def tn(left, right):
    return lax.dot_general(
        left, right, (((0,), (0,)), ((), ())), preferred_element_type=jnp.float32
    )


BLOCK = 64
TILE = 256


def row_block(step):
    return pl.ds(pl.multiple_of(step * BLOCK, BLOCK), BLOCK)


def weight_slot(part, side):
    return 2 * (part % 2) + (side if part < 2 else 1 - side)


def forward_kernel(side_ref, own_pack, far_pack, layer_in, cotangent, vectors_ref, bias_ref, *refs):
    up_hbm, down_hbm, out_hbm = refs[0:4], refs[4:8], refs[8:10]
    out_ref, ctx_ref, first_low, act_ref, slope_ref, second_low, grad_second = refs[10:17]
    normed_one, inv_one, sums_ref = refs[17:20]
    ups, downs, outs, rows_in, cot, acc, first_norm, sem = refs[20:]
    low = jnp.bfloat16
    width = acc.shape[1]
    start = pl.multiple_of(side_ref[0] * CH, CH)
    copies = [
        pltpu.make_async_copy(layer_in.at[pl.ds(start, CH)], rows_in, sem.at[0]),
        pltpu.make_async_copy(out_hbm[0], outs.at[0], sem.at[1]),
        pltpu.make_async_copy(out_hbm[1], outs.at[1], sem.at[2]),
    ]
    copies.append(pltpu.make_async_copy(cotangent.at[pl.ds(start, CH)], cot, sem.at[11]))
    for copy in copies[:3]:
        copy.start()
    for n in range(4):
        slot = weight_slot(n, side_ref[0])
        pltpu.make_async_copy(up_hbm[n], ups.at[slot], sem.at[3 + 2 * slot]).start()
        pltpu.make_async_copy(down_hbm[n], downs.at[slot], sem.at[4 + 2 * slot]).start()
    copies[3].start()
    out_bias, gain_one, shift_one, down_bias, gain_two, shift_two = (
        vectors_ref[n : n + 1, :] for n in range(6)
    )
    heads = own_pack.shape[0]
    half = CH // 2

    for source, pack in enumerate((own_pack, far_pack)):
        for pair in range(heads // 2):
            first, first_roll = unfold(pack[2 * pair])
            second, second_roll = unfold(pack[2 * pair + 1])
            lanes = low_half(first)
            base = (source * heads // 2 + pair) * 128
            ctx_ref[0:half, base : base + 128] = jnp.where(lanes, first, second_roll).astype(low)
            ctx_ref[half:CH, base : base + 128] = jnp.where(lanes, first_roll, second).astype(low)
    for copy in copies[:3]:
        copy.wait()
    span = heads * HD
    acc[...] = mm(ctx_ref[:, 0:span], outs[0]) + mm(ctx_ref[:, span : 2 * span], outs[1])

    def first_step(step, carry):
        at = row_block(step)
        hidden = rows_in[at, :].astype(jnp.float32) + acc[at, :] + out_bias
        value, normed, inv = norm_forward(hidden, gain_one, shift_one)
        first_norm[at, :] = value
        normed_one[at, :] = normed
        inv_one[at, :] = jnp.broadcast_to(inv, (BLOCK, 128))
        first_low[at, :] = value.astype(low)
        return carry

    lax.fori_loop(0, CH // BLOCK, first_step, 0)
    acc[...] = jnp.zeros(acc.shape, jnp.float32)

    def forward(n, carry):
        pltpu.make_async_copy(up_hbm[0], ups.at[n], sem.at[3 + 2 * n]).wait()
        base = pl.multiple_of(n * width, width)
        for c in range(0, width, TILE):
            for r in range(0, CH, TILE):
                rows = slice(r, r + TILE)
                pre = mm(first_low[rows, :], ups[n, :, c : c + TILE]) + bias_ref[n, :, c : c + TILE]
                act, slope = gelu_both(pre)
                act_ref[rows, pl.ds(base + c, TILE)] = act
                slope_ref[rows, pl.ds(base + c, TILE)] = slope.astype(low)
        pltpu.make_async_copy(down_hbm[0], downs.at[n], sem.at[4 + 2 * n]).wait()
        acc[...] += mm(act_ref[:, pl.ds(base, width)], downs[n])
        return carry

    lax.fori_loop(0, 4, forward, 0)
    copies[-1].wait()
    zero = jnp.zeros((1, width), jnp.float32)

    def second_step(step, carry):
        at = row_block(step)
        second = first_norm[at, :] + acc[at, :] + down_bias
        value, normed, inv = norm_forward(second, gain_two, shift_two)
        out_ref[at, :] = value.astype(low)
        gradient = cot[at, :].astype(jnp.float32)
        grad, gain_sum, shift_sum = norm_backward(gradient, normed, inv, gain_two)
        grad_second[at, :] = grad
        second_low[at, :] = grad.astype(low)
        return (
            carry[0] + jnp.sum(grad, axis=0, keepdims=True),
            carry[1] + gain_sum[None],
            carry[2] + shift_sum[None],
        )

    sums = lax.fori_loop(0, CH // BLOCK, second_step, (zero, zero, zero))
    for n in range(3):
        sums_ref[n : n + 1, :] = sums[n]


def backward_kernel(side_ref, slope_ref, second_low, grad_second, normed_one, inv_one, gain_ref, *refs):
    up_hbm, down_hbm, out_hbm = refs[0:4], refs[4:8], refs[8:10]
    grad_pre_ref, hidden_ref, hidden_low, gc_own, gc_far, sums_ref, bias_grad_ref = refs[10:17]
    ups, downs, outs, acc, sem = refs[17:]
    low = jnp.bfloat16
    width = acc.shape[1]
    for n in range(4):
        slot = weight_slot(n, side_ref[0])
        pltpu.make_async_copy(down_hbm[n], downs.at[slot], sem.at[2 * slot]).start()
        pltpu.make_async_copy(up_hbm[n], ups.at[slot], sem.at[2 * slot + 1]).start()
    copies = [pltpu.make_async_copy(out_hbm[n], outs.at[n], sem.at[8 + n]) for n in range(2)]
    for copy in copies:
        copy.start()
    heads = gc_own.shape[0]
    half = CH // 2
    acc[...] = jnp.zeros(acc.shape, jnp.float32)

    def backward(n, carry):
        pltpu.make_async_copy(down_hbm[0], downs.at[n], sem.at[2 * n]).wait()
        base = pl.multiple_of(n * width, width)
        for c in range(0, width, TILE):
            total = None
            for r in range(0, CH, TILE):
                rows = slice(r, r + TILE)
                grad_act = nt(second_low[rows, :], downs[n, c : c + TILE, :])
                slope = slope_ref[rows, pl.ds(base + c, TILE)].astype(jnp.float32)
                grad_pre = (grad_act * slope).astype(low)
                grad_pre_ref[rows, pl.ds(base + c, TILE)] = grad_pre
                part = jnp.sum(grad_pre.astype(jnp.float32), axis=0, keepdims=True)
                total = part if total is None else total + part
            bias_grad_ref[n, :, c : c + TILE] = total
        pltpu.make_async_copy(up_hbm[0], ups.at[n], sem.at[2 * n + 1]).wait()
        acc[...] += nt(grad_pre_ref[:, pl.ds(base, width)], ups[n])
        return carry

    lax.fori_loop(0, 4, backward, 0)
    zero = jnp.zeros((1, width), jnp.float32)
    gain_one = gain_ref[...]

    def last_step(step, carry):
        at = row_block(step)
        gradient = acc[at, :] + grad_second[at, :]
        grad, gain_sum, shift_sum = norm_backward(
            gradient, normed_one[at, :], inv_one[at, 0:1], gain_one
        )
        hidden_ref[at, :] = grad
        hidden_low[at, :] = grad.astype(low)
        return (
            carry[0] + jnp.sum(grad, axis=0, keepdims=True),
            carry[1] + gain_sum[None],
            carry[2] + shift_sum[None],
        )

    sums = lax.fori_loop(0, CH // BLOCK, last_step, (zero, zero, zero))
    for n in range(3):
        sums_ref[n : n + 1, :] = sums[n]
    for copy in copies:
        copy.wait()
    for source, pack in enumerate((gc_own, gc_far)):
        for pair in range(heads // 2):
            both = nt(hidden_low[...], outs[source, pair * 128 : pair * 128 + 128, :])
            top, bottom = both[:half], both[half:]
            lanes = low_half(top)
            pack[2 * pair] = jnp.where(lanes, top, pltpu.roll(bottom, HD, 1)).astype(low)
            pack[2 * pair + 1] = jnp.where(lanes, pltpu.roll(top, HD, 1), bottom).astype(low)


def dense_call(kernel, name, in_specs, operands, weights, shapes, scratch, width):
    low = jnp.bfloat16
    vmem, anywhere = pl.BlockSpec(memory_space=pltpu.VMEM), pl.BlockSpec(memory_space=pl.ANY)
    return pl.pallas_call(
        kernel,
        in_specs=in_specs + [anywhere] * 10,
        out_specs=[vmem] * len(shapes),
        out_shape=[jax.ShapeDtypeStruct(shape, dtype) for shape, dtype in shapes],
        scratch_shapes=[
            pltpu.VMEM((4, width, width), low),
            pltpu.VMEM((4, width, width), low),
            pltpu.VMEM((2,) + weights[-1].shape, low),
        ]
        + scratch
        + [pltpu.SemaphoreType.DMA((12,))],
        compiler_params=pltpu.CompilerParams(vmem_limit_bytes=VMEM_LIMIT),
        cost_estimate=pl.CostEstimate(
            flops=8 * CH * width * width, bytes_accessed=8 << 20, transcendentals=0
        ),
        name=name,
    )(*operands, *weights)


def forward_rows(side, own_pack, far_pack, layer_in, cotangent, vectors, biases, weights):
    width = layer_in.shape[1]
    units = 4 * width
    low = jnp.bfloat16
    vmem, anywhere = pl.BlockSpec(memory_space=pltpu.VMEM), pl.BlockSpec(memory_space=pl.ANY)
    return dense_call(
        forward_kernel,
        "forward_rows",
        [pl.BlockSpec(memory_space=pltpu.SMEM), vmem, vmem, anywhere, anywhere, vmem, vmem],
        (side, own_pack, far_pack, layer_in, cotangent, vectors, biases),
        weights,
        [
            ((CH, width), low),
            ((CH, width), low),
            ((CH, width), low),
            ((CH, units), low),
            ((CH, units), low),
            ((CH, width), low),
            ((CH, width), jnp.float32),
            ((CH, width), jnp.float32),
            ((CH, 128), jnp.float32),
            ((3, width), jnp.float32),
        ],
        [
            pltpu.VMEM((CH, width), low),
            pltpu.VMEM((CH, width), low),
            pltpu.VMEM((CH, width), jnp.float32),
            pltpu.VMEM((CH, width), jnp.float32),
        ],
        width,
    )


def backward_rows(side, slopes, second_low, grad_second, normed_one, inv_one, gain, heads, weights):
    width = second_low.shape[1]
    units = 4 * width
    low = jnp.bfloat16
    return dense_call(
        backward_kernel,
        "backward_rows",
        [pl.BlockSpec(memory_space=pltpu.SMEM)] + [pl.BlockSpec(memory_space=pltpu.VMEM)] * 6,
        (side, slopes, second_low, grad_second, normed_one, inv_one, gain),
        weights,
        [
            ((CH, units), low),
            ((CH, width), jnp.float32),
            ((CH, width), low),
            ((heads, CH // 2, 128), low),
            ((heads, CH // 2, 128), low),
            ((3, width), jnp.float32),
            ((4, 1, width), jnp.float32),
        ],
        [pltpu.VMEM((CH, width), jnp.float32)],
        width,
    )


def project_back_kernel(
    side_ref, near_ref, kv_ref, layer_t, w_ref, hidden_ref, *refs
):
    grad_w, far_out, own_out, sums_ref, grad_q, grad_k, grad_v = refs
    low = jnp.bfloat16
    side = side_ref[0]
    half = CH // 2
    heads = kv_ref.shape[0]
    near_row = pl.multiple_of(side * CH, CH)
    far_row = pl.multiple_of((1 - side) * CH, CH)
    for pair in range(heads // 2):
        cols = slice(pair * 128, pair * 128 + 128)
        for pack, base in ((near_ref, near_row), (kv_ref.at[:, 2 * CH :], far_row)):
            first, first_roll = unfold(pack[2 * pair])
            second, second_roll = unfold(pack[2 * pair + 1])
            lanes = low_half(first)
            grad_q[pl.ds(base, half), cols] = jnp.where(lanes, first, second_roll).astype(low)
            grad_q[pl.ds(base + half, half), cols] = jnp.where(lanes, first_roll, second).astype(low)
        for r in range(0, 2 * CH, half):
            rows = slice(r, r + half)
            first, first_roll = unfold(kv_ref[2 * pair, rows, :])
            second, second_roll = unfold(kv_ref[2 * pair + 1, rows, :])
            lanes = low_half(first)
            grad_k[rows, cols] = jnp.where(lanes, first, second_roll).astype(low)
            grad_v[rows, cols] = jnp.where(lanes, first_roll, second).astype(low)
    parts = (grad_q, grad_k, grad_v)
    width = layer_t.shape[0]
    own_width = width // 2
    near_cols = pl.ds(pl.multiple_of(side * own_width, own_width), own_width)
    far_cols = pl.ds(pl.multiple_of((1 - side) * own_width, own_width), own_width)
    far = own = None
    for n, part in enumerate(parts):
        far_term, own_term = nt(part[...], w_ref[n, far_cols, :]), nt(part[...], w_ref[n, near_cols, :])
        far = far_term if far is None else far + far_term
        own = own_term if own is None else own + own_term
    far_out[...] = far.astype(low)
    own_out[...] = own
    near_rows = pl.ds(near_row, CH)
    far_out[near_rows, :] = (far_out[near_rows, :].astype(jnp.float32) + hidden_ref[:, far_cols]).astype(low)
    own_out[near_rows, :] += hidden_ref[:, near_cols]
    count, _, piece, _ = grad_w.shape
    for n, part in enumerate(parts):
        total = mm(layer_t[...], part[...]).astype(low)
        grad_w[:, n] = total.reshape(count, piece, total.shape[1])
    sums_ref[0:1, :] = jnp.sum(grad_q[...].astype(jnp.float32), axis=0, keepdims=True)
    sums_ref[1:2, :] = jnp.sum(grad_v[...].astype(jnp.float32), axis=0, keepdims=True)


def project_back(side, near, kv, layer_t, weight, hidden, pieces):
    heads = kv.shape[0]
    cols = heads * HD
    width, rows = layer_t.shape
    low = jnp.bfloat16
    vmem = pl.BlockSpec(memory_space=pltpu.VMEM)
    return pl.pallas_call(
        project_back_kernel,
        in_specs=[pl.BlockSpec(memory_space=pltpu.SMEM)] + [vmem] * 5,
        out_specs=[vmem] * 4,
        out_shape=[
            jax.ShapeDtypeStruct((pieces, 3, width // pieces, cols), low),
            jax.ShapeDtypeStruct((rows, width // 2), low),
            jax.ShapeDtypeStruct((rows, width // 2), jnp.float32),
            jax.ShapeDtypeStruct((2, cols), jnp.float32),
        ],
        scratch_shapes=[pltpu.VMEM((rows, cols), low)] * 3,
        compiler_params=pltpu.CompilerParams(vmem_limit_bytes=40 * 1024 * 1024),
        cost_estimate=pl.CostEstimate(
            flops=2 * rows * width * cols, bytes_accessed=8 << 20, transcendentals=0
        ),
        name="project_back",
    )(side, near, kv, layer_t, weight, hidden)


def fast_local(
    layer_in,
    slot_stretch,
    seq_stretches,
    w_qkv,
    qv_bias,
    w_out,
    out_bias,
    norm1_gain,
    norm1_shift,
    w_up,
    up_bias,
    w_down,
    down_bias,
    norm2_gain,
    norm2_shift,
    cotangent,
):
    width = layer_in.shape[1]
    cols = w_qkv.shape[2]
    heads = cols // HD
    units = w_up.shape[1]
    half = units // 2
    side = lax.axis_index("head")
    core = lax.axis_index("core")
    far_place = jnp.stack([core, 1 - side]).astype(jnp.int32)
    near_place = jnp.stack([core, side]).astype(jnp.int32)
    side_vec = side.reshape(1).astype(jnp.int32)
    tables = (slot_stretch, seq_stretches)
    low = jnp.bfloat16

    w_three = w_qkv.transpose(1, 0, 2)
    layer_t = layer_in.T
    send_kv, send_far, send_near = project(side_vec, layer_in, w_three, qv_bias)
    send_kv, w_up, w_down, w_out, up_bias = lax.optimization_barrier(
        (send_kv, w_up, w_down, w_out, up_bias)
    )
    own_kv = spread(send_kv)
    low_slices = [
        lax.dynamic_slice_in_dim(array, place * half, half, axis)
        for array, axis in ((w_up, 1), (w_down, 0), (up_bias, 0))
        for place in (core, 1 - core)
    ]
    up_far = swap_across(low_slices[0], "head")
    own_kv, low_slices, w_out, up_far = lax.optimization_barrier(
        (own_kv, low_slices, w_out, up_far)
    )
    other_kv = swap_across(own_kv, "core")
    own_keys = own_kv.reshape(2 * heads, CH, 128)
    other_keys = other_kv.reshape(2 * heads, CH, 128)

    q_far = spread(send_far)
    q_near = spread(send_near)

    downs, biases = (
        (low_slices[n], low_slices[n + 1], swap_across(low_slices[n], "head")) for n in (2, 4)
    )
    ups, down_far = low_slices[:2], downs[2]
    w_out_far = swap_across(w_out, "head")
    ctx_far, ctx_t_far, lse_far = attend(*tables, far_place, q_far, own_keys, other_keys)
    q_near, ctx_far, down_far = lax.optimization_barrier((q_near, ctx_far, down_far))
    ctx_far = swap_across(ctx_far, "head")
    ctx_near, ctx_t_near, lse_near = attend(*tables, near_place, q_near, own_keys, other_keys)

    def row_major(pack):
        block = pack.reshape(heads, CH // 2, 2, HD).transpose(2, 1, 0, 3)
        return block.reshape(CH, cols)

    ctx_other = spread(ctx_far)
    ctx_near, up_far, down_far, w_out_far, bias_far = lax.optimization_barrier(
        (ctx_near, up_far, down_far, w_out_far, biases[2])
    )
    ctx_own = spread(ctx_near)
    up_parts = [ups[0], ups[1], up_far, swap_across(up_far, "core")]
    down_parts = [downs[0], downs[1], down_far, swap_across(down_far, "core")]
    up_biases = [biases[0], biases[1], bias_far, swap_across(bias_far, "core")]
    vectors = jnp.stack([out_bias, norm1_gain, norm1_shift, down_bias, norm2_gain, norm2_shift])
    vectors = vectors.astype(jnp.float32)
    weights = (*up_parts, *down_parts, w_out, w_out_far)
    is_low = side == 0
    own_biases, far_biases = jnp.stack(up_biases[:2]), jnp.stack(up_biases[2:])
    biases = jnp.stack(
        [jnp.where(is_low, own_biases, far_biases), jnp.where(is_low, far_biases, own_biases)],
        axis=1,
    )
    (
        out_rows,
        ctx_rows,
        first_low,
        acts,
        slopes,
        second_low,
        grad_second,
        normed_one,
        inv_one,
        second_sums,
    ) = forward_rows(
        side_vec,
        ctx_own,
        ctx_other,
        layer_in,
        cotangent,
        vectors,
        biases.astype(jnp.float32).reshape(4, 1, half),
        weights,
    )
    is_low = side == 0

    is_first = core == 0
    row = lax.axis_index("y")

    def add_low(kept, got):
        return (kept.astype(jnp.float32) + got.astype(jnp.float32)).astype(low)

    def on_chip(pair):
        return add_low(pair[0], swap_across(pair[1].astype(low), "core"))

    def halves(block, bit):
        size = block.shape[0] // 2
        return (
            lax.dynamic_slice_in_dim(block, bit * size, size, 0),
            lax.dynamic_slice_in_dim(block, (1 - bit) * size, size, 0),
        )

    def partner(block, step):
        if step == "y":
            return swap_across(block, "y")
        hop = 1 if step == "z_near" else 2
        return lax.ppermute(block, "z", [(n, n ^ hop) for n in range(lax.axis_size("z"))])

    place_in_z = lax.axis_index("z")
    bits = {"y": row, "z_near": place_in_z % 2, "z_far": place_in_z // 2}

    def reduce_send(block, step):
        kept, gone = halves(block, bits[step])
        return kept, partner(gone, step)

    def reduce_step(block, step):
        return add_low(*reduce_send(block, step))

    def gather_step(block, step):
        return in_order(bits[step] == 0, block, partner(block, step), 0)

    def scatter_sum(block):
        return lax.psum_scatter(block, ("head", "z", "y"), scatter_dimension=0, tiled=True)

    def collect(block):
        return lax.all_gather(block, ("z", "y"), axis=0, tiled=True)

    def sum_over(vector, steps):
        for step in steps:
            if step in ("core", "head"):
                vector = vector + swap_across(vector, step)
            else:
                vector = vector + partner(vector, step)
        return vector

    def in_order(bit, mine, rest, axis):
        return jnp.concatenate(
            [jnp.where(bit, mine, rest), jnp.where(bit, rest, mine)], axis=axis
        )

    def join(mine, step, axis):
        rest = partner(mine, step)
        mine_far, rest_far = swap_across(mine, "core"), swap_across(rest, "core")
        bit = bits[step] == 0
        own, other = in_order(bit, mine, rest, 0), in_order(bit, mine_far, rest_far, 0)
        return in_order(is_first, own, other, axis).astype(jnp.float32)

    half_rows = cols // 2

    def parts_of(block):
        return [block[:, n * width : (n + 1) * width] for n in range(4)]

    pair = 2 * width

    down_sum = on_chip([tn(acts[:, n : n + pair], second_low) for n in (0, pair)])
    down_sum = down_sum.reshape(2, width, width)
    down_own = lax.dynamic_index_in_dim(down_sum, side, 0, keepdims=False)
    down_far = lax.dynamic_index_in_dim(down_sum, 1 - side, 0, keepdims=False)
    down_far, grad_second = lax.optimization_barrier((down_far, grad_second))
    down_got = swap_across(down_far, "head")
    grad_pres, grad_hidden, hidden_low, gc_own, gc_far, first_sums, bias_grads = backward_rows(
        side_vec, slopes, second_low, grad_second, normed_one, inv_one, vectors[1:2], heads, weights
    )
    gc_in = swap_across(gc_far, "head")
    g_near = spread(gc_own)
    def take(block, start, size):
        return lax.dynamic_slice_in_dim(block, start, size, 1)

    up_own, up_far = (
        on_chip([tn(first_low, take(grad_pres, (n + place) * width, width)) for n in (0, 2)])
        for place in (side, 1 - side)
    )
    out_own, out_far = (
        on_chip(
            [
                tn(take(ctx_rows, base + which * half_rows, half_rows), hidden_low)
                for which in (core, 1 - core)
            ]
        )
        for base in (0, cols)
    )

    def ordered(first, second):
        return jnp.concatenate(
            [jnp.where(is_first, first, second), jnp.where(is_first, second, first)]
        )

    small = jnp.concatenate(
        [
            ordered(bias_grads[0, 0], bias_grads[2, 0]),
            ordered(bias_grads[1, 0], bias_grads[3, 0]),
            first_sums.reshape(-1),
            second_sums.reshape(-1),
        ]
    )
    small = small.reshape(-1, 128)
    small = sum_over(small.reshape(-1, 128), ("core",))
    down_kept, down_sent = halves(add_low(down_own, down_got), bits["y"])
    g_near, gc_in, up_far, out_far, small, down_sent = lax.optimization_barrier(
        (g_near, gc_in, up_far, out_far, small, down_sent)
    )
    up_got, out_got = swap_across(up_far, "head"), swap_across(out_far, "head")
    small_got = swap_across(small, "head")
    down_got = partner(down_sent, "y")
    g_far = spread(gc_in)
    dq_near, part_grad = attend_back(
        tables, near_place, q_near, g_near, ctx_t_near, lse_near, own_keys, other_keys
    )
    part_grad, g_far, down_got, up_got, out_got, small_got = lax.optimization_barrier(
        (part_grad, g_far, down_got, up_got, out_got, small_got)
    )
    both_sum = jnp.concatenate([add_low(up_own, up_got), add_low(out_own, out_got)])
    down_kept, down_sent = halves(add_low(down_kept, down_got), bits["z_near"])
    small = small + small_got
    part_grad, both_sum, small, down_sent = lax.optimization_barrier(
        (part_grad, both_sum, small, down_sent)
    )
    both_sum = lax.psum_scatter(both_sum, ("z", "y"), scatter_dimension=0, tiled=True)
    small_got = partner(small, "z_near")
    down_got = partner(down_sent, "z_near")
    dq_far, own_grad, other_grad = attend_back(
        tables, far_place, q_far, g_far, ctx_t_far, lse_far, own_keys, other_keys, part_grad
    )
    dq_near = spread(dq_near)
    own_grad, other_grad, dq_far, dq_near, small_got, down_got = lax.optimization_barrier(
        (own_grad, other_grad, dq_far, dq_near, small_got, down_got)
    )
    kv_grad = add_low(own_grad, swap_across(other_grad, "core"))
    kv_grad = jnp.concatenate([kv_grad.reshape(heads, 2 * CH, 128), dq_far], axis=1)
    kv_grad, both_sum = lax.optimization_barrier((kv_grad, both_sum))
    kv_grad = spread(kv_grad)
    small = small + small_got
    small_got = partner(small, "y")
    down_sum = reduce_step(add_low(down_kept, down_got), "z_far")
    kv_grad, small_got, both_sum, down_sum = lax.optimization_barrier(
        (kv_grad, small_got, both_sum, down_sum)
    )
    both_sum = collect(both_sum)
    small = small + small_got
    small_got = partner(small, "z_far")
    down_sum = gather_step(down_sum, "z_far")
    deep = lax.axis_size("z")
    grad_w, far_part, own_part, grad_qv = project_back(
        side_vec, dq_near, kv_grad, layer_t, w_three, grad_hidden, 4 * deep
    )
    arrived = swap_across(far_part, "head")
    kept, gone = halves(grad_w, core)
    kept, gone = halves(add_low(kept, swap_across(gone, "core")), row)
    kept = add_low(kept, swap_across(gone, "y"))
    pieces = lax.all_to_all(kept, "z", 0, 0, tiled=True)
    layer_out_pair = jnp.stack([out_rows, swap_across(out_rows, "head")])
    layer_out = jnp.where(is_low, layer_out_pair, layer_out_pair[::-1]).reshape(2 * CH, width)
    small = small + small_got
    down_sum = gather_step(down_sum, "z_near")
    grad_qv = sum_over(grad_qv.reshape(-1, 128), ("core", "y"))
    pieces, grad_qv, both_sum, down_sum = lax.optimization_barrier(
        (pieces, grad_qv, both_sum, down_sum)
    )
    mine = jnp.sum(pieces.astype(jnp.float32), axis=0).astype(low)
    every = lax.all_to_all(jnp.broadcast_to(mine[None], pieces.shape), "z", 0, 0, tiled=True)
    bit = bits["y"] == 0
    grad_down = join(down_sum, "y", 0)
    both_far = swap_across(both_sum, "core")
    grad_up = in_order(is_first, both_sum[:width], both_far[:width], 1).astype(jnp.float32)
    grad_out = in_order(is_first, both_sum[width:], both_far[width:], 0).astype(jnp.float32)
    grad_qv = sum_over(grad_qv, ("z_near", "z_far")).reshape(2, cols)
    small = small.reshape(-1)
    grad_up_bias = lax.dynamic_slice_in_dim(small, side * units, units)
    vectors = small[2 * units : 2 * units + 6 * width].reshape(6, width)
    every = in_order(bit, every, swap_across(every, "y"), 0)
    every = in_order(is_first, every, swap_across(every, "core"), 0)
    grad_qkv = every.astype(jnp.float32).transpose(0, 2, 1, 3).reshape(width, 3, cols)
    grad_in = own_part + arrived.astype(jnp.float32)
    return (
        layer_out,
        grad_in,
        grad_qkv,
        grad_qv,
        grad_out,
        vectors[0],
        vectors[1],
        vectors[2],
        grad_up,
        grad_up_bias,
        grad_down,
        vectors[3],
        vectors[4],
        vectors[5],
    )


def solution(mesh):
    batch, head = mesh.shape["batch"], mesh.shape["head"]

    def whole(*arrays):
        tokens, width = arrays[0].shape
        heads = arrays[3].shape[2] // head // HD
        fits = (
            head == 2
            and batch == 2 * heads
            and tokens == batch * 2 * CH
            and arrays[9].shape[1] % (4 * 128) == 0
        )
        if fits:
            split = Mesh(mesh.devices.reshape(batch // 4, 2, 2, head), ("z", "y", "core", "head"))
            return run(fast_local, split, ("z", "y", "core"))(*arrays)
        return run(local, mesh, "batch")(*arrays)

    return whole


def run(body, mesh, rows):
    in_specs = (
        P(rows, None),
        P(),
        P(),
        P(None, None, "head"),
        P(None, "head"),
        P("head", None),
        P(),
        P(),
        P(),
        P(None, "head"),
        P("head"),
        P("head", None),
        P(),
        P(),
        P(),
        P(rows, None),
    )
    out_specs = (
        P(rows, None),
        P(rows, "head"),
        P(None, None, "head"),
        P(None, "head"),
        P("head", None),
        P(),
        P(),
        P(),
        P(None, "head"),
        P("head"),
        P("head", None),
        P(),
        P(),
        P(),
    )
    return jax.shard_map(body, mesh=mesh, in_specs=in_specs, out_specs=out_specs, check_vma=False)
```

```python
import functools
import math

import jax
import jax.numpy as jnp
from jax import lax
from jax.experimental import pallas as pl
from jax.experimental.pallas import tpu as pltpu
from jax.sharding import Mesh
from jax.sharding import PartitionSpec as P

HD = 64
CH = 512

EPSILON = 1e-05


def norm_forward(values, gain_vec, shift_vec):
    centre = jnp.mean(values, axis=-1, keepdims=True)
    centred = values - centre
    spread = jnp.mean(centred * centred, axis=-1, keepdims=True)
    inv_std = lax.rsqrt(spread + EPSILON)
    normed = centred * inv_std
    return (normed * gain_vec + shift_vec, normed, inv_std)


def norm_backward(gradient, normed, inv_std, gain_vec):
    scaled = gradient * gain_vec
    mean_one = jnp.mean(scaled, axis=-1, keepdims=True)
    mean_two = jnp.mean(scaled * normed, axis=-1, keepdims=True)
    back_grad = inv_std * (scaled - mean_one - normed * mean_two)
    return (back_grad, jnp.sum(gradient * normed, axis=0), jnp.sum(gradient, axis=0))


def gelu_exact(values):
    return jax.nn.gelu(values, approximate=False)


def lookup(table_vec, index_vec):
    table_width = table_vec.shape[0]
    is_match = index_vec[:, None] == jnp.arange(table_width, dtype=jnp.int32)[None, :]
    return jnp.sum(jnp.where(is_match, table_vec[None, :], 0), axis=1)


def pick_one(table_vec, position):
    return lax.dynamic_index_in_dim(table_vec, position, 0, keepdims=False)


def split_heads(block, head_count):
    return block.reshape(block.shape[0], head_count, HD)


def head_scores(query_block, key_block, head_count):
    return jnp.einsum(
        "qhd,khd->hqk",
        split_heads(query_block, head_count),
        split_heads(key_block, head_count),
        preferred_element_type=jnp.float32,
    ) * HD ** (-0.5)


def score_grads(
    query_block, key_block, value_block, grad_block, log_total, delta_block, head_count
):
    weights = jnp.exp(head_scores(query_block, key_block, head_count) - log_total[..., None])
    grad_weights = jnp.einsum(
        "qhd,khd->hqk",
        split_heads(grad_block, head_count),
        split_heads(value_block, head_count),
        preferred_element_type=jnp.float32,
    )
    grad_score = (weights * (grad_weights - delta_block[..., None])).astype(jnp.bfloat16)
    return (weights.astype(jnp.bfloat16), grad_score)


def stretch_tables(slot_stretch, seq_stretches):
    stretch_count = slot_stretch.shape[0]
    seq_ends = jnp.cumsum(seq_stretches)
    seq_starts = seq_ends - seq_stretches
    stretch_index = jnp.arange(stretch_count, dtype=jnp.int32)
    seq_of = jnp.sum((stretch_index[:, None] >= seq_ends[None, :]).astype(jnp.int32), axis=1)
    first_stretch = lookup(seq_starts, seq_of)
    stretch_span = lookup(seq_stretches, seq_of)
    is_match = slot_stretch[None, :] == stretch_index[:, None]
    stretch_slot = jnp.sum(jnp.where(is_match, stretch_index[None, :], 0), axis=1)
    return (first_stretch, stretch_span, stretch_slot)


def local(
    layer_in,
    slot_stretch,
    seq_stretches,
    w_qkv,
    qv_bias,
    w_out,
    out_bias,
    norm1_gain,
    norm1_shift,
    w_up,
    up_bias,
    w_down,
    down_bias,
    norm2_gain,
    norm2_shift,
    cotangent,
):
    tok_rows = layer_in.shape[0]
    model_width = layer_in.shape[1]
    slot_count = tok_rows // CH
    col_count = w_qkv.shape[2]
    head_count = col_count // HD
    score_scale = HD ** (-0.5)
    first_stretch, stretch_span, stretch_slot = stretch_tables(slot_stretch, seq_stretches)
    group_index = lax.axis_index("batch")
    local_stretches = lax.dynamic_slice_in_dim(slot_stretch, group_index * slot_count, slot_count)
    local_first = lookup(first_stretch, local_stretches)
    local_span = lookup(stretch_span, local_stretches)
    proj_weight = w_qkv.reshape(model_width, 3 * col_count)
    projected = jnp.dot(layer_in, proj_weight, preferred_element_type=jnp.float32)
    queries = (projected[:, :col_count] + qv_bias[0]).astype(jnp.bfloat16)
    key_rows = projected[:, col_count : 2 * col_count].astype(jnp.bfloat16)
    value_rows = (projected[:, 2 * col_count :] + qv_bias[1]).astype(jnp.bfloat16)
    query_slots = queries.reshape(slot_count, CH, col_count)
    own_keys = key_rows.reshape(slot_count, CH, col_count)
    own_values = value_rows.reshape(slot_count, CH, col_count)
    key_all, value_all = (
        lax.all_gather(own_keys, "batch", axis=0, tiled=True),
        lax.all_gather(own_values, "batch", axis=0, tiled=True),
    )

    def attend(inputs):
        query_block, begin_stretch, length = inputs

        def norm_step(offset, running):
            row_max, row_total = running
            key_slot = pick_one(stretch_slot, begin_stretch + offset)
            score_block = head_scores(query_block, pick_one(key_all, key_slot), head_count)
            new_max = jnp.maximum(row_max, jnp.max(score_block, axis=-1))
            row_total = row_total * jnp.exp(row_max - new_max) + jnp.sum(
                jnp.exp(score_block - new_max[..., None]), axis=-1
            )
            return (new_max, row_total)

        initial = (
            jnp.full((head_count, CH), -1e30, jnp.float32),
            jnp.zeros((head_count, CH), jnp.float32),
        )
        row_max, row_total = lax.fori_loop(0, length, norm_step, initial)
        log_total = row_max + jnp.log(row_total)

        def value_step(offset, summed):
            key_slot = pick_one(stretch_slot, begin_stretch + offset)
            score_block = head_scores(query_block, pick_one(key_all, key_slot), head_count)
            weights = jnp.exp(score_block - log_total[..., None]).astype(jnp.bfloat16)
            value_heads = split_heads(pick_one(value_all, key_slot), head_count)
            return summed + jnp.einsum(
                "hqk,khd->qhd", weights, value_heads, preferred_element_type=jnp.float32
            )

        summed = lax.fori_loop(0, length, value_step, jnp.zeros((CH, head_count, HD), jnp.float32))
        return (summed.reshape(CH, col_count), log_total)

    context, log_totals = lax.map(attend, (query_slots, local_first, local_span))
    context = context.reshape(tok_rows, col_count)
    context_low = context.astype(jnp.bfloat16)
    attn_part = jnp.dot(context_low, w_out, preferred_element_type=jnp.float32)
    hidden = (
        layer_in.astype(jnp.float32)
        + lax.psum(attn_part.astype(jnp.bfloat16), "head").astype(jnp.float32)
        + out_bias
    )
    first_norm, normed_one, inv_one = norm_forward(hidden, norm1_gain, norm1_shift)
    first_low = first_norm.astype(jnp.bfloat16)
    pre_act = jnp.dot(first_low, w_up, preferred_element_type=jnp.float32) + up_bias
    activation, gelu_back = jax.vjp(gelu_exact, pre_act)
    act_low = activation.astype(jnp.bfloat16)
    down_part = jnp.dot(act_low, w_down, preferred_element_type=jnp.float32)
    second_in = (
        first_norm
        + lax.psum(down_part.astype(jnp.bfloat16), "head").astype(jnp.float32)
        + down_bias
    )
    normed_out, normed_two, inv_two = norm_forward(second_in, norm2_gain, norm2_shift)
    grad_second, grad_gain_two, grad_shift_two = norm_backward(
        cotangent.astype(jnp.float32), normed_two, inv_two, norm2_gain
    )
    layer_out = normed_out.astype(jnp.bfloat16)
    second_low = grad_second.astype(jnp.bfloat16)
    grad_down = jnp.einsum("tf,td->fd", act_low, second_low, preferred_element_type=jnp.float32)
    grad_down_bias = jnp.sum(grad_second, axis=0)
    grad_act = jnp.einsum("td,fd->tf", second_low, w_down, preferred_element_type=jnp.float32)
    grad_pre_low = gelu_back(grad_act)[0].astype(jnp.bfloat16)
    grad_up = jnp.einsum("td,tf->df", first_low, grad_pre_low, preferred_element_type=jnp.float32)
    grad_up_bias = jnp.sum(grad_pre_low.astype(jnp.float32), axis=0)
    ffn_back = jnp.einsum("tf,df->td", grad_pre_low, w_up, preferred_element_type=jnp.float32)
    grad_first = lax.psum(ffn_back.astype(jnp.bfloat16), "head").astype(jnp.float32) + grad_second
    grad_hidden, grad_gain_one, grad_shift_one = norm_backward(
        grad_first, normed_one, inv_one, norm1_gain
    )
    grad_out_bias = jnp.sum(grad_hidden, axis=0)
    hidden_low = grad_hidden.astype(jnp.bfloat16)
    grad_out = jnp.einsum("tc,td->cd", context_low, hidden_low, preferred_element_type=jnp.float32)
    grad_context = jnp.einsum(
        "td,cd->tc", hidden_low, w_out, preferred_element_type=jnp.float32
    ).astype(jnp.bfloat16)
    delta_rows = jnp.sum(
        (grad_context.astype(jnp.float32) * context).reshape(tok_rows, head_count, HD), axis=-1
    )
    delta_slots = jnp.swapaxes(delta_rows.reshape(slot_count, CH, head_count), 1, 2)
    grad_slots = grad_context.reshape(slot_count, CH, col_count)

    def back_slot(key_total, inputs):
        query_block, grad_block, log_total, delta_block, begin_stretch, length = inputs

        def key_step(offset, running):
            grad_query, key_sum = running
            key_slot = pick_one(stretch_slot, begin_stretch + offset)
            key_block = pick_one(key_all, key_slot)
            value_block = pick_one(value_all, key_slot)
            weights_low, grad_score = score_grads(
                query_block, key_block, value_block, grad_block, log_total, delta_block, head_count
            )
            grad_query = (
                grad_query
                + jnp.einsum(
                    "hqk,khd->qhd",
                    grad_score,
                    split_heads(key_block, head_count),
                    preferred_element_type=jnp.float32,
                )
                * score_scale
            )
            grad_key = (
                jnp.einsum(
                    "hqk,qhd->khd",
                    grad_score,
                    split_heads(query_block, head_count),
                    preferred_element_type=jnp.float32,
                )
                * score_scale
            )
            grad_value = jnp.einsum(
                "hqk,qhd->khd",
                weights_low,
                split_heads(grad_block, head_count),
                preferred_element_type=jnp.float32,
            )
            update = jnp.concatenate(
                [grad_key.reshape(CH, col_count), grad_value.reshape(CH, col_count)], axis=1
            )
            key_sum = lax.dynamic_update_index_in_dim(
                key_sum, pick_one(key_sum, key_slot) + update, key_slot, 0
            )
            return (grad_query, key_sum)

        start_state = (jnp.zeros((CH, head_count, HD), jnp.float32), key_total)
        grad_query, key_total = lax.fori_loop(0, length, key_step, start_state)
        return (key_total, grad_query.reshape(CH, col_count))

    key_start = jnp.zeros((key_all.shape[0], CH, 2 * col_count), jnp.float32)
    key_total, grad_query_slots = lax.scan(
        back_slot,
        key_start,
        (query_slots, grad_slots, log_totals, delta_slots, local_first, local_span),
    )
    key_grads = lax.psum_scatter(
        key_total.astype(jnp.bfloat16), "batch", scatter_dimension=0, tiled=True
    ).astype(jnp.float32)
    grad_keys = key_grads[:, :, :col_count].astype(jnp.bfloat16)
    grad_values = key_grads[:, :, col_count:].astype(jnp.bfloat16)
    grad_queries = grad_query_slots.reshape(tok_rows, col_count).astype(jnp.bfloat16)
    grad_keys = grad_keys.reshape(tok_rows, col_count)
    grad_values = grad_values.reshape(tok_rows, col_count)
    grad_proj = jnp.concatenate([grad_queries, grad_keys, grad_values], axis=1)
    grad_qkv = jnp.einsum(
        "td,tc->dc", layer_in, grad_proj, preferred_element_type=jnp.float32
    ).reshape(model_width, 3, col_count)
    grad_qv = jnp.stack(
        [
            jnp.sum(grad_queries.astype(jnp.float32), axis=0),
            jnp.sum(grad_values.astype(jnp.float32), axis=0),
        ]
    )
    input_part = jnp.einsum("tc,dc->td", grad_proj, proj_weight, preferred_element_type=jnp.float32)
    own_width = model_width // lax.axis_size("head")
    own_grad = lax.dynamic_slice_in_dim(
        grad_hidden, lax.axis_index("head") * own_width, own_width, 1
    )
    grad_in = (
        lax.psum_scatter(
            input_part.astype(jnp.bfloat16), "head", scatter_dimension=1, tiled=True
        ).astype(jnp.float32)
        + own_grad
    )
    totals = (
        lax.psum(grad_qkv.astype(jnp.bfloat16), "batch").astype(jnp.float32),
        lax.psum(grad_qv.astype(jnp.bfloat16), "batch").astype(jnp.float32),
        lax.psum(grad_out.astype(jnp.bfloat16), "batch").astype(jnp.float32),
        lax.psum(grad_out_bias.astype(jnp.bfloat16), "batch").astype(jnp.float32),
        lax.psum(grad_gain_one.astype(jnp.bfloat16), "batch").astype(jnp.float32),
        lax.psum(grad_shift_one.astype(jnp.bfloat16), "batch").astype(jnp.float32),
        lax.psum(grad_up.astype(jnp.bfloat16), "batch").astype(jnp.float32),
        lax.psum(grad_up_bias.astype(jnp.bfloat16), "batch").astype(jnp.float32),
        lax.psum(grad_down.astype(jnp.bfloat16), "batch").astype(jnp.float32),
        lax.psum(grad_down_bias.astype(jnp.bfloat16), "batch").astype(jnp.float32),
        lax.psum(grad_gain_two.astype(jnp.bfloat16), "batch").astype(jnp.float32),
        lax.psum(grad_shift_two.astype(jnp.bfloat16), "batch").astype(jnp.float32),
    )
    return (
        layer_out,
        grad_in,
        totals[0],
        totals[1],
        totals[2],
        totals[3],
        totals[4],
        totals[5],
        totals[6],
        totals[7],
        totals[8],
        totals[9],
        totals[10],
        totals[11],
    )


MAXCH = 6
LOG2E = 1.4426950408889634
SCORE = HD ** (-0.5)
SWAP = [(0, 1), (1, 0)]
VMEM_LIMIT = 56 * 1024 * 1024


def nt(left, right):
    return lax.dot_general(
        left, right, (((1,), (1,)), ((), ())), preferred_element_type=jnp.float32
    )


def mm(left, right):
    return jnp.dot(left, right, preferred_element_type=jnp.float32)


def low_half(block):
    lane = lax.broadcasted_iota(jnp.int32, block.shape, 1)
    return lane < HD


def unfold(packed):
    wide = packed.astype(jnp.float32)
    return wide, pltpu.roll(wide, HD, 1)


def project_kernel(side_ref, x_ref, wq_ref, wk_ref, wv_ref, bias_ref, kv_ref, far_ref, near_ref):
    order = pl.program_id(1)
    rows = x_ref[...]
    q_all = mm(rows, wq_ref[0]) + bias_ref[0:1, :].astype(jnp.float32)
    k_all = mm(rows, wk_ref[0])
    v_all = mm(rows, wv_ref[0]) + bias_ref[1:2, :].astype(jnp.float32)
    packs = []
    for pair in range(q_all.shape[1] // 128):
        cols = slice(pair * 128, pair * 128 + 128)
        q_pair, k_pair, v_pair = q_all[:, cols], k_all[:, cols], v_all[:, cols]
        low = low_half(q_pair)
        kv_ref[2 * pair] = jnp.where(low, k_pair, pltpu.roll(v_pair, HD, 1)).astype(jnp.bfloat16)
        kv_ref[2 * pair + 1] = jnp.where(low, pltpu.roll(k_pair, HD, 1), v_pair).astype(
            jnp.bfloat16
        )
        top, bottom = q_pair[: CH // 2], q_pair[CH // 2 :]
        low = low[: CH // 2]
        packs.append(jnp.where(low, top, pltpu.roll(bottom, HD, 1)).astype(jnp.bfloat16))
        packs.append(jnp.where(low, pltpu.roll(top, HD, 1), bottom).astype(jnp.bfloat16))

    @pl.when(order == 0)
    def _():
        for head, pack in enumerate(packs):
            far_ref[head] = pack

    @pl.when(order == 1)
    def _():
        for head, pack in enumerate(packs):
            near_ref[head] = pack


def project(side, layer_in, weight, bias):
    width = layer_in.shape[1]
    heads = weight.shape[2] // HD
    step = 4
    groups = heads // step
    cols = step * HD

    def slot_of(order, side_ref):
        return (order + side_ref[0] + 1) % 2

    return pl.pallas_call(
        project_kernel,
        grid_spec=pltpu.PrefetchScalarGridSpec(
            num_scalar_prefetch=1,
            grid=(groups, 2),
            in_specs=[
                pl.BlockSpec((CH, width), lambda g, o, side: (slot_of(o, side), 0)),
                pl.BlockSpec((1, width, cols), lambda g, o, side: (0, 0, g)),
                pl.BlockSpec((1, width, cols), lambda g, o, side: (1, 0, g)),
                pl.BlockSpec((1, width, cols), lambda g, o, side: (2, 0, g)),
                pl.BlockSpec((2, cols), lambda g, o, side: (0, g)),
            ],
            out_specs=[
                pl.BlockSpec((step, CH, 128), lambda g, o, side: (g, slot_of(o, side), 0)),
                pl.BlockSpec((step, CH // 2, 128), lambda g, o, side: (g, 0, 0)),
                pl.BlockSpec((step, CH // 2, 128), lambda g, o, side: (g, 0, 0)),
            ],
        ),
        out_shape=[
            jax.ShapeDtypeStruct((heads, 2 * CH, 128), jnp.bfloat16),
            jax.ShapeDtypeStruct((heads, CH // 2, 128), jnp.bfloat16),
            jax.ShapeDtypeStruct((heads, CH // 2, 128), jnp.bfloat16),
        ],
        compiler_params=pltpu.CompilerParams(vmem_limit_bytes=VMEM_LIMIT),
        cost_estimate=pl.CostEstimate(
            flops=6 * layer_in.size * weight.shape[2],
            bytes_accessed=2 * (layer_in.size + weight.size) + 6 * layer_in.size,
            transcendentals=0,
        ),
        name="project",
    )(side, layer_in, weight, weight, weight, bias)


def fill_tables(slot_ref, seq_ref, stretch_slot, seq_first, seq_length):
    def place(slot, carry):
        stretch_slot[slot_ref[slot]] = slot
        return carry

    lax.fori_loop(0, slot_ref.shape[0], place, 0)

    def one_sequence(seq, start):
        length = seq_ref[seq]

        def one_stretch(offset, carry):
            seq_first[start + offset] = start
            seq_length[start + offset] = length
            return carry

        lax.fori_loop(0, length, one_stretch, 0)
        return start + length

    lax.fori_loop(0, seq_ref.shape[0], one_sequence, jnp.int32(0))


def key_index(slot, core, half):
    own = ((slot >> 1) & 1) == core
    return jnp.where(own, 0, half) + ((slot >> 2) << 1) + (slot & 1)


def load_keys(own_hbm, other_hbm, keys, sem):
    half = own_hbm.shape[0]
    first = pltpu.make_async_copy(own_hbm, keys.at[pl.ds(0, half)], sem.at[0])
    second = pltpu.make_async_copy(other_hbm, keys.at[pl.ds(half, half)], sem.at[1])
    first.start()
    second.start()
    first.wait()
    second.wait()


def my_slot(place_ref, chip):
    return 4 * chip + 2 * place_ref[0] + place_ref[1]


def attend_kernel(
    slot_ref,
    seq_ref,
    place_ref,
    q_ref,
    own_hbm,
    other_hbm,
    ctx_ref,
    ctx_t_ref,
    lse_ref,
    keys,
    values_t,
    held,
    stretch_slot,
    seq_first,
    seq_length,
    sem,
):
    chip = pl.program_id(0)
    half = own_hbm.shape[0]

    @pl.when(chip == 0)
    def _():
        load_keys(own_hbm, other_hbm, keys, sem)
        fill_tables(slot_ref, seq_ref, stretch_slot, seq_first, seq_length)

        def turn(index, carry):
            values_t[index] = keys[index].T[HD:128, :]
            return carry

        lax.fori_loop(0, 2 * half, turn, 0)

    core = place_ref[0]
    stretch = slot_ref[my_slot(place_ref, chip)]
    begin, length = seq_first[stretch], seq_length[stretch]
    part = CH // 2
    low = low_half(q_ref[0])
    queries = [jnp.where(low, q, 0.0).astype(jnp.bfloat16) for q in unfold(q_ref[0])]

    def scores(offset, tops):
        index = key_index(stretch_slot[begin + offset], core, half)
        block = keys[index]
        fresh = []
        for n in range(2):
            score = nt(block, queries[n]) * (SCORE * LOG2E)
            held[offset, :, n * part : (n + 1) * part] = score
            fresh.append(jnp.maximum(tops[n], jnp.max(score.reshape(CH // 8, 8, part), axis=0)))
        return tuple(fresh)

    lowest = jnp.full((8, part), -3e38, jnp.float32)
    tops = lax.fori_loop(0, length, scores, (lowest, lowest))
    tops = [jnp.max(top, axis=0, keepdims=True) for top in tops]

    def step(offset, state):
        index = key_index(stretch_slot[begin + offset], core, half)
        block_t = values_t[index]
        fresh = []
        for n in range(2):
            total, acc = state[n]
            weight = jnp.exp2(held[offset, :, n * part : (n + 1) * part] - tops[n])
            total = total + jnp.sum(weight.reshape(CH // 8, 8, part), axis=0)
            acc = acc + mm(block_t, weight.astype(jnp.bfloat16))
            fresh.append((total, acc))
        return tuple(fresh)

    start = (jnp.zeros((8, part), jnp.float32), jnp.zeros((HD, part), jnp.float32))
    final = lax.fori_loop(0, length, step, (start, start))
    final = [(tops[n], jnp.sum(final[n][0], axis=0, keepdims=True), final[n][1]) for n in range(2)]
    for n in range(2):
        top, total, acc = final[n]
        cols = slice(n * part, (n + 1) * part)
        context_t = acc / total
        ctx_t_ref[0, :, cols] = context_t
        lse_ref[0, :, cols] = top + jnp.log2(total)
        ctx_ref[0, :, n * HD : (n + 1) * HD] = context_t.T.astype(jnp.bfloat16)


def table_scratch(stretches):
    return [pltpu.SMEM((stretches,), jnp.int32) for _ in range(3)] + [
        pltpu.SemaphoreType.DMA((2,))
    ]


def attend(slot_stretch, seq_stretches, place, q_pack, own_keys, other_keys):
    chips = q_pack.shape[0]
    keys = 2 * own_keys.shape[0]
    stretches = slot_stretch.shape[0]
    pairs = chips * 5 * CH * CH
    return pl.pallas_call(
        attend_kernel,
        grid_spec=pltpu.PrefetchScalarGridSpec(
            num_scalar_prefetch=3,
            grid=(chips,),
            in_specs=[
                pl.BlockSpec((1, CH // 2, 128), lambda z, *_: (z, 0, 0)),
                pl.BlockSpec(memory_space=pl.ANY),
                pl.BlockSpec(memory_space=pl.ANY),
            ],
            out_specs=[
                pl.BlockSpec((1, CH // 2, 128), lambda z, *_: (z, 0, 0)),
                pl.BlockSpec((1, HD, CH), lambda z, *_: (z, 0, 0)),
                pl.BlockSpec((1, 1, CH), lambda z, *_: (z, 0, 0)),
            ],
            scratch_shapes=[
                pltpu.VMEM((keys, CH, 128), jnp.bfloat16),
                pltpu.VMEM((keys, HD, CH), jnp.bfloat16),
                pltpu.VMEM((MAXCH, CH, CH), jnp.float32),
            ]
            + table_scratch(stretches),
        ),
        out_shape=[
            jax.ShapeDtypeStruct((chips, CH // 2, 128), jnp.bfloat16),
            jax.ShapeDtypeStruct((chips, HD, CH), jnp.float32),
            jax.ShapeDtypeStruct((chips, 1, CH), jnp.float32),
        ],
        compiler_params=pltpu.CompilerParams(vmem_limit_bytes=24 * 1024 * 1024),
        cost_estimate=pl.CostEstimate(
            flops=HD * pairs, bytes_accessed=16 * q_pack.size, transcendentals=0
        ),
        name="attend",
    )(slot_stretch, seq_stretches, place, q_pack, own_keys, other_keys)


def attend_back_kernel(first, slot_ref, seq_ref, place_ref, *refs):
    q_ref, g_ref, ctx_t_ref, lse_ref, own_hbm, other_hbm = refs[:6]
    if first:
        dq_ref, total_ref = refs[6:8]
    else:
        total_hbm, dq_ref, own_grad_ref, other_grad_ref = refs[6:10]
    keys, keys_t, grads, stretch_slot, seq_first, seq_length, sem = refs[-7:]
    chip = pl.program_id(0)
    half = own_hbm.shape[0]

    @pl.when(chip == 0)
    def _():
        if not first:
            copy = pltpu.make_async_copy(total_hbm, grads, sem.at[2])
            copy.start()
        load_keys(own_hbm, other_hbm, keys, sem)
        fill_tables(slot_ref, seq_ref, stretch_slot, seq_first, seq_length)

        def turn(index, carry):
            keys_t[index] = keys[index].T[0:HD, :]
            if first:
                grads[index] = jnp.zeros((CH, 128), jnp.float32)
            return carry

        lax.fori_loop(0, 2 * half, turn, 0)
        if not first:
            copy.wait()

    core = place_ref[0]
    stretch = slot_ref[my_slot(place_ref, chip)]
    begin, length = seq_first[stretch], seq_length[stretch]
    part = CH // 2
    low = low_half(q_ref[0])
    queries = [jnp.where(low, q, 0.0).astype(jnp.bfloat16) for q in unfold(q_ref[0])]
    wide, rolled = unfold(g_ref[0])
    slopes = [jnp.where(low, 0.0, g) for g in (rolled, wide)]
    delta = [
        jnp.sum(slopes[n].T[HD:128, :] * ctx_t_ref[0, :, n * part : (n + 1) * part], axis=0)[None]
        for n in range(2)
    ]
    slopes = [g.astype(jnp.bfloat16) for g in slopes]
    lse = [lse_ref[0, :, n * part : (n + 1) * part] for n in range(2)]

    def step(offset, state):
        index = key_index(stretch_slot[begin + offset], core, half)
        block = keys[index]
        block_t = keys_t[index]
        fresh = []
        total = None
        for n in range(2):
            score = nt(block, queries[n]) * (SCORE * LOG2E)
            weight = jnp.exp2(score - lse[n])
            slope = weight * (nt(block, slopes[n]) - delta[n])
            slope = slope.astype(jnp.bfloat16)
            weight = weight.astype(jnp.bfloat16)
            fresh.append(state[n] + mm(block_t, slope))
            update = mm(slope, queries[n]) + mm(weight, slopes[n])
            total = update if total is None else total + update
        grads[index] += total
        return tuple(fresh)

    start = tuple(jnp.zeros((HD, part), jnp.float32) for _ in range(2))
    final = lax.fori_loop(0, length, step, start)
    for n in range(2):
        dq_ref[0, :, n * HD : (n + 1) * HD] = (final[n] * SCORE).T.astype(jnp.bfloat16)

    @pl.when(chip == pl.num_programs(0) - 1)
    def _():
        if first:
            copy = pltpu.make_async_copy(grads, total_ref, sem.at[2])
            copy.start()
            copy.wait()
        else:
            scale = jnp.where(low_half(keys[0]), SCORE, 1.0)

            def leave(index, carry):
                own_grad_ref[index] = (grads[index] * scale).astype(jnp.bfloat16)
                other_grad_ref[index] = (grads[half + index] * scale).astype(jnp.bfloat16)
                return carry

            lax.fori_loop(0, half, leave, 0)


def attend_back(tables, place, q_pack, g_pack, ctx_t, lse, own_keys, other_keys, total=None):
    first = total is None
    chips = q_pack.shape[0]
    slots = own_keys.shape[0]
    stretches = tables[0].shape[0]
    pairs = chips * 5 * CH * CH
    pack = pl.BlockSpec((1, CH // 2, 128), lambda z, *_: (z, 0, 0))
    anywhere = pl.BlockSpec(memory_space=pl.ANY)
    in_specs = [
        pack,
        pack,
        pl.BlockSpec((1, HD, CH), lambda z, *_: (z, 0, 0)),
        pl.BlockSpec((1, 1, CH), lambda z, *_: (z, 0, 0)),
        anywhere,
        anywhere,
    ]
    pack_shape = jax.ShapeDtypeStruct((chips, CH // 2, 128), jnp.bfloat16)
    if first:
        out_specs = [pack, anywhere]
        out_shape = [pack_shape, jax.ShapeDtypeStruct((2 * slots, CH, 128), jnp.float32)]
    else:
        in_specs = in_specs + [anywhere]
        whole = pl.BlockSpec((slots, CH, 128), lambda z, *_: (0, 0, 0))
        out_specs = [pack, whole, whole]
        out_shape = [
            pack_shape,
            jax.ShapeDtypeStruct((slots, CH, 128), jnp.bfloat16),
            jax.ShapeDtypeStruct((slots, CH, 128), jnp.bfloat16),
        ]
    operands = (q_pack, g_pack, ctx_t, lse, own_keys, other_keys) + (() if first else (total,))
    return pl.pallas_call(
        functools.partial(attend_back_kernel, first),
        grid_spec=pltpu.PrefetchScalarGridSpec(
            num_scalar_prefetch=3,
            grid=(chips,),
            in_specs=in_specs,
            out_specs=out_specs,
            scratch_shapes=[
                pltpu.VMEM((2 * slots, CH, 128), jnp.bfloat16),
                pltpu.VMEM((2 * slots, HD, CH), jnp.bfloat16),
                pltpu.VMEM((2 * slots, CH, 128), jnp.float32),
            ]
            + table_scratch(stretches)[:3]
            + [pltpu.SemaphoreType.DMA((3,))],
        ),
        out_shape=out_shape,
        compiler_params=pltpu.CompilerParams(vmem_limit_bytes=36 * 1024 * 1024),
        cost_estimate=pl.CostEstimate(
            flops=HD * pairs, bytes_accessed=24 * q_pack.size, transcendentals=0
        ),
        name="attend_back",
    )(*tables, place, *operands)


def swap_across(block, axis_name):
    return lax.ppermute(block, axis_name, SWAP)


def spread(block):
    return lax.all_to_all(block, ("z", "y"), 0, 0, tiled=True)


def gelu_both(pre):
    phi = 0.5 + 0.5 * lax.erf(pre * (2.0**-0.5))
    density = jnp.exp(-0.5 * pre * pre) * ((2.0 * math.pi) ** -0.5)
    return ((pre * phi).astype(jnp.bfloat16), phi + pre * density)


def tn(left, right):
    return lax.dot_general(
        left, right, (((0,), (0,)), ((), ())), preferred_element_type=jnp.float32
    )


BLOCK = 64
TILE = 256


def row_block(step):
    return pl.ds(pl.multiple_of(step * BLOCK, BLOCK), BLOCK)


def weight_slot(part, side):
    return 2 * (part % 2) + (side if part < 2 else 1 - side)


def forward_kernel(side_ref, pack_ref, layer_in, cotangent, vectors_ref, bias_ref, *refs):
    up_hbm, down_hbm, out_hbm = refs[0:4], refs[4:8], refs[8:10]
    out_ref, ctx_ref, first_low, act_ref, slope_ref, second_low, grad_second = refs[10:17]
    normed_one, inv_one, sums_ref = refs[17:20]
    ups, downs, outs, rows_in, cot, acc, first_norm, sem = refs[20:]
    low = jnp.bfloat16
    width = acc.shape[1]
    start = pl.multiple_of(side_ref[0] * CH, CH)
    copies = [
        pltpu.make_async_copy(layer_in.at[pl.ds(start, CH)], rows_in, sem.at[0]),
        pltpu.make_async_copy(out_hbm[0], outs.at[0], sem.at[1]),
        pltpu.make_async_copy(out_hbm[1], outs.at[1], sem.at[2]),
    ]
    copies.append(pltpu.make_async_copy(cotangent.at[pl.ds(start, CH)], cot, sem.at[11]))
    for copy in copies[:3]:
        copy.start()
    for n in range(4):
        slot = weight_slot(n, side_ref[0])
        pltpu.make_async_copy(up_hbm[n], ups.at[slot], sem.at[3 + 2 * slot]).start()
        pltpu.make_async_copy(down_hbm[n], downs.at[slot], sem.at[4 + 2 * slot]).start()
    copies[3].start()
    out_bias, gain_one, shift_one, down_bias, gain_two, shift_two = (
        vectors_ref[n : n + 1, :] for n in range(6)
    )
    heads = pack_ref.shape[0]
    half = CH // 2

    for source in range(2):
        at = slice(source * half, source * half + half)
        for pair in range(heads // 2):
            first, first_roll = unfold(pack_ref[2 * pair, at, :])
            second, second_roll = unfold(pack_ref[2 * pair + 1, at, :])
            lanes = low_half(first)
            base = (source * heads // 2 + pair) * 128
            ctx_ref[0:half, base : base + 128] = jnp.where(lanes, first, second_roll).astype(low)
            ctx_ref[half:CH, base : base + 128] = jnp.where(lanes, first_roll, second).astype(low)
    for copy in copies[:3]:
        copy.wait()
    span = heads * HD
    acc[...] = mm(ctx_ref[:, 0:span], outs[0]) + mm(ctx_ref[:, span : 2 * span], outs[1])

    def first_step(step, carry):
        at = row_block(step)
        hidden = rows_in[at, :].astype(jnp.float32) + acc[at, :] + out_bias
        value, normed, inv = norm_forward(hidden, gain_one, shift_one)
        first_norm[at, :] = value
        normed_one[at, :] = normed
        inv_one[at, :] = jnp.broadcast_to(inv, (BLOCK, 128))
        first_low[at, :] = value.astype(low)
        return carry

    lax.fori_loop(0, CH // BLOCK, first_step, 0)
    acc[...] = jnp.zeros(acc.shape, jnp.float32)

    def forward(n, carry):
        pltpu.make_async_copy(up_hbm[0], ups.at[n], sem.at[3 + 2 * n]).wait()
        base = pl.multiple_of(n * width, width)
        for c in range(0, width, TILE):
            for r in range(0, CH, TILE):
                rows = slice(r, r + TILE)
                pre = mm(first_low[rows, :], ups[n, :, c : c + TILE]) + bias_ref[n, :, c : c + TILE]
                act, slope = gelu_both(pre)
                act_ref[rows, pl.ds(base + c, TILE)] = act
                slope_ref[rows, pl.ds(base + c, TILE)] = slope.astype(low)
        pltpu.make_async_copy(down_hbm[0], downs.at[n], sem.at[4 + 2 * n]).wait()
        acc[...] += mm(act_ref[:, pl.ds(base, width)], downs[n])
        return carry

    lax.fori_loop(0, 4, forward, 0)
    copies[-1].wait()
    zero = jnp.zeros((1, width), jnp.float32)

    def second_step(step, carry):
        at = row_block(step)
        second = first_norm[at, :] + acc[at, :] + down_bias
        value, normed, inv = norm_forward(second, gain_two, shift_two)
        out_ref[at, :] = value.astype(low)
        gradient = cot[at, :].astype(jnp.float32)
        grad, gain_sum, shift_sum = norm_backward(gradient, normed, inv, gain_two)
        grad_second[at, :] = grad
        second_low[at, :] = grad.astype(low)
        return (
            carry[0] + jnp.sum(grad, axis=0, keepdims=True),
            carry[1] + gain_sum[None],
            carry[2] + shift_sum[None],
        )

    sums = lax.fori_loop(0, CH // BLOCK, second_step, (zero, zero, zero))
    for n in range(3):
        sums_ref[n : n + 1, :] = sums[n]


def backward_kernel(side_ref, slope_ref, second_low, grad_second, normed_one, inv_one, gain_ref, *refs):
    up_hbm, down_hbm, out_hbm = refs[0:4], refs[4:8], refs[8:10]
    grad_pre_ref, hidden_ref, hidden_low, gc_own, gc_far, sums_ref, bias_grad_ref = refs[10:17]
    ups, downs, outs, acc, sem = refs[17:]
    low = jnp.bfloat16
    width = acc.shape[1]
    for n in range(4):
        slot = weight_slot(n, side_ref[0])
        pltpu.make_async_copy(down_hbm[n], downs.at[slot], sem.at[2 * slot]).start()
        pltpu.make_async_copy(up_hbm[n], ups.at[slot], sem.at[2 * slot + 1]).start()
    copies = [pltpu.make_async_copy(out_hbm[n], outs.at[n], sem.at[8 + n]) for n in range(2)]
    for copy in copies:
        copy.start()
    heads = gc_own.shape[0]
    half = CH // 2
    acc[...] = jnp.zeros(acc.shape, jnp.float32)

    def backward(n, carry):
        pltpu.make_async_copy(down_hbm[0], downs.at[n], sem.at[2 * n]).wait()
        base = pl.multiple_of(n * width, width)
        for c in range(0, width, TILE):
            total = None
            for r in range(0, CH, TILE):
                rows = slice(r, r + TILE)
                grad_act = nt(second_low[rows, :], downs[n, c : c + TILE, :])
                slope = slope_ref[rows, pl.ds(base + c, TILE)].astype(jnp.float32)
                grad_pre = (grad_act * slope).astype(low)
                grad_pre_ref[rows, pl.ds(base + c, TILE)] = grad_pre
                part = jnp.sum(grad_pre.astype(jnp.float32), axis=0, keepdims=True)
                total = part if total is None else total + part
            bias_grad_ref[n, :, c : c + TILE] = total
        pltpu.make_async_copy(up_hbm[0], ups.at[n], sem.at[2 * n + 1]).wait()
        acc[...] += nt(grad_pre_ref[:, pl.ds(base, width)], ups[n])
        return carry

    lax.fori_loop(0, 4, backward, 0)
    zero = jnp.zeros((1, width), jnp.float32)
    gain_one = gain_ref[...]

    def last_step(step, carry):
        at = row_block(step)
        gradient = acc[at, :] + grad_second[at, :]
        grad, gain_sum, shift_sum = norm_backward(
            gradient, normed_one[at, :], inv_one[at, 0:1], gain_one
        )
        hidden_ref[at, :] = grad
        hidden_low[at, :] = grad.astype(low)
        return (
            carry[0] + jnp.sum(grad, axis=0, keepdims=True),
            carry[1] + gain_sum[None],
            carry[2] + shift_sum[None],
        )

    sums = lax.fori_loop(0, CH // BLOCK, last_step, (zero, zero, zero))
    for n in range(3):
        sums_ref[n : n + 1, :] = sums[n]
    for copy in copies:
        copy.wait()
    for source, pack in enumerate((gc_own, gc_far)):
        for pair in range(heads // 2):
            both = nt(hidden_low[...], outs[source, pair * 128 : pair * 128 + 128, :])
            top, bottom = both[:half], both[half:]
            lanes = low_half(top)
            pack[2 * pair] = jnp.where(lanes, top, pltpu.roll(bottom, HD, 1)).astype(low)
            pack[2 * pair + 1] = jnp.where(lanes, pltpu.roll(top, HD, 1), bottom).astype(low)


def dense_call(kernel, name, in_specs, operands, weights, shapes, scratch, width):
    low = jnp.bfloat16
    vmem, anywhere = pl.BlockSpec(memory_space=pltpu.VMEM), pl.BlockSpec(memory_space=pl.ANY)
    return pl.pallas_call(
        kernel,
        in_specs=in_specs + [anywhere] * 10,
        out_specs=[vmem] * len(shapes),
        out_shape=[jax.ShapeDtypeStruct(shape, dtype) for shape, dtype in shapes],
        scratch_shapes=[
            pltpu.VMEM((4, width, width), low),
            pltpu.VMEM((4, width, width), low),
            pltpu.VMEM((2,) + weights[-1].shape, low),
        ]
        + scratch
        + [pltpu.SemaphoreType.DMA((12,))],
        compiler_params=pltpu.CompilerParams(vmem_limit_bytes=VMEM_LIMIT),
        cost_estimate=pl.CostEstimate(
            flops=8 * CH * width * width, bytes_accessed=8 << 20, transcendentals=0
        ),
        name=name,
    )(*operands, *weights)


def forward_rows(side, pack, layer_in, cotangent, vectors, biases, weights):
    width = layer_in.shape[1]
    units = 4 * width
    low = jnp.bfloat16
    vmem, anywhere = pl.BlockSpec(memory_space=pltpu.VMEM), pl.BlockSpec(memory_space=pl.ANY)
    return dense_call(
        forward_kernel,
        "forward_rows",
        [pl.BlockSpec(memory_space=pltpu.SMEM), vmem, anywhere, anywhere, vmem, vmem],
        (side, pack, layer_in, cotangent, vectors, biases),
        weights,
        [
            ((CH, width), low),
            ((CH, width), low),
            ((CH, width), low),
            ((CH, units), low),
            ((CH, units), low),
            ((CH, width), low),
            ((CH, width), jnp.float32),
            ((CH, width), jnp.float32),
            ((CH, 128), jnp.float32),
            ((3, width), jnp.float32),
        ],
        [
            pltpu.VMEM((CH, width), low),
            pltpu.VMEM((CH, width), low),
            pltpu.VMEM((CH, width), jnp.float32),
            pltpu.VMEM((CH, width), jnp.float32),
        ],
        width,
    )


def backward_rows(side, slopes, second_low, grad_second, normed_one, inv_one, gain, heads, weights):
    width = second_low.shape[1]
    units = 4 * width
    low = jnp.bfloat16
    return dense_call(
        backward_kernel,
        "backward_rows",
        [pl.BlockSpec(memory_space=pltpu.SMEM)] + [pl.BlockSpec(memory_space=pltpu.VMEM)] * 6,
        (side, slopes, second_low, grad_second, normed_one, inv_one, gain),
        weights,
        [
            ((CH, units), low),
            ((CH, width), jnp.float32),
            ((CH, width), low),
            ((heads, CH // 2, 128), low),
            ((heads, CH // 2, 128), low),
            ((3, width), jnp.float32),
            ((4, 1, width), jnp.float32),
        ],
        [pltpu.VMEM((CH, width), jnp.float32)],
        width,
    )


def project_back_kernel(
    side_ref, near_ref, kv_ref, layer_t, w_ref, hidden_ref, *refs
):
    grad_w, far_out, own_out, sums_ref, grad_q, grad_k, grad_v = refs
    low = jnp.bfloat16
    side = side_ref[0]
    half = CH // 2
    heads = kv_ref.shape[0]
    near_row = pl.multiple_of(side * CH, CH)
    far_row = pl.multiple_of((1 - side) * CH, CH)
    for pair in range(heads // 2):
        cols = slice(pair * 128, pair * 128 + 128)
        for pack, base in ((near_ref, near_row), (kv_ref.at[:, 2 * CH :], far_row)):
            first, first_roll = unfold(pack[2 * pair])
            second, second_roll = unfold(pack[2 * pair + 1])
            lanes = low_half(first)
            grad_q[pl.ds(base, half), cols] = jnp.where(lanes, first, second_roll).astype(low)
            grad_q[pl.ds(base + half, half), cols] = jnp.where(lanes, first_roll, second).astype(low)
        for r in range(0, 2 * CH, half):
            rows = slice(r, r + half)
            first, first_roll = unfold(kv_ref[2 * pair, rows, :])
            second, second_roll = unfold(kv_ref[2 * pair + 1, rows, :])
            lanes = low_half(first)
            grad_k[rows, cols] = jnp.where(lanes, first, second_roll).astype(low)
            grad_v[rows, cols] = jnp.where(lanes, first_roll, second).astype(low)
    parts = (grad_q, grad_k, grad_v)
    width = layer_t.shape[0]
    own_width = width // 2
    near_cols = pl.ds(pl.multiple_of(side * own_width, own_width), own_width)
    far_cols = pl.ds(pl.multiple_of((1 - side) * own_width, own_width), own_width)
    far = own = None
    for n, part in enumerate(parts):
        far_term, own_term = nt(part[...], w_ref[n, far_cols, :]), nt(part[...], w_ref[n, near_cols, :])
        far = far_term if far is None else far + far_term
        own = own_term if own is None else own + own_term
    far_out[...] = far.astype(low)
    own_out[...] = own
    near_rows = pl.ds(near_row, CH)
    far_out[near_rows, :] = (far_out[near_rows, :].astype(jnp.float32) + hidden_ref[:, far_cols]).astype(low)
    own_out[near_rows, :] += hidden_ref[:, near_cols]
    count, _, piece, _ = grad_w.shape
    for n, part in enumerate(parts):
        total = mm(layer_t[...], part[...]).astype(low)
        grad_w[:, n] = total.reshape(count, piece, total.shape[1])
    sums_ref[0:1, :] = jnp.sum(grad_q[...].astype(jnp.float32), axis=0, keepdims=True)
    sums_ref[1:2, :] = jnp.sum(grad_v[...].astype(jnp.float32), axis=0, keepdims=True)


def project_back(side, near, kv, layer_t, weight, hidden, pieces):
    heads = kv.shape[0]
    cols = heads * HD
    width, rows = layer_t.shape
    low = jnp.bfloat16
    vmem = pl.BlockSpec(memory_space=pltpu.VMEM)
    return pl.pallas_call(
        project_back_kernel,
        in_specs=[pl.BlockSpec(memory_space=pltpu.SMEM)] + [vmem] * 5,
        out_specs=[vmem] * 4,
        out_shape=[
            jax.ShapeDtypeStruct((pieces, 3, width // pieces, cols), low),
            jax.ShapeDtypeStruct((rows, width // 2), low),
            jax.ShapeDtypeStruct((rows, width // 2), jnp.float32),
            jax.ShapeDtypeStruct((2, cols), jnp.float32),
        ],
        scratch_shapes=[pltpu.VMEM((rows, cols), low)] * 3,
        compiler_params=pltpu.CompilerParams(vmem_limit_bytes=40 * 1024 * 1024),
        cost_estimate=pl.CostEstimate(
            flops=2 * rows * width * cols, bytes_accessed=8 << 20, transcendentals=0
        ),
        name="project_back",
    )(side, near, kv, layer_t, weight, hidden)


def fast_local(
    layer_in,
    slot_stretch,
    seq_stretches,
    w_qkv,
    qv_bias,
    w_out,
    out_bias,
    norm1_gain,
    norm1_shift,
    w_up,
    up_bias,
    w_down,
    down_bias,
    norm2_gain,
    norm2_shift,
    cotangent,
):
    width = layer_in.shape[1]
    cols = w_qkv.shape[2]
    heads = cols // HD
    units = w_up.shape[1]
    half = units // 2
    side = lax.axis_index("head")
    core = lax.axis_index("core")
    far_place = jnp.stack([core, 1 - side]).astype(jnp.int32)
    near_place = jnp.stack([core, side]).astype(jnp.int32)
    side_vec = side.reshape(1).astype(jnp.int32)
    tables = (slot_stretch, seq_stretches)
    low = jnp.bfloat16

    w_three = w_qkv.transpose(1, 0, 2)
    layer_t = layer_in.T
    send_kv, send_far, send_near = project(side_vec, layer_in, w_three, qv_bias)
    send_kv, w_up, w_down, w_out, up_bias = lax.optimization_barrier(
        (send_kv, w_up, w_down, w_out, up_bias)
    )
    own_kv = spread(send_kv)
    low_slices = [
        lax.dynamic_slice_in_dim(array, place * half, half, axis)
        for array, axis in ((w_up, 1), (w_down, 0), (up_bias, 0))
        for place in (core, 1 - core)
    ]
    up_far = swap_across(low_slices[0], "head")
    own_kv, low_slices, w_out, up_far = lax.optimization_barrier(
        (own_kv, low_slices, w_out, up_far)
    )
    other_kv = swap_across(own_kv, "core")
    own_keys = own_kv.reshape(2 * heads, CH, 128)
    other_keys = other_kv.reshape(2 * heads, CH, 128)

    q_far = spread(send_far)
    q_near = spread(send_near)

    downs, biases = (
        (low_slices[n], low_slices[n + 1], swap_across(low_slices[n], "head")) for n in (2, 4)
    )
    ups, down_far = low_slices[:2], downs[2]
    w_out_far = swap_across(w_out, "head")
    ctx_far, ctx_t_far, lse_far = attend(*tables, far_place, q_far, own_keys, other_keys)
    q_near, ctx_far, down_far = lax.optimization_barrier((q_near, ctx_far, down_far))
    ctx_other = swap_across(ctx_far, "head")
    ctx_near, ctx_t_near, lse_near = attend(*tables, near_place, q_near, own_keys, other_keys)

    def row_major(pack):
        block = pack.reshape(heads, CH // 2, 2, HD).transpose(2, 1, 0, 3)
        return block.reshape(CH, cols)

    ctx_near, ctx_other, up_far, down_far, w_out_far, bias_far = lax.optimization_barrier(
        (ctx_near, ctx_other, up_far, down_far, w_out_far, biases[2])
    )
    ctx_pack = spread(jnp.concatenate([ctx_near, ctx_other], axis=1))
    up_parts = [ups[0], ups[1], up_far, swap_across(up_far, "core")]
    down_parts = [downs[0], downs[1], down_far, swap_across(down_far, "core")]
    up_biases = [biases[0], biases[1], bias_far, swap_across(bias_far, "core")]
    vectors = jnp.stack([out_bias, norm1_gain, norm1_shift, down_bias, norm2_gain, norm2_shift])
    vectors = vectors.astype(jnp.float32)
    weights = (*up_parts, *down_parts, w_out, w_out_far)
    is_low = side == 0
    own_biases, far_biases = jnp.stack(up_biases[:2]), jnp.stack(up_biases[2:])
    biases = jnp.stack(
        [jnp.where(is_low, own_biases, far_biases), jnp.where(is_low, far_biases, own_biases)],
        axis=1,
    )
    (
        out_rows,
        ctx_rows,
        first_low,
        acts,
        slopes,
        second_low,
        grad_second,
        normed_one,
        inv_one,
        second_sums,
    ) = forward_rows(
        side_vec,
        ctx_pack,
        layer_in,
        cotangent,
        vectors,
        biases.astype(jnp.float32).reshape(4, 1, half),
        weights,
    )
    is_low = side == 0

    is_first = core == 0
    row = lax.axis_index("y")

    def add_low(kept, got):
        return (kept.astype(jnp.float32) + got.astype(jnp.float32)).astype(low)

    def on_chip(pair):
        return add_low(pair[0], swap_across(pair[1].astype(low), "core"))

    def halves(block, bit):
        size = block.shape[0] // 2
        return (
            lax.dynamic_slice_in_dim(block, bit * size, size, 0),
            lax.dynamic_slice_in_dim(block, (1 - bit) * size, size, 0),
        )

    def partner(block, step):
        if step == "y":
            return swap_across(block, "y")
        hop = 1 if step == "z_near" else 2
        return lax.ppermute(block, "z", [(n, n ^ hop) for n in range(lax.axis_size("z"))])

    place_in_z = lax.axis_index("z")
    bits = {"y": row, "z_near": place_in_z % 2, "z_far": place_in_z // 2}

    def reduce_send(block, step):
        kept, gone = halves(block, bits[step])
        return kept, partner(gone, step)

    def reduce_step(block, step):
        return add_low(*reduce_send(block, step))

    def gather_step(block, step):
        return in_order(bits[step] == 0, block, partner(block, step), 0)

    def scatter_sum(block):
        return lax.psum_scatter(block, ("head", "z", "y"), scatter_dimension=0, tiled=True)

    def collect(block):
        return lax.all_gather(block, ("z", "y"), axis=0, tiled=True)

    def sum_over(vector, steps):
        for step in steps:
            if step in ("core", "head"):
                vector = vector + swap_across(vector, step)
            else:
                vector = vector + partner(vector, step)
        return vector

    def in_order(bit, mine, rest, axis):
        return jnp.concatenate(
            [jnp.where(bit, mine, rest), jnp.where(bit, rest, mine)], axis=axis
        )

    def join(mine, step, axis):
        rest = partner(mine, step)
        mine_far, rest_far = swap_across(mine, "core"), swap_across(rest, "core")
        bit = bits[step] == 0
        own, other = in_order(bit, mine, rest, 0), in_order(bit, mine_far, rest_far, 0)
        return in_order(is_first, own, other, axis).astype(jnp.float32)

    half_rows = cols // 2

    def parts_of(block):
        return [block[:, n * width : (n + 1) * width] for n in range(4)]

    pair = 2 * width

    down_sum = on_chip([tn(acts[:, n : n + pair], second_low) for n in (0, pair)])
    down_sum = down_sum.reshape(2, width, width)
    down_own = lax.dynamic_index_in_dim(down_sum, side, 0, keepdims=False)
    down_far = lax.dynamic_index_in_dim(down_sum, 1 - side, 0, keepdims=False)
    down_far, grad_second = lax.optimization_barrier((down_far, grad_second))
    down_got = swap_across(down_far, "head")
    grad_pres, grad_hidden, hidden_low, gc_own, gc_far, first_sums, bias_grads = backward_rows(
        side_vec, slopes, second_low, grad_second, normed_one, inv_one, vectors[1:2], heads, weights
    )
    gc_in = swap_across(gc_far, "head")
    g_near = spread(gc_own)
    def take(block, start, size):
        return lax.dynamic_slice_in_dim(block, start, size, 1)

    up_own, up_far = (
        on_chip([tn(first_low, take(grad_pres, (n + place) * width, width)) for n in (0, 2)])
        for place in (side, 1 - side)
    )
    out_own, out_far = (
        on_chip(
            [
                tn(take(ctx_rows, base + which * half_rows, half_rows), hidden_low)
                for which in (core, 1 - core)
            ]
        )
        for base in (0, cols)
    )

    def ordered(first, second):
        return jnp.concatenate(
            [jnp.where(is_first, first, second), jnp.where(is_first, second, first)]
        )

    small = jnp.concatenate(
        [
            ordered(bias_grads[0, 0], bias_grads[2, 0]),
            ordered(bias_grads[1, 0], bias_grads[3, 0]),
            first_sums.reshape(-1),
            second_sums.reshape(-1),
        ]
    )
    small = small.reshape(-1, 128)
    small = sum_over(small.reshape(-1, 128), ("core",))
    down_kept, down_sent = halves(add_low(down_own, down_got), bits["y"])
    g_near, gc_in, up_far, out_far, small, down_sent = lax.optimization_barrier(
        (g_near, gc_in, up_far, out_far, small, down_sent)
    )
    up_got, out_got = swap_across(up_far, "head"), swap_across(out_far, "head")
    small_got = swap_across(small, "head")
    down_got = partner(down_sent, "y")
    g_far = spread(gc_in)
    dq_near, part_grad = attend_back(
        tables, near_place, q_near, g_near, ctx_t_near, lse_near, own_keys, other_keys
    )
    part_grad, g_far, down_got, up_got, out_got, small_got = lax.optimization_barrier(
        (part_grad, g_far, down_got, up_got, out_got, small_got)
    )
    both_sum = jnp.concatenate([add_low(up_own, up_got), add_low(out_own, out_got)])
    down_kept, down_sent = halves(add_low(down_kept, down_got), bits["z_near"])
    small = small + small_got
    part_grad, both_sum, small, down_sent = lax.optimization_barrier(
        (part_grad, both_sum, small, down_sent)
    )
    both_sum = lax.psum_scatter(both_sum, ("z", "y"), scatter_dimension=0, tiled=True)
    small_got = partner(small, "z_near")
    down_got = partner(down_sent, "z_near")
    dq_far, own_grad, other_grad = attend_back(
        tables, far_place, q_far, g_far, ctx_t_far, lse_far, own_keys, other_keys, part_grad
    )
    dq_near = spread(dq_near)
    own_grad, other_grad, dq_far, dq_near, small_got, down_got = lax.optimization_barrier(
        (own_grad, other_grad, dq_far, dq_near, small_got, down_got)
    )
    kv_grad = add_low(own_grad, swap_across(other_grad, "core"))
    kv_grad = jnp.concatenate([kv_grad.reshape(heads, 2 * CH, 128), dq_far], axis=1)
    kv_grad, both_sum = lax.optimization_barrier((kv_grad, both_sum))
    kv_grad = spread(kv_grad)
    small = small + small_got
    small_got = partner(small, "y")
    down_sum = reduce_step(add_low(down_kept, down_got), "z_far")
    out_other = swap_across(out_rows, "head")
    kv_grad, small_got, both_sum, down_sum, out_other = lax.optimization_barrier(
        (kv_grad, small_got, both_sum, down_sum, out_other)
    )
    both_sum = collect(both_sum)
    small = small + small_got
    small_got = partner(small, "z_far")
    down_sum = gather_step(down_sum, "z_far")
    deep = lax.axis_size("z")
    grad_w, far_part, own_part, grad_qv = project_back(
        side_vec, dq_near, kv_grad, layer_t, w_three, grad_hidden, 4 * deep
    )
    arrived = swap_across(far_part, "head")
    kept, gone = halves(grad_w, core)
    kept, gone = halves(add_low(kept, swap_across(gone, "core")), row)
    kept = add_low(kept, swap_across(gone, "y"))
    pieces = lax.all_to_all(kept, "z", 0, 0, tiled=True)
    layer_out_pair = jnp.stack([out_rows, out_other])
    layer_out = jnp.where(is_low, layer_out_pair, layer_out_pair[::-1]).reshape(2 * CH, width)
    small = small + small_got
    down_sum = gather_step(down_sum, "z_near")
    grad_qv = sum_over(grad_qv.reshape(-1, 128), ("core", "y"))
    pieces, grad_qv, both_sum, down_sum, arrived = lax.optimization_barrier(
        (pieces, grad_qv, both_sum, down_sum, arrived)
    )
    mine = jnp.sum(pieces.astype(jnp.float32), axis=0).astype(low)
    every = lax.all_to_all(jnp.broadcast_to(mine[None], pieces.shape), "z", 0, 0, tiled=True)
    bit = bits["y"] == 0
    grad_down = join(down_sum, "y", 0)
    both_far = swap_across(both_sum, "core")
    grad_up = in_order(is_first, both_sum[:width], both_far[:width], 1).astype(jnp.float32)
    grad_out = in_order(is_first, both_sum[width:], both_far[width:], 0).astype(jnp.float32)
    grad_qv = sum_over(grad_qv, ("z_near", "z_far")).reshape(2, cols)
    small = small.reshape(-1)
    grad_up_bias = lax.dynamic_slice_in_dim(small, side * units, units)
    vectors = small[2 * units : 2 * units + 6 * width].reshape(6, width)
    every, grad_up, grad_out = lax.optimization_barrier((every, grad_up, grad_out))
    every = in_order(bit, every, swap_across(every, "y"), 0)
    every = in_order(is_first, every, swap_across(every, "core"), 0)
    grad_qkv = every.astype(jnp.float32).transpose(0, 2, 1, 3).reshape(width, 3, cols)
    grad_in = own_part + arrived.astype(jnp.float32)
    return (
        layer_out,
        grad_in,
        grad_qkv,
        grad_qv,
        grad_out,
        vectors[0],
        vectors[1],
        vectors[2],
        grad_up,
        grad_up_bias,
        grad_down,
        vectors[3],
        vectors[4],
        vectors[5],
    )


def solution(mesh):
    batch, head = mesh.shape["batch"], mesh.shape["head"]

    def whole(*arrays):
        tokens, width = arrays[0].shape
        heads = arrays[3].shape[2] // head // HD
        fits = (
            head == 2
            and batch == 2 * heads
            and tokens == batch * 2 * CH
            and arrays[9].shape[1] % (4 * 128) == 0
        )
        if fits:
            split = Mesh(mesh.devices.reshape(batch // 4, 2, 2, head), ("z", "y", "core", "head"))
            return run(fast_local, split, ("z", "y", "core"))(*arrays)
        return run(local, mesh, "batch")(*arrays)

    return whole


def run(body, mesh, rows):
    in_specs = (
        P(rows, None),
        P(),
        P(),
        P(None, None, "head"),
        P(None, "head"),
        P("head", None),
        P(),
        P(),
        P(),
        P(None, "head"),
        P("head"),
        P("head", None),
        P(),
        P(),
        P(),
        P(rows, None),
    )
    out_specs = (
        P(rows, None),
        P(rows, "head"),
        P(None, None, "head"),
        P(None, "head"),
        P("head", None),
        P(),
        P(),
        P(),
        P(None, "head"),
        P("head"),
        P("head", None),
        P(),
        P(),
        P(),
    )
    return jax.shard_map(body, mesh=mesh, in_specs=in_specs, out_specs=out_specs, check_vma=False)
```

```python
import functools
import math

import jax
import jax.numpy as jnp
from jax import lax
from jax.experimental import pallas as pl
from jax.experimental.pallas import tpu as pltpu
from jax.sharding import Mesh
from jax.sharding import PartitionSpec as P

HD = 64
CH = 512

EPSILON = 1e-05


def norm_forward(values, gain_vec, shift_vec):
    centre = jnp.mean(values, axis=-1, keepdims=True)
    centred = values - centre
    spread = jnp.mean(centred * centred, axis=-1, keepdims=True)
    inv_std = lax.rsqrt(spread + EPSILON)
    normed = centred * inv_std
    return (normed * gain_vec + shift_vec, normed, inv_std)


def norm_backward(gradient, normed, inv_std, gain_vec):
    scaled = gradient * gain_vec
    mean_one = jnp.mean(scaled, axis=-1, keepdims=True)
    mean_two = jnp.mean(scaled * normed, axis=-1, keepdims=True)
    back_grad = inv_std * (scaled - mean_one - normed * mean_two)
    return (back_grad, jnp.sum(gradient * normed, axis=0), jnp.sum(gradient, axis=0))


def gelu_exact(values):
    return jax.nn.gelu(values, approximate=False)


def lookup(table_vec, index_vec):
    table_width = table_vec.shape[0]
    is_match = index_vec[:, None] == jnp.arange(table_width, dtype=jnp.int32)[None, :]
    return jnp.sum(jnp.where(is_match, table_vec[None, :], 0), axis=1)


def pick_one(table_vec, position):
    return lax.dynamic_index_in_dim(table_vec, position, 0, keepdims=False)


def split_heads(block, head_count):
    return block.reshape(block.shape[0], head_count, HD)


def head_scores(query_block, key_block, head_count):
    return jnp.einsum(
        "qhd,khd->hqk",
        split_heads(query_block, head_count),
        split_heads(key_block, head_count),
        preferred_element_type=jnp.float32,
    ) * HD ** (-0.5)


def score_grads(
    query_block, key_block, value_block, grad_block, log_total, delta_block, head_count
):
    weights = jnp.exp(head_scores(query_block, key_block, head_count) - log_total[..., None])
    grad_weights = jnp.einsum(
        "qhd,khd->hqk",
        split_heads(grad_block, head_count),
        split_heads(value_block, head_count),
        preferred_element_type=jnp.float32,
    )
    grad_score = (weights * (grad_weights - delta_block[..., None])).astype(jnp.bfloat16)
    return (weights.astype(jnp.bfloat16), grad_score)


def stretch_tables(slot_stretch, seq_stretches):
    stretch_count = slot_stretch.shape[0]
    seq_ends = jnp.cumsum(seq_stretches)
    seq_starts = seq_ends - seq_stretches
    stretch_index = jnp.arange(stretch_count, dtype=jnp.int32)
    seq_of = jnp.sum((stretch_index[:, None] >= seq_ends[None, :]).astype(jnp.int32), axis=1)
    first_stretch = lookup(seq_starts, seq_of)
    stretch_span = lookup(seq_stretches, seq_of)
    is_match = slot_stretch[None, :] == stretch_index[:, None]
    stretch_slot = jnp.sum(jnp.where(is_match, stretch_index[None, :], 0), axis=1)
    return (first_stretch, stretch_span, stretch_slot)


def local(
    layer_in,
    slot_stretch,
    seq_stretches,
    w_qkv,
    qv_bias,
    w_out,
    out_bias,
    norm1_gain,
    norm1_shift,
    w_up,
    up_bias,
    w_down,
    down_bias,
    norm2_gain,
    norm2_shift,
    cotangent,
):
    tok_rows = layer_in.shape[0]
    model_width = layer_in.shape[1]
    slot_count = tok_rows // CH
    col_count = w_qkv.shape[2]
    head_count = col_count // HD
    score_scale = HD ** (-0.5)
    first_stretch, stretch_span, stretch_slot = stretch_tables(slot_stretch, seq_stretches)
    group_index = lax.axis_index("batch")
    local_stretches = lax.dynamic_slice_in_dim(slot_stretch, group_index * slot_count, slot_count)
    local_first = lookup(first_stretch, local_stretches)
    local_span = lookup(stretch_span, local_stretches)
    proj_weight = w_qkv.reshape(model_width, 3 * col_count)
    projected = jnp.dot(layer_in, proj_weight, preferred_element_type=jnp.float32)
    queries = (projected[:, :col_count] + qv_bias[0]).astype(jnp.bfloat16)
    key_rows = projected[:, col_count : 2 * col_count].astype(jnp.bfloat16)
    value_rows = (projected[:, 2 * col_count :] + qv_bias[1]).astype(jnp.bfloat16)
    query_slots = queries.reshape(slot_count, CH, col_count)
    own_keys = key_rows.reshape(slot_count, CH, col_count)
    own_values = value_rows.reshape(slot_count, CH, col_count)
    key_all, value_all = (
        lax.all_gather(own_keys, "batch", axis=0, tiled=True),
        lax.all_gather(own_values, "batch", axis=0, tiled=True),
    )

    def attend(inputs):
        query_block, begin_stretch, length = inputs

        def norm_step(offset, running):
            row_max, row_total = running
            key_slot = pick_one(stretch_slot, begin_stretch + offset)
            score_block = head_scores(query_block, pick_one(key_all, key_slot), head_count)
            new_max = jnp.maximum(row_max, jnp.max(score_block, axis=-1))
            row_total = row_total * jnp.exp(row_max - new_max) + jnp.sum(
                jnp.exp(score_block - new_max[..., None]), axis=-1
            )
            return (new_max, row_total)

        initial = (
            jnp.full((head_count, CH), -1e30, jnp.float32),
            jnp.zeros((head_count, CH), jnp.float32),
        )
        row_max, row_total = lax.fori_loop(0, length, norm_step, initial)
        log_total = row_max + jnp.log(row_total)

        def value_step(offset, summed):
            key_slot = pick_one(stretch_slot, begin_stretch + offset)
            score_block = head_scores(query_block, pick_one(key_all, key_slot), head_count)
            weights = jnp.exp(score_block - log_total[..., None]).astype(jnp.bfloat16)
            value_heads = split_heads(pick_one(value_all, key_slot), head_count)
            return summed + jnp.einsum(
                "hqk,khd->qhd", weights, value_heads, preferred_element_type=jnp.float32
            )

        summed = lax.fori_loop(0, length, value_step, jnp.zeros((CH, head_count, HD), jnp.float32))
        return (summed.reshape(CH, col_count), log_total)

    context, log_totals = lax.map(attend, (query_slots, local_first, local_span))
    context = context.reshape(tok_rows, col_count)
    context_low = context.astype(jnp.bfloat16)
    attn_part = jnp.dot(context_low, w_out, preferred_element_type=jnp.float32)
    hidden = (
        layer_in.astype(jnp.float32)
        + lax.psum(attn_part.astype(jnp.bfloat16), "head").astype(jnp.float32)
        + out_bias
    )
    first_norm, normed_one, inv_one = norm_forward(hidden, norm1_gain, norm1_shift)
    first_low = first_norm.astype(jnp.bfloat16)
    pre_act = jnp.dot(first_low, w_up, preferred_element_type=jnp.float32) + up_bias
    activation, gelu_back = jax.vjp(gelu_exact, pre_act)
    act_low = activation.astype(jnp.bfloat16)
    down_part = jnp.dot(act_low, w_down, preferred_element_type=jnp.float32)
    second_in = (
        first_norm
        + lax.psum(down_part.astype(jnp.bfloat16), "head").astype(jnp.float32)
        + down_bias
    )
    normed_out, normed_two, inv_two = norm_forward(second_in, norm2_gain, norm2_shift)
    grad_second, grad_gain_two, grad_shift_two = norm_backward(
        cotangent.astype(jnp.float32), normed_two, inv_two, norm2_gain
    )
    layer_out = normed_out.astype(jnp.bfloat16)
    second_low = grad_second.astype(jnp.bfloat16)
    grad_down = jnp.einsum("tf,td->fd", act_low, second_low, preferred_element_type=jnp.float32)
    grad_down_bias = jnp.sum(grad_second, axis=0)
    grad_act = jnp.einsum("td,fd->tf", second_low, w_down, preferred_element_type=jnp.float32)
    grad_pre_low = gelu_back(grad_act)[0].astype(jnp.bfloat16)
    grad_up = jnp.einsum("td,tf->df", first_low, grad_pre_low, preferred_element_type=jnp.float32)
    grad_up_bias = jnp.sum(grad_pre_low.astype(jnp.float32), axis=0)
    ffn_back = jnp.einsum("tf,df->td", grad_pre_low, w_up, preferred_element_type=jnp.float32)
    grad_first = lax.psum(ffn_back.astype(jnp.bfloat16), "head").astype(jnp.float32) + grad_second
    grad_hidden, grad_gain_one, grad_shift_one = norm_backward(
        grad_first, normed_one, inv_one, norm1_gain
    )
    grad_out_bias = jnp.sum(grad_hidden, axis=0)
    hidden_low = grad_hidden.astype(jnp.bfloat16)
    grad_out = jnp.einsum("tc,td->cd", context_low, hidden_low, preferred_element_type=jnp.float32)
    grad_context = jnp.einsum(
        "td,cd->tc", hidden_low, w_out, preferred_element_type=jnp.float32
    ).astype(jnp.bfloat16)
    delta_rows = jnp.sum(
        (grad_context.astype(jnp.float32) * context).reshape(tok_rows, head_count, HD), axis=-1
    )
    delta_slots = jnp.swapaxes(delta_rows.reshape(slot_count, CH, head_count), 1, 2)
    grad_slots = grad_context.reshape(slot_count, CH, col_count)

    def back_slot(key_total, inputs):
        query_block, grad_block, log_total, delta_block, begin_stretch, length = inputs

        def key_step(offset, running):
            grad_query, key_sum = running
            key_slot = pick_one(stretch_slot, begin_stretch + offset)
            key_block = pick_one(key_all, key_slot)
            value_block = pick_one(value_all, key_slot)
            weights_low, grad_score = score_grads(
                query_block, key_block, value_block, grad_block, log_total, delta_block, head_count
            )
            grad_query = (
                grad_query
                + jnp.einsum(
                    "hqk,khd->qhd",
                    grad_score,
                    split_heads(key_block, head_count),
                    preferred_element_type=jnp.float32,
                )
                * score_scale
            )
            grad_key = (
                jnp.einsum(
                    "hqk,qhd->khd",
                    grad_score,
                    split_heads(query_block, head_count),
                    preferred_element_type=jnp.float32,
                )
                * score_scale
            )
            grad_value = jnp.einsum(
                "hqk,qhd->khd",
                weights_low,
                split_heads(grad_block, head_count),
                preferred_element_type=jnp.float32,
            )
            update = jnp.concatenate(
                [grad_key.reshape(CH, col_count), grad_value.reshape(CH, col_count)], axis=1
            )
            key_sum = lax.dynamic_update_index_in_dim(
                key_sum, pick_one(key_sum, key_slot) + update, key_slot, 0
            )
            return (grad_query, key_sum)

        start_state = (jnp.zeros((CH, head_count, HD), jnp.float32), key_total)
        grad_query, key_total = lax.fori_loop(0, length, key_step, start_state)
        return (key_total, grad_query.reshape(CH, col_count))

    key_start = jnp.zeros((key_all.shape[0], CH, 2 * col_count), jnp.float32)
    key_total, grad_query_slots = lax.scan(
        back_slot,
        key_start,
        (query_slots, grad_slots, log_totals, delta_slots, local_first, local_span),
    )
    key_grads = lax.psum_scatter(
        key_total.astype(jnp.bfloat16), "batch", scatter_dimension=0, tiled=True
    ).astype(jnp.float32)
    grad_keys = key_grads[:, :, :col_count].astype(jnp.bfloat16)
    grad_values = key_grads[:, :, col_count:].astype(jnp.bfloat16)
    grad_queries = grad_query_slots.reshape(tok_rows, col_count).astype(jnp.bfloat16)
    grad_keys = grad_keys.reshape(tok_rows, col_count)
    grad_values = grad_values.reshape(tok_rows, col_count)
    grad_proj = jnp.concatenate([grad_queries, grad_keys, grad_values], axis=1)
    grad_qkv = jnp.einsum(
        "td,tc->dc", layer_in, grad_proj, preferred_element_type=jnp.float32
    ).reshape(model_width, 3, col_count)
    grad_qv = jnp.stack(
        [
            jnp.sum(grad_queries.astype(jnp.float32), axis=0),
            jnp.sum(grad_values.astype(jnp.float32), axis=0),
        ]
    )
    input_part = jnp.einsum("tc,dc->td", grad_proj, proj_weight, preferred_element_type=jnp.float32)
    own_width = model_width // lax.axis_size("head")
    own_grad = lax.dynamic_slice_in_dim(
        grad_hidden, lax.axis_index("head") * own_width, own_width, 1
    )
    grad_in = (
        lax.psum_scatter(
            input_part.astype(jnp.bfloat16), "head", scatter_dimension=1, tiled=True
        ).astype(jnp.float32)
        + own_grad
    )
    totals = (
        lax.psum(grad_qkv.astype(jnp.bfloat16), "batch").astype(jnp.float32),
        lax.psum(grad_qv.astype(jnp.bfloat16), "batch").astype(jnp.float32),
        lax.psum(grad_out.astype(jnp.bfloat16), "batch").astype(jnp.float32),
        lax.psum(grad_out_bias.astype(jnp.bfloat16), "batch").astype(jnp.float32),
        lax.psum(grad_gain_one.astype(jnp.bfloat16), "batch").astype(jnp.float32),
        lax.psum(grad_shift_one.astype(jnp.bfloat16), "batch").astype(jnp.float32),
        lax.psum(grad_up.astype(jnp.bfloat16), "batch").astype(jnp.float32),
        lax.psum(grad_up_bias.astype(jnp.bfloat16), "batch").astype(jnp.float32),
        lax.psum(grad_down.astype(jnp.bfloat16), "batch").astype(jnp.float32),
        lax.psum(grad_down_bias.astype(jnp.bfloat16), "batch").astype(jnp.float32),
        lax.psum(grad_gain_two.astype(jnp.bfloat16), "batch").astype(jnp.float32),
        lax.psum(grad_shift_two.astype(jnp.bfloat16), "batch").astype(jnp.float32),
    )
    return (
        layer_out,
        grad_in,
        totals[0],
        totals[1],
        totals[2],
        totals[3],
        totals[4],
        totals[5],
        totals[6],
        totals[7],
        totals[8],
        totals[9],
        totals[10],
        totals[11],
    )


MAXCH = 6
LOG2E = 1.4426950408889634
SCORE = HD ** (-0.5)
SWAP = [(0, 1), (1, 0)]
VMEM_LIMIT = 56 * 1024 * 1024


def nt(left, right):
    return lax.dot_general(
        left, right, (((1,), (1,)), ((), ())), preferred_element_type=jnp.float32
    )


def mm(left, right):
    return jnp.dot(left, right, preferred_element_type=jnp.float32)


def low_half(block):
    lane = lax.broadcasted_iota(jnp.int32, block.shape, 1)
    return lane < HD


def unfold(packed):
    wide = packed.astype(jnp.float32)
    return wide, pltpu.roll(wide, HD, 1)


def project_kernel(side_ref, x_ref, wq_ref, wk_ref, wv_ref, bias_ref, kv_ref, far_ref, near_ref):
    order = pl.program_id(1)
    rows = x_ref[...]
    q_all = mm(rows, wq_ref[0]) + bias_ref[0:1, :].astype(jnp.float32)
    k_all = mm(rows, wk_ref[0])
    v_all = mm(rows, wv_ref[0]) + bias_ref[1:2, :].astype(jnp.float32)
    packs = []
    for pair in range(q_all.shape[1] // 128):
        cols = slice(pair * 128, pair * 128 + 128)
        q_pair, k_pair, v_pair = q_all[:, cols], k_all[:, cols], v_all[:, cols]
        low = low_half(q_pair)
        kv_ref[2 * pair] = jnp.where(low, k_pair, pltpu.roll(v_pair, HD, 1)).astype(jnp.bfloat16)
        kv_ref[2 * pair + 1] = jnp.where(low, pltpu.roll(k_pair, HD, 1), v_pair).astype(
            jnp.bfloat16
        )
        top, bottom = q_pair[: CH // 2], q_pair[CH // 2 :]
        low = low[: CH // 2]
        packs.append(jnp.where(low, top, pltpu.roll(bottom, HD, 1)).astype(jnp.bfloat16))
        packs.append(jnp.where(low, pltpu.roll(top, HD, 1), bottom).astype(jnp.bfloat16))

    @pl.when(order == 0)
    def _():
        for head, pack in enumerate(packs):
            far_ref[head] = pack

    @pl.when(order == 1)
    def _():
        for head, pack in enumerate(packs):
            near_ref[head] = pack


def project(side, layer_in, weight, bias):
    width = layer_in.shape[1]
    heads = weight.shape[2] // HD
    step = 4
    groups = heads // step
    cols = step * HD

    def slot_of(order, side_ref):
        return (order + side_ref[0] + 1) % 2

    return pl.pallas_call(
        project_kernel,
        grid_spec=pltpu.PrefetchScalarGridSpec(
            num_scalar_prefetch=1,
            grid=(groups, 2),
            in_specs=[
                pl.BlockSpec((CH, width), lambda g, o, side: (slot_of(o, side), 0)),
                pl.BlockSpec((1, width, cols), lambda g, o, side: (0, 0, g)),
                pl.BlockSpec((1, width, cols), lambda g, o, side: (1, 0, g)),
                pl.BlockSpec((1, width, cols), lambda g, o, side: (2, 0, g)),
                pl.BlockSpec((2, cols), lambda g, o, side: (0, g)),
            ],
            out_specs=[
                pl.BlockSpec((step, CH, 128), lambda g, o, side: (g, slot_of(o, side), 0)),
                pl.BlockSpec((step, CH // 2, 128), lambda g, o, side: (g, 0, 0)),
                pl.BlockSpec((step, CH // 2, 128), lambda g, o, side: (g, 0, 0)),
            ],
        ),
        out_shape=[
            jax.ShapeDtypeStruct((heads, 2 * CH, 128), jnp.bfloat16),
            jax.ShapeDtypeStruct((heads, CH // 2, 128), jnp.bfloat16),
            jax.ShapeDtypeStruct((heads, CH // 2, 128), jnp.bfloat16),
        ],
        compiler_params=pltpu.CompilerParams(vmem_limit_bytes=VMEM_LIMIT),
        cost_estimate=pl.CostEstimate(
            flops=6 * layer_in.size * weight.shape[2],
            bytes_accessed=2 * (layer_in.size + weight.size) + 6 * layer_in.size,
            transcendentals=0,
        ),
        name="project",
    )(side, layer_in, weight, weight, weight, bias)


def fill_tables(slot_ref, seq_ref, stretch_slot, seq_first, seq_length):
    def place(slot, carry):
        stretch_slot[slot_ref[slot]] = slot
        return carry

    lax.fori_loop(0, slot_ref.shape[0], place, 0)

    def one_sequence(seq, start):
        length = seq_ref[seq]

        def one_stretch(offset, carry):
            seq_first[start + offset] = start
            seq_length[start + offset] = length
            return carry

        lax.fori_loop(0, length, one_stretch, 0)
        return start + length

    lax.fori_loop(0, seq_ref.shape[0], one_sequence, jnp.int32(0))


def key_index(slot, core, half):
    own = ((slot >> 1) & 1) == core
    return jnp.where(own, 0, half) + ((slot >> 2) << 1) + (slot & 1)


def load_keys(own_hbm, other_hbm, keys, sem):
    half = own_hbm.shape[0]
    first = pltpu.make_async_copy(own_hbm, keys.at[pl.ds(0, half)], sem.at[0])
    second = pltpu.make_async_copy(other_hbm, keys.at[pl.ds(half, half)], sem.at[1])
    first.start()
    second.start()
    first.wait()
    second.wait()


def my_slot(place_ref, chip):
    return 4 * chip + 2 * place_ref[0] + place_ref[1]


def attend_kernel(
    slot_ref,
    seq_ref,
    place_ref,
    q_ref,
    own_hbm,
    other_hbm,
    ctx_ref,
    ctx_t_ref,
    lse_ref,
    keys,
    values_t,
    held,
    stretch_slot,
    seq_first,
    seq_length,
    sem,
):
    chip = pl.program_id(0)
    half = own_hbm.shape[0]

    @pl.when(chip == 0)
    def _():
        load_keys(own_hbm, other_hbm, keys, sem)
        fill_tables(slot_ref, seq_ref, stretch_slot, seq_first, seq_length)

        def turn(index, carry):
            values_t[index] = keys[index].T[HD:128, :]
            return carry

        lax.fori_loop(0, 2 * half, turn, 0)

    core = place_ref[0]
    stretch = slot_ref[my_slot(place_ref, chip)]
    begin, length = seq_first[stretch], seq_length[stretch]
    part = CH // 2
    low = low_half(q_ref[0])
    queries = [jnp.where(low, q, 0.0).astype(jnp.bfloat16) for q in unfold(q_ref[0])]

    def scores(offset, tops):
        index = key_index(stretch_slot[begin + offset], core, half)
        block = keys[index]
        fresh = []
        for n in range(2):
            score = nt(block, queries[n]) * (SCORE * LOG2E)
            held[offset, :, n * part : (n + 1) * part] = score
            fresh.append(jnp.maximum(tops[n], jnp.max(score.reshape(CH // 8, 8, part), axis=0)))
        return tuple(fresh)

    lowest = jnp.full((8, part), -3e38, jnp.float32)
    tops = lax.fori_loop(0, length, scores, (lowest, lowest))
    tops = [jnp.max(top, axis=0, keepdims=True) for top in tops]

    def step(offset, state):
        index = key_index(stretch_slot[begin + offset], core, half)
        block_t = values_t[index]
        fresh = []
        for n in range(2):
            total, acc = state[n]
            weight = jnp.exp2(held[offset, :, n * part : (n + 1) * part] - tops[n])
            total = total + jnp.sum(weight.reshape(CH // 8, 8, part), axis=0)
            acc = acc + mm(block_t, weight.astype(jnp.bfloat16))
            fresh.append((total, acc))
        return tuple(fresh)

    start = (jnp.zeros((8, part), jnp.float32), jnp.zeros((HD, part), jnp.float32))
    final = lax.fori_loop(0, length, step, (start, start))
    final = [(tops[n], jnp.sum(final[n][0], axis=0, keepdims=True), final[n][1]) for n in range(2)]
    for n in range(2):
        top, total, acc = final[n]
        cols = slice(n * part, (n + 1) * part)
        context_t = acc / total
        ctx_t_ref[0, :, cols] = context_t
        lse_ref[0, :, cols] = top + jnp.log2(total)
        ctx_ref[0, :, n * HD : (n + 1) * HD] = context_t.T.astype(jnp.bfloat16)


def table_scratch(stretches):
    return [pltpu.SMEM((stretches,), jnp.int32) for _ in range(3)] + [
        pltpu.SemaphoreType.DMA((2,))
    ]


def attend(slot_stretch, seq_stretches, place, q_pack, own_keys, other_keys):
    chips = q_pack.shape[0]
    keys = 2 * own_keys.shape[0]
    stretches = slot_stretch.shape[0]
    pairs = chips * 5 * CH * CH
    return pl.pallas_call(
        attend_kernel,
        grid_spec=pltpu.PrefetchScalarGridSpec(
            num_scalar_prefetch=3,
            grid=(chips,),
            in_specs=[
                pl.BlockSpec((1, CH // 2, 128), lambda z, *_: (z, 0, 0)),
                pl.BlockSpec(memory_space=pl.ANY),
                pl.BlockSpec(memory_space=pl.ANY),
            ],
            out_specs=[
                pl.BlockSpec((1, CH // 2, 128), lambda z, *_: (z, 0, 0)),
                pl.BlockSpec((1, HD, CH), lambda z, *_: (z, 0, 0)),
                pl.BlockSpec((1, 1, CH), lambda z, *_: (z, 0, 0)),
            ],
            scratch_shapes=[
                pltpu.VMEM((keys, CH, 128), jnp.bfloat16),
                pltpu.VMEM((keys, HD, CH), jnp.bfloat16),
                pltpu.VMEM((MAXCH, CH, CH), jnp.float32),
            ]
            + table_scratch(stretches),
        ),
        out_shape=[
            jax.ShapeDtypeStruct((chips, CH // 2, 128), jnp.bfloat16),
            jax.ShapeDtypeStruct((chips, HD, CH), jnp.float32),
            jax.ShapeDtypeStruct((chips, 1, CH), jnp.float32),
        ],
        compiler_params=pltpu.CompilerParams(vmem_limit_bytes=24 * 1024 * 1024),
        cost_estimate=pl.CostEstimate(
            flops=HD * pairs, bytes_accessed=16 * q_pack.size, transcendentals=0
        ),
        name="attend",
    )(slot_stretch, seq_stretches, place, q_pack, own_keys, other_keys)


def attend_back_kernel(first, slot_ref, seq_ref, place_ref, *refs):
    q_ref, g_ref, ctx_t_ref, lse_ref, own_hbm, other_hbm = refs[:6]
    if first:
        dq_ref, total_ref = refs[6:8]
    else:
        total_hbm, dq_ref, own_grad_ref, other_grad_ref = refs[6:10]
    keys, keys_t, grads, stretch_slot, seq_first, seq_length, sem = refs[-7:]
    chip = pl.program_id(0)
    half = own_hbm.shape[0]

    @pl.when(chip == 0)
    def _():
        if not first:
            copy = pltpu.make_async_copy(total_hbm, grads, sem.at[2])
            copy.start()
        load_keys(own_hbm, other_hbm, keys, sem)
        fill_tables(slot_ref, seq_ref, stretch_slot, seq_first, seq_length)

        def turn(index, carry):
            keys_t[index] = keys[index].T[0:HD, :]
            if first:
                grads[index] = jnp.zeros((CH, 128), jnp.float32)
            return carry

        lax.fori_loop(0, 2 * half, turn, 0)
        if not first:
            copy.wait()

    core = place_ref[0]
    stretch = slot_ref[my_slot(place_ref, chip)]
    begin, length = seq_first[stretch], seq_length[stretch]
    part = CH // 2
    low = low_half(q_ref[0])
    queries = [jnp.where(low, q, 0.0).astype(jnp.bfloat16) for q in unfold(q_ref[0])]
    wide, rolled = unfold(g_ref[0])
    slopes = [jnp.where(low, 0.0, g) for g in (rolled, wide)]
    delta = [
        jnp.sum(slopes[n].T[HD:128, :] * ctx_t_ref[0, :, n * part : (n + 1) * part], axis=0)[None]
        for n in range(2)
    ]
    slopes = [g.astype(jnp.bfloat16) for g in slopes]
    lse = [lse_ref[0, :, n * part : (n + 1) * part] for n in range(2)]

    def step(offset, state):
        index = key_index(stretch_slot[begin + offset], core, half)
        block = keys[index]
        block_t = keys_t[index]
        fresh = []
        total = None
        for n in range(2):
            score = nt(block, queries[n]) * (SCORE * LOG2E)
            weight = jnp.exp2(score - lse[n])
            slope = weight * (nt(block, slopes[n]) - delta[n])
            slope = slope.astype(jnp.bfloat16)
            weight = weight.astype(jnp.bfloat16)
            fresh.append(state[n] + mm(block_t, slope))
            update = mm(slope, queries[n]) + mm(weight, slopes[n])
            total = update if total is None else total + update
        grads[index] += total
        return tuple(fresh)

    start = tuple(jnp.zeros((HD, part), jnp.float32) for _ in range(2))
    final = lax.fori_loop(0, length, step, start)
    for n in range(2):
        dq_ref[0, :, n * HD : (n + 1) * HD] = (final[n] * SCORE).T.astype(jnp.bfloat16)

    @pl.when(chip == pl.num_programs(0) - 1)
    def _():
        if first:
            copy = pltpu.make_async_copy(grads, total_ref, sem.at[2])
            copy.start()
            copy.wait()
        else:
            scale = jnp.where(low_half(keys[0]), SCORE, 1.0)

            def leave(index, carry):
                own_grad_ref[index] = (grads[index] * scale).astype(jnp.bfloat16)
                other_grad_ref[index] = (grads[half + index] * scale).astype(jnp.bfloat16)
                return carry

            lax.fori_loop(0, half, leave, 0)


def attend_back(tables, place, q_pack, g_pack, ctx_t, lse, own_keys, other_keys, total=None):
    first = total is None
    chips = q_pack.shape[0]
    slots = own_keys.shape[0]
    stretches = tables[0].shape[0]
    pairs = chips * 5 * CH * CH
    pack = pl.BlockSpec((1, CH // 2, 128), lambda z, *_: (z, 0, 0))
    anywhere = pl.BlockSpec(memory_space=pl.ANY)
    in_specs = [
        pack,
        pack,
        pl.BlockSpec((1, HD, CH), lambda z, *_: (z, 0, 0)),
        pl.BlockSpec((1, 1, CH), lambda z, *_: (z, 0, 0)),
        anywhere,
        anywhere,
    ]
    pack_shape = jax.ShapeDtypeStruct((chips, CH // 2, 128), jnp.bfloat16)
    if first:
        out_specs = [pack, anywhere]
        out_shape = [pack_shape, jax.ShapeDtypeStruct((2 * slots, CH, 128), jnp.float32)]
    else:
        in_specs = in_specs + [anywhere]
        whole = pl.BlockSpec((slots, CH, 128), lambda z, *_: (0, 0, 0))
        out_specs = [pack, whole, whole]
        out_shape = [
            pack_shape,
            jax.ShapeDtypeStruct((slots, CH, 128), jnp.bfloat16),
            jax.ShapeDtypeStruct((slots, CH, 128), jnp.bfloat16),
        ]
    operands = (q_pack, g_pack, ctx_t, lse, own_keys, other_keys) + (() if first else (total,))
    return pl.pallas_call(
        functools.partial(attend_back_kernel, first),
        grid_spec=pltpu.PrefetchScalarGridSpec(
            num_scalar_prefetch=3,
            grid=(chips,),
            in_specs=in_specs,
            out_specs=out_specs,
            scratch_shapes=[
                pltpu.VMEM((2 * slots, CH, 128), jnp.bfloat16),
                pltpu.VMEM((2 * slots, HD, CH), jnp.bfloat16),
                pltpu.VMEM((2 * slots, CH, 128), jnp.float32),
            ]
            + table_scratch(stretches)[:3]
            + [pltpu.SemaphoreType.DMA((3,))],
        ),
        out_shape=out_shape,
        compiler_params=pltpu.CompilerParams(vmem_limit_bytes=36 * 1024 * 1024),
        cost_estimate=pl.CostEstimate(
            flops=HD * pairs, bytes_accessed=24 * q_pack.size, transcendentals=0
        ),
        name="attend_back",
    )(*tables, place, *operands)


def swap_across(block, axis_name):
    return lax.ppermute(block, axis_name, SWAP)


def spread(block):
    return lax.all_to_all(block, ("z", "y"), 0, 0, tiled=True)


def gelu_both(pre):
    phi = 0.5 + 0.5 * lax.erf(pre * (2.0**-0.5))
    density = jnp.exp(-0.5 * pre * pre) * ((2.0 * math.pi) ** -0.5)
    return ((pre * phi).astype(jnp.bfloat16), phi + pre * density)


def tn(left, right):
    return lax.dot_general(
        left, right, (((0,), (0,)), ((), ())), preferred_element_type=jnp.float32
    )


BLOCK = 64
TILE = 256


def row_block(step):
    return pl.ds(pl.multiple_of(step * BLOCK, BLOCK), BLOCK)


def weight_slot(part, side):
    return 2 * (part % 2) + (side if part < 2 else 1 - side)


def forward_kernel(side_ref, pack_ref, layer_in, cotangent, vectors_ref, bias_ref, *refs):
    up_hbm, down_hbm, out_hbm = refs[0:4], refs[4:8], refs[8:10]
    out_ref, ctx_ref, first_low, act_ref, slope_ref, second_low, grad_second = refs[10:17]
    normed_one, inv_one, sums_ref = refs[17:20]
    ups, downs, outs, rows_in, cot, acc, first_norm, sem = refs[20:]
    low = jnp.bfloat16
    width = acc.shape[1]
    start = pl.multiple_of(side_ref[0] * CH, CH)
    copies = [
        pltpu.make_async_copy(layer_in.at[pl.ds(start, CH)], rows_in, sem.at[0]),
        pltpu.make_async_copy(out_hbm[0], outs.at[0], sem.at[1]),
        pltpu.make_async_copy(out_hbm[1], outs.at[1], sem.at[2]),
    ]
    copies.append(pltpu.make_async_copy(cotangent.at[pl.ds(start, CH)], cot, sem.at[11]))
    for copy in copies[:3]:
        copy.start()
    for n in range(4):
        slot = weight_slot(n, side_ref[0])
        pltpu.make_async_copy(up_hbm[n], ups.at[slot], sem.at[3 + 2 * slot]).start()
        pltpu.make_async_copy(down_hbm[n], downs.at[slot], sem.at[4 + 2 * slot]).start()
    copies[3].start()
    out_bias, gain_one, shift_one, down_bias, gain_two, shift_two = (
        vectors_ref[n : n + 1, :] for n in range(6)
    )
    heads = pack_ref.shape[0]
    half = CH // 2

    for source in range(2):
        at = slice(source * half, source * half + half)
        for pair in range(heads // 2):
            first, first_roll = unfold(pack_ref[2 * pair, at, :])
            second, second_roll = unfold(pack_ref[2 * pair + 1, at, :])
            lanes = low_half(first)
            base = (source * heads // 2 + pair) * 128
            ctx_ref[0:half, base : base + 128] = jnp.where(lanes, first, second_roll).astype(low)
            ctx_ref[half:CH, base : base + 128] = jnp.where(lanes, first_roll, second).astype(low)
    for copy in copies[:3]:
        copy.wait()
    span = heads * HD
    acc[...] = mm(ctx_ref[:, 0:span], outs[0]) + mm(ctx_ref[:, span : 2 * span], outs[1])

    def first_step(step, carry):
        at = row_block(step)
        hidden = rows_in[at, :].astype(jnp.float32) + acc[at, :] + out_bias
        value, normed, inv = norm_forward(hidden, gain_one, shift_one)
        first_norm[at, :] = value
        normed_one[at, :] = normed
        inv_one[at, :] = jnp.broadcast_to(inv, (BLOCK, 128))
        first_low[at, :] = value.astype(low)
        return carry

    lax.fori_loop(0, CH // BLOCK, first_step, 0)
    acc[...] = jnp.zeros(acc.shape, jnp.float32)

    def forward(n, carry):
        pltpu.make_async_copy(up_hbm[0], ups.at[n], sem.at[3 + 2 * n]).wait()
        base = pl.multiple_of(n * width, width)
        for c in range(0, width, TILE):
            for r in range(0, CH, TILE):
                rows = slice(r, r + TILE)
                pre = mm(first_low[rows, :], ups[n, :, c : c + TILE]) + bias_ref[n, :, c : c + TILE]
                act, slope = gelu_both(pre)
                act_ref[rows, pl.ds(base + c, TILE)] = act
                slope_ref[rows, pl.ds(base + c, TILE)] = slope.astype(low)
        pltpu.make_async_copy(down_hbm[0], downs.at[n], sem.at[4 + 2 * n]).wait()
        acc[...] += mm(act_ref[:, pl.ds(base, width)], downs[n])
        return carry

    lax.fori_loop(0, 4, forward, 0)
    copies[-1].wait()
    zero = jnp.zeros((1, width), jnp.float32)

    def second_step(step, carry):
        at = row_block(step)
        second = first_norm[at, :] + acc[at, :] + down_bias
        value, normed, inv = norm_forward(second, gain_two, shift_two)
        out_ref[at, :] = value.astype(low)
        gradient = cot[at, :].astype(jnp.float32)
        grad, gain_sum, shift_sum = norm_backward(gradient, normed, inv, gain_two)
        grad_second[at, :] = grad
        second_low[at, :] = grad.astype(low)
        return (
            carry[0] + jnp.sum(grad, axis=0, keepdims=True),
            carry[1] + gain_sum[None],
            carry[2] + shift_sum[None],
        )

    sums = lax.fori_loop(0, CH // BLOCK, second_step, (zero, zero, zero))
    for n in range(3):
        sums_ref[n : n + 1, :] = sums[n]


def backward_kernel(
    place_ref, slope_ref, second_low, grad_second, normed_one, inv_one, gain_ref, second_sums, *refs
):
    up_hbm, down_hbm, out_hbm = refs[0:4], refs[4:8], refs[8:10]
    grad_pre_ref, hidden_ref, hidden_low, gc_own, gc_far, sums_ref = refs[10:16]
    ups, downs, outs, acc, sem = refs[16:]
    side, core = place_ref[0], place_ref[1]
    low = jnp.bfloat16
    width = acc.shape[1]
    for n in range(4):
        slot = weight_slot(n, side)
        pltpu.make_async_copy(down_hbm[n], downs.at[slot], sem.at[2 * slot]).start()
        pltpu.make_async_copy(up_hbm[n], ups.at[slot], sem.at[2 * slot + 1]).start()
    copies = [pltpu.make_async_copy(out_hbm[n], outs.at[n], sem.at[8 + n]) for n in range(2)]
    for copy in copies:
        copy.start()
    heads = gc_own.shape[0]
    half = CH // 2
    acc[...] = jnp.zeros(acc.shape, jnp.float32)

    def backward(n, carry):
        pltpu.make_async_copy(down_hbm[0], downs.at[n], sem.at[2 * n]).wait()
        base = pl.multiple_of(n * width, width)
        row = 2 * (n % 2) + jnp.where(n < 2, core, 1 - core)
        for c in range(0, width, TILE):
            total = None
            for r in range(0, CH, TILE):
                rows = slice(r, r + TILE)
                grad_act = nt(second_low[rows, :], downs[n, c : c + TILE, :])
                slope = slope_ref[rows, pl.ds(base + c, TILE)].astype(jnp.float32)
                grad_pre = (grad_act * slope).astype(low)
                grad_pre_ref[rows, pl.ds(base + c, TILE)] = grad_pre
                part = jnp.sum(grad_pre.astype(jnp.float32), axis=0, keepdims=True)
                total = part if total is None else total + part
            sums_ref[pl.ds(row, 1), c : c + TILE] = total
        pltpu.make_async_copy(up_hbm[0], ups.at[n], sem.at[2 * n + 1]).wait()
        acc[...] += nt(grad_pre_ref[:, pl.ds(base, width)], ups[n])
        return carry

    lax.fori_loop(0, 4, backward, 0)
    zero = jnp.zeros((1, width), jnp.float32)
    gain_one = gain_ref[...]

    def last_step(step, carry):
        at = row_block(step)
        gradient = acc[at, :] + grad_second[at, :]
        grad, gain_sum, shift_sum = norm_backward(
            gradient, normed_one[at, :], inv_one[at, 0:1], gain_one
        )
        hidden_ref[at, :] = grad
        hidden_low[at, :] = grad.astype(low)
        return (
            carry[0] + jnp.sum(grad, axis=0, keepdims=True),
            carry[1] + gain_sum[None],
            carry[2] + shift_sum[None],
        )

    sums = lax.fori_loop(0, CH // BLOCK, last_step, (zero, zero, zero))
    for n in range(3):
        sums_ref[4 + n : 5 + n, :] = sums[n]
        sums_ref[7 + n : 8 + n, :] = second_sums[n : n + 1, :]
    sums_ref[10:16, :] = jnp.zeros((6, width), jnp.float32)
    for copy in copies:
        copy.wait()
    for source, pack in enumerate((gc_own, gc_far)):
        for pair in range(heads // 2):
            both = nt(hidden_low[...], outs[source, pair * 128 : pair * 128 + 128, :])
            top, bottom = both[:half], both[half:]
            lanes = low_half(top)
            pack[2 * pair] = jnp.where(lanes, top, pltpu.roll(bottom, HD, 1)).astype(low)
            pack[2 * pair + 1] = jnp.where(lanes, pltpu.roll(top, HD, 1), bottom).astype(low)


def dense_call(kernel, name, in_specs, operands, weights, shapes, scratch, width):
    low = jnp.bfloat16
    vmem, anywhere = pl.BlockSpec(memory_space=pltpu.VMEM), pl.BlockSpec(memory_space=pl.ANY)
    return pl.pallas_call(
        kernel,
        in_specs=in_specs + [anywhere] * 10,
        out_specs=[vmem] * len(shapes),
        out_shape=[jax.ShapeDtypeStruct(shape, dtype) for shape, dtype in shapes],
        scratch_shapes=[
            pltpu.VMEM((4, width, width), low),
            pltpu.VMEM((4, width, width), low),
            pltpu.VMEM((2,) + weights[-1].shape, low),
        ]
        + scratch
        + [pltpu.SemaphoreType.DMA((12,))],
        compiler_params=pltpu.CompilerParams(vmem_limit_bytes=VMEM_LIMIT),
        cost_estimate=pl.CostEstimate(
            flops=8 * CH * width * width, bytes_accessed=8 << 20, transcendentals=0
        ),
        name=name,
    )(*operands, *weights)


def forward_rows(side, pack, layer_in, cotangent, vectors, biases, weights):
    width = layer_in.shape[1]
    units = 4 * width
    low = jnp.bfloat16
    vmem, anywhere = pl.BlockSpec(memory_space=pltpu.VMEM), pl.BlockSpec(memory_space=pl.ANY)
    return dense_call(
        forward_kernel,
        "forward_rows",
        [pl.BlockSpec(memory_space=pltpu.SMEM), vmem, anywhere, anywhere, vmem, vmem],
        (side, pack, layer_in, cotangent, vectors, biases),
        weights,
        [
            ((CH, width), low),
            ((CH, width), low),
            ((CH, width), low),
            ((CH, units), low),
            ((CH, units), low),
            ((CH, width), low),
            ((CH, width), jnp.float32),
            ((CH, width), jnp.float32),
            ((CH, 128), jnp.float32),
            ((3, width), jnp.float32),
        ],
        [
            pltpu.VMEM((CH, width), low),
            pltpu.VMEM((CH, width), low),
            pltpu.VMEM((CH, width), jnp.float32),
            pltpu.VMEM((CH, width), jnp.float32),
        ],
        width,
    )


def backward_rows(
    place, slopes, second_low, grad_second, normed_one, inv_one, gain, second_sums, heads, weights
):
    width = second_low.shape[1]
    units = 4 * width
    low = jnp.bfloat16
    return dense_call(
        backward_kernel,
        "backward_rows",
        [pl.BlockSpec(memory_space=pltpu.SMEM)] + [pl.BlockSpec(memory_space=pltpu.VMEM)] * 7,
        (place, slopes, second_low, grad_second, normed_one, inv_one, gain, second_sums),
        weights,
        [
            ((CH, units), low),
            ((CH, width), jnp.float32),
            ((CH, width), low),
            ((heads, CH // 2, 128), low),
            ((heads, CH // 2, 128), low),
            ((16, width), jnp.float32),
        ],
        [pltpu.VMEM((CH, width), jnp.float32)],
        width,
    )


def project_back_kernel(
    side_ref, near_ref, kv_ref, layer_t, w_ref, hidden_ref, *refs
):
    grad_w, far_out, own_out, sums_ref, grad_q, grad_k, grad_v = refs
    low = jnp.bfloat16
    side = side_ref[0]
    half = CH // 2
    heads = kv_ref.shape[0]
    near_row = pl.multiple_of(side * CH, CH)
    far_row = pl.multiple_of((1 - side) * CH, CH)
    for pair in range(heads // 2):
        cols = slice(pair * 128, pair * 128 + 128)
        for pack, base in ((near_ref, near_row), (kv_ref.at[:, 2 * CH :], far_row)):
            first, first_roll = unfold(pack[2 * pair])
            second, second_roll = unfold(pack[2 * pair + 1])
            lanes = low_half(first)
            grad_q[pl.ds(base, half), cols] = jnp.where(lanes, first, second_roll).astype(low)
            grad_q[pl.ds(base + half, half), cols] = jnp.where(lanes, first_roll, second).astype(low)
        for r in range(0, 2 * CH, half):
            rows = slice(r, r + half)
            first, first_roll = unfold(kv_ref[2 * pair, rows, :])
            second, second_roll = unfold(kv_ref[2 * pair + 1, rows, :])
            lanes = low_half(first)
            grad_k[rows, cols] = jnp.where(lanes, first, second_roll).astype(low)
            grad_v[rows, cols] = jnp.where(lanes, first_roll, second).astype(low)
    parts = (grad_q, grad_k, grad_v)
    width = layer_t.shape[0]
    own_width = width // 2
    near_cols = pl.ds(pl.multiple_of(side * own_width, own_width), own_width)
    far_cols = pl.ds(pl.multiple_of((1 - side) * own_width, own_width), own_width)
    far = own = None
    for n, part in enumerate(parts):
        far_term, own_term = nt(part[...], w_ref[n, far_cols, :]), nt(part[...], w_ref[n, near_cols, :])
        far = far_term if far is None else far + far_term
        own = own_term if own is None else own + own_term
    far_out[...] = far.astype(low)
    own_out[...] = own
    near_rows = pl.ds(near_row, CH)
    far_out[near_rows, :] = (far_out[near_rows, :].astype(jnp.float32) + hidden_ref[:, far_cols]).astype(low)
    own_out[near_rows, :] += hidden_ref[:, near_cols]
    count, _, piece, _ = grad_w.shape
    for n, part in enumerate(parts):
        total = mm(layer_t[...], part[...]).astype(low)
        grad_w[:, n] = total.reshape(count, piece, total.shape[1])
    sums_ref[0:1, :] = jnp.sum(grad_q[...].astype(jnp.float32), axis=0, keepdims=True)
    sums_ref[1:2, :] = jnp.sum(grad_v[...].astype(jnp.float32), axis=0, keepdims=True)


def project_back(side, near, kv, layer_t, weight, hidden, pieces):
    heads = kv.shape[0]
    cols = heads * HD
    width, rows = layer_t.shape
    low = jnp.bfloat16
    vmem = pl.BlockSpec(memory_space=pltpu.VMEM)
    return pl.pallas_call(
        project_back_kernel,
        in_specs=[pl.BlockSpec(memory_space=pltpu.SMEM)] + [vmem] * 5,
        out_specs=[vmem] * 4,
        out_shape=[
            jax.ShapeDtypeStruct((pieces, 3, width // pieces, cols), low),
            jax.ShapeDtypeStruct((rows, width // 2), low),
            jax.ShapeDtypeStruct((rows, width // 2), jnp.float32),
            jax.ShapeDtypeStruct((2, cols), jnp.float32),
        ],
        scratch_shapes=[pltpu.VMEM((rows, cols), low)] * 3,
        compiler_params=pltpu.CompilerParams(vmem_limit_bytes=40 * 1024 * 1024),
        cost_estimate=pl.CostEstimate(
            flops=2 * rows * width * cols, bytes_accessed=8 << 20, transcendentals=0
        ),
        name="project_back",
    )(side, near, kv, layer_t, weight, hidden)


def weight_kernel(kept, place_ref, first_low, grad_pres, ctx_ref, hidden_low, *refs):
    got_ref = refs[0] if kept else None
    out_ref, first_t = refs[-2:]
    far = pl.program_id(0)
    side, core = place_ref[0], place_ref[1]
    width, cols = first_t.shape[0], ctx_ref.shape[1] // 2

    @pl.when(far == 0)
    def _():
        first_t[...] = first_low[...].T

    slot = (0 if kept else 2) + jnp.where(far == 0, side, 1 - side)
    for c in range(0, width, TILE):
        at = pl.ds(pl.multiple_of(slot * width + c, TILE), TILE)
        total = mm(first_t[...], grad_pres[:, at])
        if kept:
            total += got_ref[0, :width, c : c + TILE].astype(jnp.float32)
        out_ref[0, :width, c : c + TILE] = total.astype(jnp.bfloat16)
    part = cols // 2
    start = far * cols + (core if kept else 1 - core) * part
    total = tn(ctx_ref[:, pl.ds(pl.multiple_of(start, part), part)], hidden_low[...])
    if kept:
        total += got_ref[0, width:, :].astype(jnp.float32)
    out_ref[0, width:, :] = total.astype(jnp.bfloat16)


def weight_grads(place, first_low, grad_pres, ctx_rows, hidden_low, got=None):
    kept = got is not None
    rows, width = first_low.shape
    height = width + ctx_rows.shape[1] // 4
    vmem = pl.BlockSpec(memory_space=pltpu.VMEM)
    block = pl.BlockSpec((1, height, width), lambda n: (n, 0, 0))
    return pl.pallas_call(
        functools.partial(weight_kernel, kept),
        grid=(2,),
        in_specs=[pl.BlockSpec(memory_space=pltpu.SMEM)] + [vmem] * 4 + ([block] if kept else []),
        out_specs=block,
        out_shape=jax.ShapeDtypeStruct((2, height, width), jnp.bfloat16),
        scratch_shapes=[pltpu.VMEM((width, rows), jnp.bfloat16)],
        compiler_params=pltpu.CompilerParams(vmem_limit_bytes=40 * 1024 * 1024),
        cost_estimate=pl.CostEstimate(
            flops=4 * rows * width * height, bytes_accessed=12 << 20, transcendentals=0
        ),
        name="weight_grads",
    )(place, first_low, grad_pres, ctx_rows, hidden_low, *((got,) if kept else ()))


def fast_local(
    layer_in,
    slot_stretch,
    seq_stretches,
    w_qkv,
    qv_bias,
    w_out,
    out_bias,
    norm1_gain,
    norm1_shift,
    w_up,
    up_bias,
    w_down,
    down_bias,
    norm2_gain,
    norm2_shift,
    cotangent,
):
    width = layer_in.shape[1]
    cols = w_qkv.shape[2]
    heads = cols // HD
    units = w_up.shape[1]
    half = units // 2
    side = lax.axis_index("head")
    core = lax.axis_index("core")
    far_place = jnp.stack([core, 1 - side]).astype(jnp.int32)
    near_place = jnp.stack([core, side]).astype(jnp.int32)
    side_vec = side.reshape(1).astype(jnp.int32)
    tables = (slot_stretch, seq_stretches)
    low = jnp.bfloat16

    w_three = w_qkv.transpose(1, 0, 2)
    layer_t = layer_in.T
    send_kv, send_far, send_near = project(side_vec, layer_in, w_three, qv_bias)
    send_kv, w_up, w_down, w_out, up_bias = lax.optimization_barrier(
        (send_kv, w_up, w_down, w_out, up_bias)
    )
    own_kv = spread(send_kv)
    low_slices = [
        lax.dynamic_slice_in_dim(array, place * half, half, axis)
        for array, axis in ((w_up, 1), (w_down, 0), (up_bias, 0))
        for place in (core, 1 - core)
    ]
    up_far = swap_across(low_slices[0], "head")
    own_kv, low_slices, w_out, up_far = lax.optimization_barrier(
        (own_kv, low_slices, w_out, up_far)
    )
    other_kv = swap_across(own_kv, "core")
    own_keys = own_kv.reshape(2 * heads, CH, 128)
    other_keys = other_kv.reshape(2 * heads, CH, 128)

    q_far = spread(send_far)
    q_near = spread(send_near)

    downs, biases = (
        (low_slices[n], low_slices[n + 1], swap_across(low_slices[n], "head")) for n in (2, 4)
    )
    ups, down_far = low_slices[:2], downs[2]
    w_out_far = swap_across(w_out, "head")
    ctx_far, ctx_t_far, lse_far = attend(*tables, far_place, q_far, own_keys, other_keys)
    q_near, ctx_far, down_far = lax.optimization_barrier((q_near, ctx_far, down_far))
    ctx_other = swap_across(ctx_far, "head")
    ctx_near, ctx_t_near, lse_near = attend(*tables, near_place, q_near, own_keys, other_keys)

    def row_major(pack):
        block = pack.reshape(heads, CH // 2, 2, HD).transpose(2, 1, 0, 3)
        return block.reshape(CH, cols)

    ctx_near, ctx_other, up_far, down_far, w_out_far, bias_far = lax.optimization_barrier(
        (ctx_near, ctx_other, up_far, down_far, w_out_far, biases[2])
    )
    ctx_pack = spread(jnp.concatenate([ctx_near, ctx_other], axis=1))
    up_parts = [ups[0], ups[1], up_far, swap_across(up_far, "core")]
    down_parts = [downs[0], downs[1], down_far, swap_across(down_far, "core")]
    up_biases = [biases[0], biases[1], bias_far, swap_across(bias_far, "core")]
    vectors = jnp.stack([out_bias, norm1_gain, norm1_shift, down_bias, norm2_gain, norm2_shift])
    vectors = vectors.astype(jnp.float32)
    weights = (*up_parts, *down_parts, w_out, w_out_far)
    is_low = side == 0
    own_biases, far_biases = jnp.stack(up_biases[:2]), jnp.stack(up_biases[2:])
    biases = jnp.stack(
        [jnp.where(is_low, own_biases, far_biases), jnp.where(is_low, far_biases, own_biases)],
        axis=1,
    )
    (
        out_rows,
        ctx_rows,
        first_low,
        acts,
        slopes,
        second_low,
        grad_second,
        normed_one,
        inv_one,
        second_sums,
    ) = forward_rows(
        side_vec,
        ctx_pack,
        layer_in,
        cotangent,
        vectors,
        biases.astype(jnp.float32).reshape(4, 1, half),
        weights,
    )
    is_low = side == 0

    is_first = core == 0
    row = lax.axis_index("y")

    def add_low(kept, got):
        return (kept.astype(jnp.float32) + got.astype(jnp.float32)).astype(low)

    def on_chip(pair):
        return add_low(pair[0], swap_across(pair[1].astype(low), "core"))

    def halves(block, bit):
        size = block.shape[0] // 2
        return (
            lax.dynamic_slice_in_dim(block, bit * size, size, 0),
            lax.dynamic_slice_in_dim(block, (1 - bit) * size, size, 0),
        )

    def partner(block, step):
        if step == "y":
            return swap_across(block, "y")
        hop = 1 if step == "z_near" else 2
        return lax.ppermute(block, "z", [(n, n ^ hop) for n in range(lax.axis_size("z"))])

    place_in_z = lax.axis_index("z")
    bits = {"y": row, "z_near": place_in_z % 2, "z_far": place_in_z // 2}

    def reduce_send(block, step):
        kept, gone = halves(block, bits[step])
        return kept, partner(gone, step)

    def reduce_step(block, step):
        return add_low(*reduce_send(block, step))

    def gather_step(block, step):
        return in_order(bits[step] == 0, block, partner(block, step), 0)

    def scatter_sum(block):
        return lax.psum_scatter(block, ("head", "z", "y"), scatter_dimension=0, tiled=True)

    def collect(block):
        return lax.all_gather(block, ("z", "y"), axis=0, tiled=True)

    def sum_over(vector, steps):
        for step in steps:
            if step in ("core", "head"):
                vector = vector + swap_across(vector, step)
            else:
                vector = vector + partner(vector, step)
        return vector

    def in_order(bit, mine, rest, axis):
        return jnp.concatenate(
            [jnp.where(bit, mine, rest), jnp.where(bit, rest, mine)], axis=axis
        )

    def join(mine, step, axis):
        rest = partner(mine, step)
        mine_far, rest_far = swap_across(mine, "core"), swap_across(rest, "core")
        bit = bits[step] == 0
        own, other = in_order(bit, mine, rest, 0), in_order(bit, mine_far, rest_far, 0)
        return in_order(is_first, own, other, axis).astype(jnp.float32)

    half_rows = cols // 2

    def parts_of(block):
        return [block[:, n * width : (n + 1) * width] for n in range(4)]

    pair = 2 * width

    down_sum = on_chip([tn(acts[:, n : n + pair], second_low) for n in (0, pair)])
    down_sum = down_sum.reshape(2, width, width)
    down_own = lax.dynamic_index_in_dim(down_sum, side, 0, keepdims=False)
    down_far = lax.dynamic_index_in_dim(down_sum, 1 - side, 0, keepdims=False)
    down_far, grad_second = lax.optimization_barrier((down_far, grad_second))
    down_got = swap_across(down_far, "head")
    side_core = jnp.stack([side, core]).astype(jnp.int32)
    grad_pres, grad_hidden, hidden_low, gc_own, gc_far, small = backward_rows(
        side_core,
        slopes,
        second_low,
        grad_second,
        normed_one,
        inv_one,
        vectors[1:2],
        second_sums,
        heads,
        weights,
    )
    gc_in = swap_across(gc_far, "head")
    g_near = spread(gc_own)
    operands = (side_core, first_low, grad_pres, ctx_rows, hidden_low)
    both_sent, down_got = lax.optimization_barrier((weight_grads(*operands), down_got))
    both_got = swap_across(both_sent, "core")
    both_sum = weight_grads(*operands, both_got)
    both_own, both_far = both_sum[0], both_sum[1]

    down_kept, down_sent = halves(add_low(down_own, down_got), bits["y"])
    g_near, gc_in, both_far, down_sent = lax.optimization_barrier(
        (g_near, gc_in, both_far, down_sent)
    )
    both_got = swap_across(both_far, "head")
    small_got = swap_across(small, "core")
    down_got = partner(down_sent, "y")
    g_far = spread(gc_in)
    dq_near, part_grad = attend_back(
        tables, near_place, q_near, g_near, ctx_t_near, lse_near, own_keys, other_keys
    )
    part_grad, g_far, down_got, both_got, small_got = lax.optimization_barrier(
        (part_grad, g_far, down_got, both_got, small_got)
    )
    both_sum = add_low(both_own, both_got)
    down_kept, down_sent = halves(add_low(down_kept, down_got), bits["z_near"])
    small = small + small_got
    part_grad, both_sum, small, down_sent = lax.optimization_barrier(
        (part_grad, both_sum, small, down_sent)
    )
    both_sum = lax.psum_scatter(both_sum, ("z", "y"), scatter_dimension=0, tiled=True)
    small_got = swap_across(small, "head")
    down_got = partner(down_sent, "z_near")
    dq_far, own_grad, other_grad = attend_back(
        tables, far_place, q_far, g_far, ctx_t_far, lse_far, own_keys, other_keys, part_grad
    )
    dq_near = spread(dq_near)
    own_grad, other_grad, dq_far, dq_near, small_got, down_got = lax.optimization_barrier(
        (own_grad, other_grad, dq_far, dq_near, small_got, down_got)
    )
    kv_grad = add_low(own_grad, swap_across(other_grad, "core"))
    kv_grad = jnp.concatenate([kv_grad.reshape(heads, 2 * CH, 128), dq_far], axis=1)
    kv_grad, both_sum = lax.optimization_barrier((kv_grad, both_sum))
    kv_grad = spread(kv_grad)
    small = small + small_got
    small_got = partner(small, "z_near")
    down_sum = reduce_step(add_low(down_kept, down_got), "z_far")
    out_other = swap_across(out_rows, "head")
    kv_grad, small_got, both_sum, down_sum, out_other = lax.optimization_barrier(
        (kv_grad, small_got, both_sum, down_sum, out_other)
    )
    both_sum = collect(both_sum)
    small = small + small_got
    small_got = partner(small, "y")
    down_sum = gather_step(down_sum, "z_far")
    deep = lax.axis_size("z")
    grad_w, far_part, own_part, grad_qv = project_back(
        side_vec, dq_near, kv_grad, layer_t, w_three, grad_hidden, 4 * deep
    )
    arrived = swap_across(far_part, "head")
    kept, gone = halves(grad_w, core)
    kept, gone = halves(add_low(kept, swap_across(gone, "core")), row)
    kept = add_low(kept, swap_across(gone, "y"))
    pieces = lax.all_to_all(kept, "z", 0, 0, tiled=True)
    layer_out_pair = jnp.stack([out_rows, out_other])
    layer_out = jnp.where(is_low, layer_out_pair, layer_out_pair[::-1]).reshape(2 * CH, width)
    small = small + small_got
    down_sum = gather_step(down_sum, "z_near")
    grad_qv = sum_over(grad_qv.reshape(-1, 128), ("core", "y"))
    small_got = partner(small, "z_far")
    pieces, grad_qv, both_sum, down_sum, arrived, small_got = lax.optimization_barrier(
        (pieces, grad_qv, both_sum, down_sum, arrived, small_got)
    )
    small = small + small_got
    mine = jnp.sum(pieces.astype(jnp.float32), axis=0).astype(low)
    every = lax.all_to_all(jnp.broadcast_to(mine[None], pieces.shape), "z", 0, 0, tiled=True)
    bit = bits["y"] == 0
    grad_down = join(down_sum, "y", 0)
    both_far = swap_across(both_sum, "core")
    grad_up = in_order(is_first, both_sum[:width], both_far[:width], 1).astype(jnp.float32)
    grad_out = in_order(is_first, both_sum[width:], both_far[width:], 0).astype(jnp.float32)
    grad_qv = sum_over(grad_qv, ("z_near", "z_far")).reshape(2, cols)
    small = small.reshape(-1)
    grad_up_bias = lax.dynamic_slice_in_dim(small, side * units, units)
    vectors = small[2 * units : 2 * units + 6 * width].reshape(6, width)
    every, grad_up, grad_out = lax.optimization_barrier((every, grad_up, grad_out))
    every = in_order(bit, every, swap_across(every, "y"), 0)
    every = in_order(is_first, every, swap_across(every, "core"), 0)
    grad_qkv = every.astype(jnp.float32).transpose(0, 2, 1, 3).reshape(width, 3, cols)
    grad_in = own_part + arrived.astype(jnp.float32)
    return (
        layer_out,
        grad_in,
        grad_qkv,
        grad_qv,
        grad_out,
        vectors[0],
        vectors[1],
        vectors[2],
        grad_up,
        grad_up_bias,
        grad_down,
        vectors[3],
        vectors[4],
        vectors[5],
    )


def solution(mesh):
    batch, head = mesh.shape["batch"], mesh.shape["head"]

    def whole(*arrays):
        tokens, width = arrays[0].shape
        heads = arrays[3].shape[2] // head // HD
        fits = (
            head == 2
            and batch == 2 * heads
            and tokens == batch * 2 * CH
            and arrays[9].shape[1] % (4 * 128) == 0
        )
        if fits:
            split = Mesh(mesh.devices.reshape(batch // 4, 2, 2, head), ("z", "y", "core", "head"))
            return run(fast_local, split, ("z", "y", "core"))(*arrays)
        return run(local, mesh, "batch")(*arrays)

    return whole


def run(body, mesh, rows):
    in_specs = (
        P(rows, None),
        P(),
        P(),
        P(None, None, "head"),
        P(None, "head"),
        P("head", None),
        P(),
        P(),
        P(),
        P(None, "head"),
        P("head"),
        P("head", None),
        P(),
        P(),
        P(),
        P(rows, None),
    )
    out_specs = (
        P(rows, None),
        P(rows, "head"),
        P(None, None, "head"),
        P(None, "head"),
        P("head", None),
        P(),
        P(),
        P(),
        P(None, "head"),
        P("head"),
        P("head", None),
        P(),
        P(),
        P(),
    )
    return jax.shard_map(body, mesh=mesh, in_specs=in_specs, out_specs=out_specs, check_vma=False)
```

```python
import functools
import math

import jax
import jax.numpy as jnp
from jax import lax
from jax.experimental import pallas as pl
from jax.experimental.pallas import tpu as pltpu
from jax.sharding import Mesh
from jax.sharding import PartitionSpec as P

HD = 64
CH = 512

EPSILON = 1e-05


def norm_forward(values, gain_vec, shift_vec):
    centre = jnp.mean(values, axis=-1, keepdims=True)
    centred = values - centre
    spread = jnp.mean(centred * centred, axis=-1, keepdims=True)
    inv_std = lax.rsqrt(spread + EPSILON)
    normed = centred * inv_std
    return (normed * gain_vec + shift_vec, normed, inv_std)


def norm_backward(gradient, normed, inv_std, gain_vec):
    scaled = gradient * gain_vec
    mean_one = jnp.mean(scaled, axis=-1, keepdims=True)
    mean_two = jnp.mean(scaled * normed, axis=-1, keepdims=True)
    back_grad = inv_std * (scaled - mean_one - normed * mean_two)
    return (back_grad, jnp.sum(gradient * normed, axis=0), jnp.sum(gradient, axis=0))


def gelu_exact(values):
    return jax.nn.gelu(values, approximate=False)


def lookup(table_vec, index_vec):
    table_width = table_vec.shape[0]
    is_match = index_vec[:, None] == jnp.arange(table_width, dtype=jnp.int32)[None, :]
    return jnp.sum(jnp.where(is_match, table_vec[None, :], 0), axis=1)


def pick_one(table_vec, position):
    return lax.dynamic_index_in_dim(table_vec, position, 0, keepdims=False)


def split_heads(block, head_count):
    return block.reshape(block.shape[0], head_count, HD)


def head_scores(query_block, key_block, head_count):
    return jnp.einsum(
        "qhd,khd->hqk",
        split_heads(query_block, head_count),
        split_heads(key_block, head_count),
        preferred_element_type=jnp.float32,
    ) * HD ** (-0.5)


def score_grads(
    query_block, key_block, value_block, grad_block, log_total, delta_block, head_count
):
    weights = jnp.exp(head_scores(query_block, key_block, head_count) - log_total[..., None])
    grad_weights = jnp.einsum(
        "qhd,khd->hqk",
        split_heads(grad_block, head_count),
        split_heads(value_block, head_count),
        preferred_element_type=jnp.float32,
    )
    grad_score = (weights * (grad_weights - delta_block[..., None])).astype(jnp.bfloat16)
    return (weights.astype(jnp.bfloat16), grad_score)


def stretch_tables(slot_stretch, seq_stretches):
    stretch_count = slot_stretch.shape[0]
    seq_ends = jnp.cumsum(seq_stretches)
    seq_starts = seq_ends - seq_stretches
    stretch_index = jnp.arange(stretch_count, dtype=jnp.int32)
    seq_of = jnp.sum((stretch_index[:, None] >= seq_ends[None, :]).astype(jnp.int32), axis=1)
    first_stretch = lookup(seq_starts, seq_of)
    stretch_span = lookup(seq_stretches, seq_of)
    is_match = slot_stretch[None, :] == stretch_index[:, None]
    stretch_slot = jnp.sum(jnp.where(is_match, stretch_index[None, :], 0), axis=1)
    return (first_stretch, stretch_span, stretch_slot)


def local(
    layer_in,
    slot_stretch,
    seq_stretches,
    w_qkv,
    qv_bias,
    w_out,
    out_bias,
    norm1_gain,
    norm1_shift,
    w_up,
    up_bias,
    w_down,
    down_bias,
    norm2_gain,
    norm2_shift,
    cotangent,
):
    tok_rows = layer_in.shape[0]
    model_width = layer_in.shape[1]
    slot_count = tok_rows // CH
    col_count = w_qkv.shape[2]
    head_count = col_count // HD
    score_scale = HD ** (-0.5)
    first_stretch, stretch_span, stretch_slot = stretch_tables(slot_stretch, seq_stretches)
    group_index = lax.axis_index("batch")
    local_stretches = lax.dynamic_slice_in_dim(slot_stretch, group_index * slot_count, slot_count)
    local_first = lookup(first_stretch, local_stretches)
    local_span = lookup(stretch_span, local_stretches)
    proj_weight = w_qkv.reshape(model_width, 3 * col_count)
    projected = jnp.dot(layer_in, proj_weight, preferred_element_type=jnp.float32)
    queries = (projected[:, :col_count] + qv_bias[0]).astype(jnp.bfloat16)
    key_rows = projected[:, col_count : 2 * col_count].astype(jnp.bfloat16)
    value_rows = (projected[:, 2 * col_count :] + qv_bias[1]).astype(jnp.bfloat16)
    query_slots = queries.reshape(slot_count, CH, col_count)
    own_keys = key_rows.reshape(slot_count, CH, col_count)
    own_values = value_rows.reshape(slot_count, CH, col_count)
    key_all, value_all = (
        lax.all_gather(own_keys, "batch", axis=0, tiled=True),
        lax.all_gather(own_values, "batch", axis=0, tiled=True),
    )

    def attend(inputs):
        query_block, begin_stretch, length = inputs

        def norm_step(offset, running):
            row_max, row_total = running
            key_slot = pick_one(stretch_slot, begin_stretch + offset)
            score_block = head_scores(query_block, pick_one(key_all, key_slot), head_count)
            new_max = jnp.maximum(row_max, jnp.max(score_block, axis=-1))
            row_total = row_total * jnp.exp(row_max - new_max) + jnp.sum(
                jnp.exp(score_block - new_max[..., None]), axis=-1
            )
            return (new_max, row_total)

        initial = (
            jnp.full((head_count, CH), -1e30, jnp.float32),
            jnp.zeros((head_count, CH), jnp.float32),
        )
        row_max, row_total = lax.fori_loop(0, length, norm_step, initial)
        log_total = row_max + jnp.log(row_total)

        def value_step(offset, summed):
            key_slot = pick_one(stretch_slot, begin_stretch + offset)
            score_block = head_scores(query_block, pick_one(key_all, key_slot), head_count)
            weights = jnp.exp(score_block - log_total[..., None]).astype(jnp.bfloat16)
            value_heads = split_heads(pick_one(value_all, key_slot), head_count)
            return summed + jnp.einsum(
                "hqk,khd->qhd", weights, value_heads, preferred_element_type=jnp.float32
            )

        summed = lax.fori_loop(0, length, value_step, jnp.zeros((CH, head_count, HD), jnp.float32))
        return (summed.reshape(CH, col_count), log_total)

    context, log_totals = lax.map(attend, (query_slots, local_first, local_span))
    context = context.reshape(tok_rows, col_count)
    context_low = context.astype(jnp.bfloat16)
    attn_part = jnp.dot(context_low, w_out, preferred_element_type=jnp.float32)
    hidden = (
        layer_in.astype(jnp.float32)
        + lax.psum(attn_part.astype(jnp.bfloat16), "head").astype(jnp.float32)
        + out_bias
    )
    first_norm, normed_one, inv_one = norm_forward(hidden, norm1_gain, norm1_shift)
    first_low = first_norm.astype(jnp.bfloat16)
    pre_act = jnp.dot(first_low, w_up, preferred_element_type=jnp.float32) + up_bias
    activation, gelu_back = jax.vjp(gelu_exact, pre_act)
    act_low = activation.astype(jnp.bfloat16)
    down_part = jnp.dot(act_low, w_down, preferred_element_type=jnp.float32)
    second_in = (
        first_norm
        + lax.psum(down_part.astype(jnp.bfloat16), "head").astype(jnp.float32)
        + down_bias
    )
    normed_out, normed_two, inv_two = norm_forward(second_in, norm2_gain, norm2_shift)
    grad_second, grad_gain_two, grad_shift_two = norm_backward(
        cotangent.astype(jnp.float32), normed_two, inv_two, norm2_gain
    )
    layer_out = normed_out.astype(jnp.bfloat16)
    second_low = grad_second.astype(jnp.bfloat16)
    grad_down = jnp.einsum("tf,td->fd", act_low, second_low, preferred_element_type=jnp.float32)
    grad_down_bias = jnp.sum(grad_second, axis=0)
    grad_act = jnp.einsum("td,fd->tf", second_low, w_down, preferred_element_type=jnp.float32)
    grad_pre_low = gelu_back(grad_act)[0].astype(jnp.bfloat16)
    grad_up = jnp.einsum("td,tf->df", first_low, grad_pre_low, preferred_element_type=jnp.float32)
    grad_up_bias = jnp.sum(grad_pre_low.astype(jnp.float32), axis=0)
    ffn_back = jnp.einsum("tf,df->td", grad_pre_low, w_up, preferred_element_type=jnp.float32)
    grad_first = lax.psum(ffn_back.astype(jnp.bfloat16), "head").astype(jnp.float32) + grad_second
    grad_hidden, grad_gain_one, grad_shift_one = norm_backward(
        grad_first, normed_one, inv_one, norm1_gain
    )
    grad_out_bias = jnp.sum(grad_hidden, axis=0)
    hidden_low = grad_hidden.astype(jnp.bfloat16)
    grad_out = jnp.einsum("tc,td->cd", context_low, hidden_low, preferred_element_type=jnp.float32)
    grad_context = jnp.einsum(
        "td,cd->tc", hidden_low, w_out, preferred_element_type=jnp.float32
    ).astype(jnp.bfloat16)
    delta_rows = jnp.sum(
        (grad_context.astype(jnp.float32) * context).reshape(tok_rows, head_count, HD), axis=-1
    )
    delta_slots = jnp.swapaxes(delta_rows.reshape(slot_count, CH, head_count), 1, 2)
    grad_slots = grad_context.reshape(slot_count, CH, col_count)

    def back_slot(key_total, inputs):
        query_block, grad_block, log_total, delta_block, begin_stretch, length = inputs

        def key_step(offset, running):
            grad_query, key_sum = running
            key_slot = pick_one(stretch_slot, begin_stretch + offset)
            key_block = pick_one(key_all, key_slot)
            value_block = pick_one(value_all, key_slot)
            weights_low, grad_score = score_grads(
                query_block, key_block, value_block, grad_block, log_total, delta_block, head_count
            )
            grad_query = (
                grad_query
                + jnp.einsum(
                    "hqk,khd->qhd",
                    grad_score,
                    split_heads(key_block, head_count),
                    preferred_element_type=jnp.float32,
                )
                * score_scale
            )
            grad_key = (
                jnp.einsum(
                    "hqk,qhd->khd",
                    grad_score,
                    split_heads(query_block, head_count),
                    preferred_element_type=jnp.float32,
                )
                * score_scale
            )
            grad_value = jnp.einsum(
                "hqk,qhd->khd",
                weights_low,
                split_heads(grad_block, head_count),
                preferred_element_type=jnp.float32,
            )
            update = jnp.concatenate(
                [grad_key.reshape(CH, col_count), grad_value.reshape(CH, col_count)], axis=1
            )
            key_sum = lax.dynamic_update_index_in_dim(
                key_sum, pick_one(key_sum, key_slot) + update, key_slot, 0
            )
            return (grad_query, key_sum)

        start_state = (jnp.zeros((CH, head_count, HD), jnp.float32), key_total)
        grad_query, key_total = lax.fori_loop(0, length, key_step, start_state)
        return (key_total, grad_query.reshape(CH, col_count))

    key_start = jnp.zeros((key_all.shape[0], CH, 2 * col_count), jnp.float32)
    key_total, grad_query_slots = lax.scan(
        back_slot,
        key_start,
        (query_slots, grad_slots, log_totals, delta_slots, local_first, local_span),
    )
    key_grads = lax.psum_scatter(
        key_total.astype(jnp.bfloat16), "batch", scatter_dimension=0, tiled=True
    ).astype(jnp.float32)
    grad_keys = key_grads[:, :, :col_count].astype(jnp.bfloat16)
    grad_values = key_grads[:, :, col_count:].astype(jnp.bfloat16)
    grad_queries = grad_query_slots.reshape(tok_rows, col_count).astype(jnp.bfloat16)
    grad_keys = grad_keys.reshape(tok_rows, col_count)
    grad_values = grad_values.reshape(tok_rows, col_count)
    grad_proj = jnp.concatenate([grad_queries, grad_keys, grad_values], axis=1)
    grad_qkv = jnp.einsum(
        "td,tc->dc", layer_in, grad_proj, preferred_element_type=jnp.float32
    ).reshape(model_width, 3, col_count)
    grad_qv = jnp.stack(
        [
            jnp.sum(grad_queries.astype(jnp.float32), axis=0),
            jnp.sum(grad_values.astype(jnp.float32), axis=0),
        ]
    )
    input_part = jnp.einsum("tc,dc->td", grad_proj, proj_weight, preferred_element_type=jnp.float32)
    own_width = model_width // lax.axis_size("head")
    own_grad = lax.dynamic_slice_in_dim(
        grad_hidden, lax.axis_index("head") * own_width, own_width, 1
    )
    grad_in = (
        lax.psum_scatter(
            input_part.astype(jnp.bfloat16), "head", scatter_dimension=1, tiled=True
        ).astype(jnp.float32)
        + own_grad
    )
    totals = (
        lax.psum(grad_qkv.astype(jnp.bfloat16), "batch").astype(jnp.float32),
        lax.psum(grad_qv.astype(jnp.bfloat16), "batch").astype(jnp.float32),
        lax.psum(grad_out.astype(jnp.bfloat16), "batch").astype(jnp.float32),
        lax.psum(grad_out_bias.astype(jnp.bfloat16), "batch").astype(jnp.float32),
        lax.psum(grad_gain_one.astype(jnp.bfloat16), "batch").astype(jnp.float32),
        lax.psum(grad_shift_one.astype(jnp.bfloat16), "batch").astype(jnp.float32),
        lax.psum(grad_up.astype(jnp.bfloat16), "batch").astype(jnp.float32),
        lax.psum(grad_up_bias.astype(jnp.bfloat16), "batch").astype(jnp.float32),
        lax.psum(grad_down.astype(jnp.bfloat16), "batch").astype(jnp.float32),
        lax.psum(grad_down_bias.astype(jnp.bfloat16), "batch").astype(jnp.float32),
        lax.psum(grad_gain_two.astype(jnp.bfloat16), "batch").astype(jnp.float32),
        lax.psum(grad_shift_two.astype(jnp.bfloat16), "batch").astype(jnp.float32),
    )
    return (
        layer_out,
        grad_in,
        totals[0],
        totals[1],
        totals[2],
        totals[3],
        totals[4],
        totals[5],
        totals[6],
        totals[7],
        totals[8],
        totals[9],
        totals[10],
        totals[11],
    )


MAXCH = 6
LOG2E = 1.4426950408889634
SCORE = HD ** (-0.5)
SWAP = [(0, 1), (1, 0)]
VMEM_LIMIT = 56 * 1024 * 1024


def nt(left, right):
    return lax.dot_general(
        left, right, (((1,), (1,)), ((), ())), preferred_element_type=jnp.float32
    )


def mm(left, right):
    return jnp.dot(left, right, preferred_element_type=jnp.float32)


def low_half(block):
    lane = lax.broadcasted_iota(jnp.int32, block.shape, 1)
    return lane < HD


def unfold(packed):
    wide = packed.astype(jnp.float32)
    return wide, pltpu.roll(wide, HD, 1)


def project_kernel(side_ref, x_ref, wq_ref, wk_ref, wv_ref, bias_ref, kv_ref, far_ref, near_ref):
    order = pl.program_id(1)
    rows = x_ref[...]
    q_all = mm(rows, wq_ref[0]) + bias_ref[0:1, :].astype(jnp.float32)
    k_all = mm(rows, wk_ref[0])
    v_all = mm(rows, wv_ref[0]) + bias_ref[1:2, :].astype(jnp.float32)
    packs = []
    for pair in range(q_all.shape[1] // 128):
        cols = slice(pair * 128, pair * 128 + 128)
        q_pair, k_pair, v_pair = q_all[:, cols], k_all[:, cols], v_all[:, cols]
        low = low_half(q_pair)
        kv_ref[2 * pair] = jnp.where(low, k_pair, pltpu.roll(v_pair, HD, 1)).astype(jnp.bfloat16)
        kv_ref[2 * pair + 1] = jnp.where(low, pltpu.roll(k_pair, HD, 1), v_pair).astype(
            jnp.bfloat16
        )
        top, bottom = q_pair[: CH // 2], q_pair[CH // 2 :]
        low = low[: CH // 2]
        packs.append(jnp.where(low, top, pltpu.roll(bottom, HD, 1)).astype(jnp.bfloat16))
        packs.append(jnp.where(low, pltpu.roll(top, HD, 1), bottom).astype(jnp.bfloat16))

    @pl.when(order == 0)
    def _():
        for head, pack in enumerate(packs):
            far_ref[head] = pack

    @pl.when(order == 1)
    def _():
        for head, pack in enumerate(packs):
            near_ref[head] = pack


def project(side, layer_in, weight, bias):
    width = layer_in.shape[1]
    heads = weight.shape[2] // HD
    step = 4
    groups = heads // step
    cols = step * HD

    def slot_of(order, side_ref):
        return (order + side_ref[0] + 1) % 2

    return pl.pallas_call(
        project_kernel,
        grid_spec=pltpu.PrefetchScalarGridSpec(
            num_scalar_prefetch=1,
            grid=(groups, 2),
            in_specs=[
                pl.BlockSpec((CH, width), lambda g, o, side: (slot_of(o, side), 0)),
                pl.BlockSpec((1, width, cols), lambda g, o, side: (0, 0, g)),
                pl.BlockSpec((1, width, cols), lambda g, o, side: (1, 0, g)),
                pl.BlockSpec((1, width, cols), lambda g, o, side: (2, 0, g)),
                pl.BlockSpec((2, cols), lambda g, o, side: (0, g)),
            ],
            out_specs=[
                pl.BlockSpec((step, CH, 128), lambda g, o, side: (g, slot_of(o, side), 0)),
                pl.BlockSpec((step, CH // 2, 128), lambda g, o, side: (g, 0, 0)),
                pl.BlockSpec((step, CH // 2, 128), lambda g, o, side: (g, 0, 0)),
            ],
        ),
        out_shape=[
            jax.ShapeDtypeStruct((heads, 2 * CH, 128), jnp.bfloat16),
            jax.ShapeDtypeStruct((heads, CH // 2, 128), jnp.bfloat16),
            jax.ShapeDtypeStruct((heads, CH // 2, 128), jnp.bfloat16),
        ],
        compiler_params=pltpu.CompilerParams(vmem_limit_bytes=VMEM_LIMIT),
        cost_estimate=pl.CostEstimate(
            flops=6 * layer_in.size * weight.shape[2],
            bytes_accessed=2 * (layer_in.size + weight.size) + 6 * layer_in.size,
            transcendentals=0,
        ),
        name="project",
    )(side, layer_in, weight, weight, weight, bias)


def fill_tables(slot_ref, seq_ref, stretch_slot, seq_first, seq_length):
    def place(slot, carry):
        stretch_slot[slot_ref[slot]] = slot
        return carry

    lax.fori_loop(0, slot_ref.shape[0], place, 0)

    def one_sequence(seq, start):
        length = seq_ref[seq]

        def one_stretch(offset, carry):
            seq_first[start + offset] = start
            seq_length[start + offset] = length
            return carry

        lax.fori_loop(0, length, one_stretch, 0)
        return start + length

    lax.fori_loop(0, seq_ref.shape[0], one_sequence, jnp.int32(0))


def key_index(slot, core, half):
    own = ((slot >> 1) & 1) == core
    return jnp.where(own, 0, half) + ((slot >> 2) << 1) + (slot & 1)


def load_keys(own_hbm, other_hbm, keys, sem):
    half = own_hbm.shape[0]
    first = pltpu.make_async_copy(own_hbm, keys.at[pl.ds(0, half)], sem.at[0])
    second = pltpu.make_async_copy(other_hbm, keys.at[pl.ds(half, half)], sem.at[1])
    first.start()
    second.start()
    first.wait()
    second.wait()


def my_slot(place_ref, chip):
    return 4 * chip + 2 * place_ref[0] + place_ref[1]


def attend_kernel(
    slot_ref,
    seq_ref,
    place_ref,
    q_ref,
    own_hbm,
    other_hbm,
    ctx_ref,
    ctx_t_ref,
    lse_ref,
    keys,
    values_t,
    held,
    stretch_slot,
    seq_first,
    seq_length,
    sem,
):
    chip = pl.program_id(0)
    half = own_hbm.shape[0]

    @pl.when(chip == 0)
    def _():
        load_keys(own_hbm, other_hbm, keys, sem)
        fill_tables(slot_ref, seq_ref, stretch_slot, seq_first, seq_length)

        def turn(index, carry):
            values_t[index] = keys[index].T[HD:128, :]
            return carry

        lax.fori_loop(0, 2 * half, turn, 0, unroll=4)

    core = place_ref[0]
    stretch = slot_ref[my_slot(place_ref, chip)]
    begin, length = seq_first[stretch], seq_length[stretch]
    part = CH // 2
    low = low_half(q_ref[0])
    queries = [jnp.where(low, q, 0.0).astype(jnp.bfloat16) for q in unfold(q_ref[0])]

    def scores(offset, tops):
        index = key_index(stretch_slot[begin + offset], core, half)
        block = keys[index]
        fresh = []
        for n in range(2):
            score = nt(block, queries[n]) * (SCORE * LOG2E)
            held[offset, :, n * part : (n + 1) * part] = score
            fresh.append(jnp.maximum(tops[n], jnp.max(score.reshape(CH // 8, 8, part), axis=0)))
        return tuple(fresh)

    lowest = jnp.full((8, part), -3e38, jnp.float32)
    tops = lax.fori_loop(0, length, scores, (lowest, lowest))
    tops = [jnp.max(top, axis=0, keepdims=True) for top in tops]

    def step(offset, state):
        index = key_index(stretch_slot[begin + offset], core, half)
        block_t = values_t[index]
        fresh = []
        for n in range(2):
            total, acc = state[n]
            weight = jnp.exp2(held[offset, :, n * part : (n + 1) * part] - tops[n])
            total = total + jnp.sum(weight.reshape(CH // 8, 8, part), axis=0)
            acc = acc + mm(block_t, weight.astype(jnp.bfloat16))
            fresh.append((total, acc))
        return tuple(fresh)

    start = (jnp.zeros((8, part), jnp.float32), jnp.zeros((HD, part), jnp.float32))
    final = lax.fori_loop(0, length, step, (start, start))
    final = [(tops[n], jnp.sum(final[n][0], axis=0, keepdims=True), final[n][1]) for n in range(2)]
    for n in range(2):
        top, total, acc = final[n]
        cols = slice(n * part, (n + 1) * part)
        context_t = acc / total
        ctx_t_ref[0, :, cols] = context_t
        lse_ref[0, :, cols] = top + jnp.log2(total)
        ctx_ref[0, :, n * HD : (n + 1) * HD] = context_t.T.astype(jnp.bfloat16)


def table_scratch(stretches):
    return [pltpu.SMEM((stretches,), jnp.int32) for _ in range(3)] + [
        pltpu.SemaphoreType.DMA((2,))
    ]


def attend(slot_stretch, seq_stretches, place, q_pack, own_keys, other_keys):
    chips = q_pack.shape[0]
    keys = 2 * own_keys.shape[0]
    stretches = slot_stretch.shape[0]
    pairs = chips * 5 * CH * CH
    return pl.pallas_call(
        attend_kernel,
        grid_spec=pltpu.PrefetchScalarGridSpec(
            num_scalar_prefetch=3,
            grid=(chips,),
            in_specs=[
                pl.BlockSpec((1, CH // 2, 128), lambda z, *_: (z, 0, 0)),
                pl.BlockSpec(memory_space=pl.ANY),
                pl.BlockSpec(memory_space=pl.ANY),
            ],
            out_specs=[
                pl.BlockSpec((1, CH // 2, 128), lambda z, *_: (z, 0, 0)),
                pl.BlockSpec((1, HD, CH), lambda z, *_: (z, 0, 0)),
                pl.BlockSpec((1, 1, CH), lambda z, *_: (z, 0, 0)),
            ],
            scratch_shapes=[
                pltpu.VMEM((keys, CH, 128), jnp.bfloat16),
                pltpu.VMEM((keys, HD, CH), jnp.bfloat16),
                pltpu.VMEM((MAXCH, CH, CH), jnp.float32),
            ]
            + table_scratch(stretches),
        ),
        out_shape=[
            jax.ShapeDtypeStruct((chips, CH // 2, 128), jnp.bfloat16),
            jax.ShapeDtypeStruct((chips, HD, CH), jnp.float32),
            jax.ShapeDtypeStruct((chips, 1, CH), jnp.float32),
        ],
        compiler_params=pltpu.CompilerParams(vmem_limit_bytes=24 * 1024 * 1024),
        cost_estimate=pl.CostEstimate(
            flops=HD * pairs, bytes_accessed=16 * q_pack.size, transcendentals=0
        ),
        name="attend",
    )(slot_stretch, seq_stretches, place, q_pack, own_keys, other_keys)


def attend_back_kernel(first, slot_ref, seq_ref, place_ref, *refs):
    q_ref, g_ref, ctx_t_ref, lse_ref, own_hbm, other_hbm = refs[:6]
    if first:
        dq_ref, total_ref = refs[6:8]
    else:
        total_hbm, dq_ref, own_grad_ref, other_grad_ref = refs[6:10]
    keys, keys_t, grads, stretch_slot, seq_first, seq_length, sem = refs[-7:]
    chip = pl.program_id(0)
    half = own_hbm.shape[0]

    @pl.when(chip == 0)
    def _():
        if not first:
            copy = pltpu.make_async_copy(total_hbm, grads, sem.at[2])
            copy.start()
        load_keys(own_hbm, other_hbm, keys, sem)
        fill_tables(slot_ref, seq_ref, stretch_slot, seq_first, seq_length)

        def turn(index, carry):
            keys_t[index] = keys[index].T[0:HD, :]
            if first:
                grads[index] = jnp.zeros((CH, 128), jnp.float32)
            return carry

        lax.fori_loop(0, 2 * half, turn, 0)
        if not first:
            copy.wait()

    core = place_ref[0]
    stretch = slot_ref[my_slot(place_ref, chip)]
    begin, length = seq_first[stretch], seq_length[stretch]
    part = CH // 2
    low = low_half(q_ref[0])
    queries = [jnp.where(low, q, 0.0).astype(jnp.bfloat16) for q in unfold(q_ref[0])]
    wide, rolled = unfold(g_ref[0])
    slopes = [jnp.where(low, 0.0, g) for g in (rolled, wide)]
    delta = [
        jnp.sum(slopes[n].T[HD:128, :] * ctx_t_ref[0, :, n * part : (n + 1) * part], axis=0)[None]
        for n in range(2)
    ]
    slopes = [g.astype(jnp.bfloat16) for g in slopes]
    lse = [lse_ref[0, :, n * part : (n + 1) * part] for n in range(2)]

    def step(offset, state):
        index = key_index(stretch_slot[begin + offset], core, half)
        block = keys[index]
        block_t = keys_t[index]
        fresh = []
        total = None
        for n in range(2):
            score = nt(block, queries[n]) * (SCORE * LOG2E)
            weight = jnp.exp2(score - lse[n])
            slope = weight * (nt(block, slopes[n]) - delta[n])
            slope = slope.astype(jnp.bfloat16)
            weight = weight.astype(jnp.bfloat16)
            fresh.append(state[n] + mm(block_t, slope))
            update = mm(slope, queries[n]) + mm(weight, slopes[n])
            total = update if total is None else total + update
        grads[index] += total
        return tuple(fresh)

    start = tuple(jnp.zeros((HD, part), jnp.float32) for _ in range(2))
    final = lax.fori_loop(0, length, step, start)
    for n in range(2):
        dq_ref[0, :, n * HD : (n + 1) * HD] = (final[n] * SCORE).T.astype(jnp.bfloat16)

    @pl.when(chip == pl.num_programs(0) - 1)
    def _():
        if first:
            copy = pltpu.make_async_copy(grads, total_ref, sem.at[2])
            copy.start()
            copy.wait()
        else:
            scale = jnp.where(low_half(keys[0]), SCORE, 1.0)

            def leave(index, carry):
                own_grad_ref[index] = (grads[index] * scale).astype(jnp.bfloat16)
                other_grad_ref[index] = (grads[half + index] * scale).astype(jnp.bfloat16)
                return carry

            lax.fori_loop(0, half, leave, 0)


def attend_back(tables, place, q_pack, g_pack, ctx_t, lse, own_keys, other_keys, total=None):
    first = total is None
    chips = q_pack.shape[0]
    slots = own_keys.shape[0]
    stretches = tables[0].shape[0]
    pairs = chips * 5 * CH * CH
    pack = pl.BlockSpec((1, CH // 2, 128), lambda z, *_: (z, 0, 0))
    anywhere = pl.BlockSpec(memory_space=pl.ANY)
    in_specs = [
        pack,
        pack,
        pl.BlockSpec((1, HD, CH), lambda z, *_: (z, 0, 0)),
        pl.BlockSpec((1, 1, CH), lambda z, *_: (z, 0, 0)),
        anywhere,
        anywhere,
    ]
    pack_shape = jax.ShapeDtypeStruct((chips, CH // 2, 128), jnp.bfloat16)
    if first:
        out_specs = [pack, anywhere]
        out_shape = [pack_shape, jax.ShapeDtypeStruct((2 * slots, CH, 128), jnp.float32)]
    else:
        in_specs = in_specs + [anywhere]
        whole = pl.BlockSpec((slots, CH, 128), lambda z, *_: (0, 0, 0))
        out_specs = [pack, whole, whole]
        out_shape = [
            pack_shape,
            jax.ShapeDtypeStruct((slots, CH, 128), jnp.bfloat16),
            jax.ShapeDtypeStruct((slots, CH, 128), jnp.bfloat16),
        ]
    operands = (q_pack, g_pack, ctx_t, lse, own_keys, other_keys) + (() if first else (total,))
    return pl.pallas_call(
        functools.partial(attend_back_kernel, first),
        grid_spec=pltpu.PrefetchScalarGridSpec(
            num_scalar_prefetch=3,
            grid=(chips,),
            in_specs=in_specs,
            out_specs=out_specs,
            scratch_shapes=[
                pltpu.VMEM((2 * slots, CH, 128), jnp.bfloat16),
                pltpu.VMEM((2 * slots, HD, CH), jnp.bfloat16),
                pltpu.VMEM((2 * slots, CH, 128), jnp.float32),
            ]
            + table_scratch(stretches)[:3]
            + [pltpu.SemaphoreType.DMA((3,))],
        ),
        out_shape=out_shape,
        compiler_params=pltpu.CompilerParams(vmem_limit_bytes=36 * 1024 * 1024),
        cost_estimate=pl.CostEstimate(
            flops=HD * pairs, bytes_accessed=24 * q_pack.size, transcendentals=0
        ),
        name="attend_back",
    )(*tables, place, *operands)


def swap_across(block, axis_name):
    return lax.ppermute(block, axis_name, SWAP)


def spread(block):
    return lax.all_to_all(block, ("z", "y"), 0, 0, tiled=True)


def gelu_both(pre):
    phi = 0.5 + 0.5 * lax.erf(pre * (2.0**-0.5))
    density = jnp.exp(-0.5 * pre * pre) * ((2.0 * math.pi) ** -0.5)
    return ((pre * phi).astype(jnp.bfloat16), phi + pre * density)


def tn(left, right):
    return lax.dot_general(
        left, right, (((0,), (0,)), ((), ())), preferred_element_type=jnp.float32
    )


BLOCK = 64
TILE = 256


def row_block(step):
    return pl.ds(pl.multiple_of(step * BLOCK, BLOCK), BLOCK)


def weight_slot(part, side):
    return 2 * (part % 2) + (side if part < 2 else 1 - side)


def forward_kernel(side_ref, pack_ref, layer_in, cotangent, vectors_ref, bias_ref, *refs):
    up_hbm, down_hbm, out_hbm = refs[0:4], refs[4:8], refs[8:10]
    out_ref, ctx_ref, first_low, act_ref, slope_ref, second_low, grad_second = refs[10:17]
    normed_one, inv_one, sums_ref = refs[17:20]
    ups, downs, outs, rows_in, cot, acc, first_norm, sem = refs[20:]
    low = jnp.bfloat16
    width = acc.shape[1]
    start = pl.multiple_of(side_ref[0] * CH, CH)
    copies = [
        pltpu.make_async_copy(layer_in.at[pl.ds(start, CH)], rows_in, sem.at[0]),
        pltpu.make_async_copy(out_hbm[0], outs.at[0], sem.at[1]),
        pltpu.make_async_copy(out_hbm[1], outs.at[1], sem.at[2]),
    ]
    copies.append(pltpu.make_async_copy(cotangent.at[pl.ds(start, CH)], cot, sem.at[11]))
    for copy in copies[:3]:
        copy.start()
    for n in range(4):
        slot = weight_slot(n, side_ref[0])
        pltpu.make_async_copy(up_hbm[n], ups.at[slot], sem.at[3 + 2 * slot]).start()
        pltpu.make_async_copy(down_hbm[n], downs.at[slot], sem.at[4 + 2 * slot]).start()
    copies[3].start()
    out_bias, gain_one, shift_one, down_bias, gain_two, shift_two = (
        vectors_ref[n : n + 1, :] for n in range(6)
    )
    heads = pack_ref.shape[0]
    half = CH // 2

    for source in range(2):
        at = slice(source * half, source * half + half)
        for pair in range(heads // 2):
            first, first_roll = unfold(pack_ref[2 * pair, at, :])
            second, second_roll = unfold(pack_ref[2 * pair + 1, at, :])
            lanes = low_half(first)
            base = (source * heads // 2 + pair) * 128
            ctx_ref[0:half, base : base + 128] = jnp.where(lanes, first, second_roll).astype(low)
            ctx_ref[half:CH, base : base + 128] = jnp.where(lanes, first_roll, second).astype(low)
    for copy in copies[:3]:
        copy.wait()
    span = heads * HD
    acc[...] = mm(ctx_ref[:, 0:span], outs[0]) + mm(ctx_ref[:, span : 2 * span], outs[1])

    def first_step(step, carry):
        at = row_block(step)
        hidden = rows_in[at, :].astype(jnp.float32) + acc[at, :] + out_bias
        value, normed, inv = norm_forward(hidden, gain_one, shift_one)
        first_norm[at, :] = value
        normed_one[at, :] = normed
        inv_one[at, :] = jnp.broadcast_to(inv, (BLOCK, 128))
        first_low[at, :] = value.astype(low)
        return carry

    lax.fori_loop(0, CH // BLOCK, first_step, 0)
    acc[...] = jnp.zeros(acc.shape, jnp.float32)

    def forward(n, carry):
        pltpu.make_async_copy(up_hbm[0], ups.at[n], sem.at[3 + 2 * n]).wait()
        base = pl.multiple_of(n * width, width)
        for c in range(0, width, TILE):
            for r in range(0, CH, TILE):
                rows = slice(r, r + TILE)
                pre = mm(first_low[rows, :], ups[n, :, c : c + TILE]) + bias_ref[n, :, c : c + TILE]
                act, slope = gelu_both(pre)
                act_ref[rows, pl.ds(base + c, TILE)] = act
                slope_ref[rows, pl.ds(base + c, TILE)] = slope.astype(low)
        pltpu.make_async_copy(down_hbm[0], downs.at[n], sem.at[4 + 2 * n]).wait()
        acc[...] += mm(act_ref[:, pl.ds(base, width)], downs[n])
        return carry

    lax.fori_loop(0, 4, forward, 0)
    copies[-1].wait()
    zero = jnp.zeros((1, width), jnp.float32)

    def second_step(step, carry):
        at = row_block(step)
        second = first_norm[at, :] + acc[at, :] + down_bias
        value, normed, inv = norm_forward(second, gain_two, shift_two)
        out_ref[at, :] = value.astype(low)
        gradient = cot[at, :].astype(jnp.float32)
        grad, gain_sum, shift_sum = norm_backward(gradient, normed, inv, gain_two)
        grad_second[at, :] = grad
        second_low[at, :] = grad.astype(low)
        return (
            carry[0] + jnp.sum(grad, axis=0, keepdims=True),
            carry[1] + gain_sum[None],
            carry[2] + shift_sum[None],
        )

    sums = lax.fori_loop(0, CH // BLOCK, second_step, (zero, zero, zero))
    for n in range(3):
        sums_ref[n : n + 1, :] = sums[n]


def backward_kernel(
    place_ref, slope_ref, second_low, grad_second, normed_one, inv_one, gain_ref, second_sums, *refs
):
    up_hbm, down_hbm, out_hbm = refs[0:4], refs[4:8], refs[8:10]
    grad_pre_ref, hidden_ref, hidden_low, gc_own, gc_far, sums_ref = refs[10:16]
    ups, downs, outs, acc, sem = refs[16:]
    side, core = place_ref[0], place_ref[1]
    low = jnp.bfloat16
    width = acc.shape[1]
    for n in range(4):
        slot = weight_slot(n, side)
        pltpu.make_async_copy(down_hbm[n], downs.at[slot], sem.at[2 * slot]).start()
        pltpu.make_async_copy(up_hbm[n], ups.at[slot], sem.at[2 * slot + 1]).start()
    copies = [pltpu.make_async_copy(out_hbm[n], outs.at[n], sem.at[8 + n]) for n in range(2)]
    for copy in copies:
        copy.start()
    heads = gc_own.shape[0]
    half = CH // 2
    acc[...] = jnp.zeros(acc.shape, jnp.float32)

    def backward(n, carry):
        pltpu.make_async_copy(down_hbm[0], downs.at[n], sem.at[2 * n]).wait()
        base = pl.multiple_of(n * width, width)
        row = 2 * (n % 2) + jnp.where(n < 2, core, 1 - core)
        for c in range(0, width, TILE):
            total = None
            for r in range(0, CH, TILE):
                rows = slice(r, r + TILE)
                grad_act = nt(second_low[rows, :], downs[n, c : c + TILE, :])
                slope = slope_ref[rows, pl.ds(base + c, TILE)].astype(jnp.float32)
                grad_pre = (grad_act * slope).astype(low)
                grad_pre_ref[rows, pl.ds(base + c, TILE)] = grad_pre
                part = jnp.sum(grad_pre.astype(jnp.float32), axis=0, keepdims=True)
                total = part if total is None else total + part
            sums_ref[pl.ds(row, 1), c : c + TILE] = total
        pltpu.make_async_copy(up_hbm[0], ups.at[n], sem.at[2 * n + 1]).wait()
        acc[...] += nt(grad_pre_ref[:, pl.ds(base, width)], ups[n])
        return carry

    lax.fori_loop(0, 4, backward, 0)
    zero = jnp.zeros((1, width), jnp.float32)
    gain_one = gain_ref[...]

    def last_step(step, carry):
        at = row_block(step)
        gradient = acc[at, :] + grad_second[at, :]
        grad, gain_sum, shift_sum = norm_backward(
            gradient, normed_one[at, :], inv_one[at, 0:1], gain_one
        )
        hidden_ref[at, :] = grad
        hidden_low[at, :] = grad.astype(low)
        return (
            carry[0] + jnp.sum(grad, axis=0, keepdims=True),
            carry[1] + gain_sum[None],
            carry[2] + shift_sum[None],
        )

    sums = lax.fori_loop(0, CH // BLOCK, last_step, (zero, zero, zero))
    for n in range(3):
        sums_ref[4 + n : 5 + n, :] = sums[n]
        sums_ref[7 + n : 8 + n, :] = second_sums[n : n + 1, :]
    sums_ref[10:16, :] = jnp.zeros((6, width), jnp.float32)
    for copy in copies:
        copy.wait()
    for source, pack in enumerate((gc_own, gc_far)):
        for pair in range(heads // 2):
            both = nt(hidden_low[...], outs[source, pair * 128 : pair * 128 + 128, :])
            top, bottom = both[:half], both[half:]
            lanes = low_half(top)
            pack[2 * pair] = jnp.where(lanes, top, pltpu.roll(bottom, HD, 1)).astype(low)
            pack[2 * pair + 1] = jnp.where(lanes, pltpu.roll(top, HD, 1), bottom).astype(low)


def dense_call(kernel, name, in_specs, operands, weights, shapes, scratch, width):
    low = jnp.bfloat16
    vmem, anywhere = pl.BlockSpec(memory_space=pltpu.VMEM), pl.BlockSpec(memory_space=pl.ANY)
    return pl.pallas_call(
        kernel,
        in_specs=in_specs + [anywhere] * 10,
        out_specs=[vmem] * len(shapes),
        out_shape=[jax.ShapeDtypeStruct(shape, dtype) for shape, dtype in shapes],
        scratch_shapes=[
            pltpu.VMEM((4, width, width), low),
            pltpu.VMEM((4, width, width), low),
            pltpu.VMEM((2,) + weights[-1].shape, low),
        ]
        + scratch
        + [pltpu.SemaphoreType.DMA((12,))],
        compiler_params=pltpu.CompilerParams(vmem_limit_bytes=VMEM_LIMIT),
        cost_estimate=pl.CostEstimate(
            flops=8 * CH * width * width, bytes_accessed=8 << 20, transcendentals=0
        ),
        name=name,
    )(*operands, *weights)


def forward_rows(side, pack, layer_in, cotangent, vectors, biases, weights):
    width = layer_in.shape[1]
    units = 4 * width
    low = jnp.bfloat16
    vmem, anywhere = pl.BlockSpec(memory_space=pltpu.VMEM), pl.BlockSpec(memory_space=pl.ANY)
    return dense_call(
        forward_kernel,
        "forward_rows",
        [pl.BlockSpec(memory_space=pltpu.SMEM), vmem, anywhere, anywhere, vmem, vmem],
        (side, pack, layer_in, cotangent, vectors, biases),
        weights,
        [
            ((CH, width), low),
            ((CH, width), low),
            ((CH, width), low),
            ((CH, units), low),
            ((CH, units), low),
            ((CH, width), low),
            ((CH, width), jnp.float32),
            ((CH, width), jnp.float32),
            ((CH, 128), jnp.float32),
            ((3, width), jnp.float32),
        ],
        [
            pltpu.VMEM((CH, width), low),
            pltpu.VMEM((CH, width), low),
            pltpu.VMEM((CH, width), jnp.float32),
            pltpu.VMEM((CH, width), jnp.float32),
        ],
        width,
    )


def backward_rows(
    place, slopes, second_low, grad_second, normed_one, inv_one, gain, second_sums, heads, weights
):
    width = second_low.shape[1]
    units = 4 * width
    low = jnp.bfloat16
    return dense_call(
        backward_kernel,
        "backward_rows",
        [pl.BlockSpec(memory_space=pltpu.SMEM)] + [pl.BlockSpec(memory_space=pltpu.VMEM)] * 7,
        (place, slopes, second_low, grad_second, normed_one, inv_one, gain, second_sums),
        weights,
        [
            ((CH, units), low),
            ((CH, width), jnp.float32),
            ((CH, width), low),
            ((heads, CH // 2, 128), low),
            ((heads, CH // 2, 128), low),
            ((16, width), jnp.float32),
        ],
        [pltpu.VMEM((CH, width), jnp.float32)],
        width,
    )


def project_back_kernel(
    side_ref, near_ref, kv_ref, layer_t, w_ref, hidden_ref, *refs
):
    grad_w, far_out, own_out, sums_ref, grad_q, grad_k, grad_v = refs
    low = jnp.bfloat16
    side = side_ref[0]
    half = CH // 2
    heads = kv_ref.shape[0]
    near_row = pl.multiple_of(side * CH, CH)
    far_row = pl.multiple_of((1 - side) * CH, CH)
    for pair in range(heads // 2):
        cols = slice(pair * 128, pair * 128 + 128)
        for pack, base in ((near_ref, near_row), (kv_ref.at[:, 2 * CH :], far_row)):
            first, first_roll = unfold(pack[2 * pair])
            second, second_roll = unfold(pack[2 * pair + 1])
            lanes = low_half(first)
            grad_q[pl.ds(base, half), cols] = jnp.where(lanes, first, second_roll).astype(low)
            grad_q[pl.ds(base + half, half), cols] = jnp.where(lanes, first_roll, second).astype(low)
        for r in range(0, 2 * CH, half):
            rows = slice(r, r + half)
            first, first_roll = unfold(kv_ref[2 * pair, rows, :])
            second, second_roll = unfold(kv_ref[2 * pair + 1, rows, :])
            lanes = low_half(first)
            grad_k[rows, cols] = jnp.where(lanes, first, second_roll).astype(low)
            grad_v[rows, cols] = jnp.where(lanes, first_roll, second).astype(low)
    parts = (grad_q, grad_k, grad_v)
    width = layer_t.shape[0]
    own_width = width // 2
    near_cols = pl.ds(pl.multiple_of(side * own_width, own_width), own_width)
    far_cols = pl.ds(pl.multiple_of((1 - side) * own_width, own_width), own_width)
    far = own = None
    for n, part in enumerate(parts):
        far_term, own_term = nt(part[...], w_ref[n, far_cols, :]), nt(part[...], w_ref[n, near_cols, :])
        far = far_term if far is None else far + far_term
        own = own_term if own is None else own + own_term
    far_out[...] = far.astype(low)
    own_out[...] = own
    near_rows = pl.ds(near_row, CH)
    far_out[near_rows, :] = (far_out[near_rows, :].astype(jnp.float32) + hidden_ref[:, far_cols]).astype(low)
    own_out[near_rows, :] += hidden_ref[:, near_cols]
    count, _, piece, _ = grad_w.shape
    for n, part in enumerate(parts):
        total = mm(layer_t[...], part[...]).astype(low)
        grad_w[:, n] = total.reshape(count, piece, total.shape[1])
    sums_ref[0:1, :] = jnp.sum(grad_q[...].astype(jnp.float32), axis=0, keepdims=True)
    sums_ref[1:2, :] = jnp.sum(grad_v[...].astype(jnp.float32), axis=0, keepdims=True)


def project_back(side, near, kv, layer_t, weight, hidden, pieces):
    heads = kv.shape[0]
    cols = heads * HD
    width, rows = layer_t.shape
    low = jnp.bfloat16
    vmem = pl.BlockSpec(memory_space=pltpu.VMEM)
    return pl.pallas_call(
        project_back_kernel,
        in_specs=[pl.BlockSpec(memory_space=pltpu.SMEM)] + [vmem] * 5,
        out_specs=[vmem] * 4,
        out_shape=[
            jax.ShapeDtypeStruct((pieces, 3, width // pieces, cols), low),
            jax.ShapeDtypeStruct((rows, width // 2), low),
            jax.ShapeDtypeStruct((rows, width // 2), jnp.float32),
            jax.ShapeDtypeStruct((2, cols), jnp.float32),
        ],
        scratch_shapes=[pltpu.VMEM((rows, cols), low)] * 3,
        compiler_params=pltpu.CompilerParams(vmem_limit_bytes=40 * 1024 * 1024),
        cost_estimate=pl.CostEstimate(
            flops=2 * rows * width * cols, bytes_accessed=8 << 20, transcendentals=0
        ),
        name="project_back",
    )(side, near, kv, layer_t, weight, hidden)


def weight_kernel(kept, place_ref, first_low, grad_pres, ctx_ref, hidden_low, *refs):
    got_ref = refs[0] if kept else None
    out_ref, first_t = refs[-2:]
    far = pl.program_id(0)
    side, core = place_ref[0], place_ref[1]
    width, cols = first_t.shape[0], ctx_ref.shape[1] // 2

    @pl.when(far == 0)
    def _():
        first_t[...] = first_low[...].T

    slot = (0 if kept else 2) + jnp.where(far == 0, side, 1 - side)
    for c in range(0, width, TILE):
        at = pl.ds(pl.multiple_of(slot * width + c, TILE), TILE)
        total = mm(first_t[...], grad_pres[:, at])
        if kept:
            total += got_ref[0, :width, c : c + TILE].astype(jnp.float32)
        out_ref[0, :width, c : c + TILE] = total.astype(jnp.bfloat16)
    part = cols // 2
    start = far * cols + (core if kept else 1 - core) * part
    total = tn(ctx_ref[:, pl.ds(pl.multiple_of(start, part), part)], hidden_low[...])
    if kept:
        total += got_ref[0, width:, :].astype(jnp.float32)
    out_ref[0, width:, :] = total.astype(jnp.bfloat16)


def weight_grads(place, first_low, grad_pres, ctx_rows, hidden_low, got=None):
    kept = got is not None
    rows, width = first_low.shape
    height = width + ctx_rows.shape[1] // 4
    vmem = pl.BlockSpec(memory_space=pltpu.VMEM)
    block = pl.BlockSpec((1, height, width), lambda n: (n, 0, 0))
    return pl.pallas_call(
        functools.partial(weight_kernel, kept),
        grid=(2,),
        in_specs=[pl.BlockSpec(memory_space=pltpu.SMEM)] + [vmem] * 4 + ([block] if kept else []),
        out_specs=block,
        out_shape=jax.ShapeDtypeStruct((2, height, width), jnp.bfloat16),
        scratch_shapes=[pltpu.VMEM((width, rows), jnp.bfloat16)],
        compiler_params=pltpu.CompilerParams(vmem_limit_bytes=40 * 1024 * 1024),
        cost_estimate=pl.CostEstimate(
            flops=4 * rows * width * height, bytes_accessed=12 << 20, transcendentals=0
        ),
        name="weight_grads",
    )(place, first_low, grad_pres, ctx_rows, hidden_low, *((got,) if kept else ()))


def fast_local(
    layer_in,
    slot_stretch,
    seq_stretches,
    w_qkv,
    qv_bias,
    w_out,
    out_bias,
    norm1_gain,
    norm1_shift,
    w_up,
    up_bias,
    w_down,
    down_bias,
    norm2_gain,
    norm2_shift,
    cotangent,
):
    width = layer_in.shape[1]
    cols = w_qkv.shape[2]
    heads = cols // HD
    units = w_up.shape[1]
    half = units // 2
    side = lax.axis_index("head")
    core = lax.axis_index("core")
    far_place = jnp.stack([core, 1 - side]).astype(jnp.int32)
    near_place = jnp.stack([core, side]).astype(jnp.int32)
    side_vec = side.reshape(1).astype(jnp.int32)
    tables = (slot_stretch, seq_stretches)
    low = jnp.bfloat16

    w_three = w_qkv.transpose(1, 0, 2)
    layer_t = layer_in.T
    send_kv, send_far, send_near = project(side_vec, layer_in, w_three, qv_bias)
    send_kv, w_up, w_down, w_out, up_bias = lax.optimization_barrier(
        (send_kv, w_up, w_down, w_out, up_bias)
    )
    own_kv = spread(send_kv)
    low_slices = [
        lax.dynamic_slice_in_dim(array, place * half, half, axis)
        for array, axis in ((w_up, 1), (w_down, 0), (up_bias, 0))
        for place in (core, 1 - core)
    ]
    up_far = swap_across(low_slices[0], "head")
    own_kv, low_slices, w_out, up_far = lax.optimization_barrier(
        (own_kv, low_slices, w_out, up_far)
    )
    other_kv = swap_across(own_kv, "core")
    own_keys = own_kv.reshape(2 * heads, CH, 128)
    other_keys = other_kv.reshape(2 * heads, CH, 128)

    q_far = spread(send_far)
    q_near = spread(send_near)

    downs, biases = (
        (low_slices[n], low_slices[n + 1], swap_across(low_slices[n], "head")) for n in (2, 4)
    )
    ups, down_far = low_slices[:2], downs[2]
    w_out_far = swap_across(w_out, "head")
    ctx_far, ctx_t_far, lse_far = attend(*tables, far_place, q_far, own_keys, other_keys)
    q_near, ctx_far, down_far = lax.optimization_barrier((q_near, ctx_far, down_far))
    ctx_other = swap_across(ctx_far, "head")
    ctx_near, ctx_t_near, lse_near = attend(*tables, near_place, q_near, own_keys, other_keys)

    def row_major(pack):
        block = pack.reshape(heads, CH // 2, 2, HD).transpose(2, 1, 0, 3)
        return block.reshape(CH, cols)

    ctx_near, ctx_other, up_far, down_far, w_out_far, bias_far = lax.optimization_barrier(
        (ctx_near, ctx_other, up_far, down_far, w_out_far, biases[2])
    )
    ctx_pack = spread(jnp.concatenate([ctx_near, ctx_other], axis=1))
    up_parts = [ups[0], ups[1], up_far, swap_across(up_far, "core")]
    down_parts = [downs[0], downs[1], down_far, swap_across(down_far, "core")]
    up_biases = [biases[0], biases[1], bias_far, swap_across(bias_far, "core")]
    vectors = jnp.stack([out_bias, norm1_gain, norm1_shift, down_bias, norm2_gain, norm2_shift])
    vectors = vectors.astype(jnp.float32)
    weights = (*up_parts, *down_parts, w_out, w_out_far)
    is_low = side == 0
    own_biases, far_biases = jnp.stack(up_biases[:2]), jnp.stack(up_biases[2:])
    biases = jnp.stack(
        [jnp.where(is_low, own_biases, far_biases), jnp.where(is_low, far_biases, own_biases)],
        axis=1,
    )
    (
        out_rows,
        ctx_rows,
        first_low,
        acts,
        slopes,
        second_low,
        grad_second,
        normed_one,
        inv_one,
        second_sums,
    ) = forward_rows(
        side_vec,
        ctx_pack,
        layer_in,
        cotangent,
        vectors,
        biases.astype(jnp.float32).reshape(4, 1, half),
        weights,
    )
    is_low = side == 0

    is_first = core == 0
    row = lax.axis_index("y")

    def add_low(kept, got):
        return (kept.astype(jnp.float32) + got.astype(jnp.float32)).astype(low)

    def on_chip(pair):
        return add_low(pair[0], swap_across(pair[1].astype(low), "core"))

    def halves(block, bit):
        size = block.shape[0] // 2
        return (
            lax.dynamic_slice_in_dim(block, bit * size, size, 0),
            lax.dynamic_slice_in_dim(block, (1 - bit) * size, size, 0),
        )

    def partner(block, step):
        if step == "y":
            return swap_across(block, "y")
        hop = 1 if step == "z_near" else 2
        return lax.ppermute(block, "z", [(n, n ^ hop) for n in range(lax.axis_size("z"))])

    place_in_z = lax.axis_index("z")
    bits = {"y": row, "z_near": place_in_z % 2, "z_far": place_in_z // 2}

    def reduce_send(block, step):
        kept, gone = halves(block, bits[step])
        return kept, partner(gone, step)

    def reduce_step(block, step):
        return add_low(*reduce_send(block, step))

    def gather_step(block, step):
        return in_order(bits[step] == 0, block, partner(block, step), 0)

    def scatter_sum(block):
        return lax.psum_scatter(block, ("head", "z", "y"), scatter_dimension=0, tiled=True)

    def collect(block):
        return lax.all_gather(block, ("z", "y"), axis=0, tiled=True)

    def sum_over(vector, steps):
        for step in steps:
            if step in ("core", "head"):
                vector = vector + swap_across(vector, step)
            else:
                vector = vector + partner(vector, step)
        return vector

    def in_order(bit, mine, rest, axis):
        return jnp.concatenate(
            [jnp.where(bit, mine, rest), jnp.where(bit, rest, mine)], axis=axis
        )

    def join(mine, step, axis):
        rest = partner(mine, step)
        mine_far, rest_far = swap_across(mine, "core"), swap_across(rest, "core")
        bit = bits[step] == 0
        own, other = in_order(bit, mine, rest, 0), in_order(bit, mine_far, rest_far, 0)
        return in_order(is_first, own, other, axis).astype(jnp.float32)

    half_rows = cols // 2

    def parts_of(block):
        return [block[:, n * width : (n + 1) * width] for n in range(4)]

    pair = 2 * width

    down_sum = on_chip([tn(acts[:, n : n + pair], second_low) for n in (0, pair)])
    down_sum = down_sum.reshape(2, width, width)
    down_own = lax.dynamic_index_in_dim(down_sum, side, 0, keepdims=False)
    down_far = lax.dynamic_index_in_dim(down_sum, 1 - side, 0, keepdims=False)
    down_far, grad_second = lax.optimization_barrier((down_far, grad_second))
    down_got = swap_across(down_far, "head")
    side_core = jnp.stack([side, core]).astype(jnp.int32)
    grad_pres, grad_hidden, hidden_low, gc_own, gc_far, small = backward_rows(
        side_core,
        slopes,
        second_low,
        grad_second,
        normed_one,
        inv_one,
        vectors[1:2],
        second_sums,
        heads,
        weights,
    )
    gc_in = swap_across(gc_far, "head")
    g_near = spread(gc_own)
    operands = (side_core, first_low, grad_pres, ctx_rows, hidden_low)
    both_sent, down_got = lax.optimization_barrier((weight_grads(*operands), down_got))
    both_got = swap_across(both_sent, "core")
    both_sum = weight_grads(*operands, both_got)
    both_own, both_far = both_sum[0], both_sum[1]

    down_kept, down_sent = halves(add_low(down_own, down_got), bits["y"])
    g_near, gc_in, both_far, down_sent = lax.optimization_barrier(
        (g_near, gc_in, both_far, down_sent)
    )
    both_got = swap_across(both_far, "head")
    small_got = swap_across(small, "core")
    down_got = partner(down_sent, "y")
    g_far = spread(gc_in)
    dq_near, part_grad = attend_back(
        tables, near_place, q_near, g_near, ctx_t_near, lse_near, own_keys, other_keys
    )
    part_grad, g_far, down_got, both_got, small_got = lax.optimization_barrier(
        (part_grad, g_far, down_got, both_got, small_got)
    )
    both_sum = add_low(both_own, both_got)
    down_kept, down_sent = halves(add_low(down_kept, down_got), bits["z_near"])
    small = small + small_got
    part_grad, both_sum, small, down_sent = lax.optimization_barrier(
        (part_grad, both_sum, small, down_sent)
    )
    both_sum = lax.psum_scatter(both_sum, ("z", "y"), scatter_dimension=0, tiled=True)
    small_got = swap_across(small, "head")
    down_got = partner(down_sent, "z_near")
    dq_far, own_grad, other_grad = attend_back(
        tables, far_place, q_far, g_far, ctx_t_far, lse_far, own_keys, other_keys, part_grad
    )
    dq_near = spread(dq_near)
    own_grad, other_grad, dq_far, dq_near, small_got, down_got = lax.optimization_barrier(
        (own_grad, other_grad, dq_far, dq_near, small_got, down_got)
    )
    kv_grad = add_low(own_grad, swap_across(other_grad, "core"))
    kv_grad = jnp.concatenate([kv_grad.reshape(heads, 2 * CH, 128), dq_far], axis=1)
    kv_grad, both_sum = lax.optimization_barrier((kv_grad, both_sum))
    kv_grad = spread(kv_grad)
    small = small + small_got
    small_got = partner(small, "z_near")
    down_sum = reduce_step(add_low(down_kept, down_got), "z_far")
    out_other = swap_across(out_rows, "head")
    kv_grad, small_got, both_sum, down_sum, out_other = lax.optimization_barrier(
        (kv_grad, small_got, both_sum, down_sum, out_other)
    )
    both_sum = collect(both_sum)
    small = small + small_got
    small_got = partner(small, "y")
    down_sum = gather_step(down_sum, "z_far")
    deep = lax.axis_size("z")
    grad_w, far_part, own_part, grad_qv = project_back(
        side_vec, dq_near, kv_grad, layer_t, w_three, grad_hidden, 4 * deep
    )
    arrived = swap_across(far_part, "head")
    kept, gone = halves(grad_w, core)
    kept, gone = halves(add_low(kept, swap_across(gone, "core")), row)
    kept = add_low(kept, swap_across(gone, "y"))
    pieces = lax.all_to_all(kept, "z", 0, 0, tiled=True)
    layer_out_pair = jnp.stack([out_rows, out_other])
    layer_out = jnp.where(is_low, layer_out_pair, layer_out_pair[::-1]).reshape(2 * CH, width)
    small = small + small_got
    down_sum = gather_step(down_sum, "z_near")
    grad_qv = sum_over(grad_qv.reshape(-1, 128), ("core", "y"))
    small_got = partner(small, "z_far")
    pieces, grad_qv, both_sum, down_sum, arrived, small_got = lax.optimization_barrier(
        (pieces, grad_qv, both_sum, down_sum, arrived, small_got)
    )
    small = small + small_got
    mine = jnp.sum(pieces.astype(jnp.float32), axis=0).astype(low)
    every = lax.all_to_all(jnp.broadcast_to(mine[None], pieces.shape), "z", 0, 0, tiled=True)
    bit = bits["y"] == 0
    grad_down = join(down_sum, "y", 0)
    both_far = swap_across(both_sum, "core")
    grad_up = in_order(is_first, both_sum[:width], both_far[:width], 1).astype(jnp.float32)
    grad_out = in_order(is_first, both_sum[width:], both_far[width:], 0).astype(jnp.float32)
    grad_qv = sum_over(grad_qv, ("z_near", "z_far")).reshape(2, cols)
    small = small.reshape(-1)
    grad_up_bias = lax.dynamic_slice_in_dim(small, side * units, units)
    vectors = small[2 * units : 2 * units + 6 * width].reshape(6, width)
    every, grad_up, grad_out = lax.optimization_barrier((every, grad_up, grad_out))
    every = in_order(bit, every, swap_across(every, "y"), 0)
    every = in_order(is_first, every, swap_across(every, "core"), 0)
    grad_qkv = every.astype(jnp.float32).transpose(0, 2, 1, 3).reshape(width, 3, cols)
    grad_in = own_part + arrived.astype(jnp.float32)
    return (
        layer_out,
        grad_in,
        grad_qkv,
        grad_qv,
        grad_out,
        vectors[0],
        vectors[1],
        vectors[2],
        grad_up,
        grad_up_bias,
        grad_down,
        vectors[3],
        vectors[4],
        vectors[5],
    )


def solution(mesh):
    batch, head = mesh.shape["batch"], mesh.shape["head"]

    def whole(*arrays):
        tokens, width = arrays[0].shape
        heads = arrays[3].shape[2] // head // HD
        fits = (
            head == 2
            and batch == 2 * heads
            and tokens == batch * 2 * CH
            and arrays[9].shape[1] % (4 * 128) == 0
        )
        if fits:
            split = Mesh(mesh.devices.reshape(batch // 4, 2, 2, head), ("z", "y", "core", "head"))
            return run(fast_local, split, ("z", "y", "core"))(*arrays)
        return run(local, mesh, "batch")(*arrays)

    return whole


def run(body, mesh, rows):
    in_specs = (
        P(rows, None),
        P(),
        P(),
        P(None, None, "head"),
        P(None, "head"),
        P("head", None),
        P(),
        P(),
        P(),
        P(None, "head"),
        P("head"),
        P("head", None),
        P(),
        P(),
        P(),
        P(rows, None),
    )
    out_specs = (
        P(rows, None),
        P(rows, "head"),
        P(None, None, "head"),
        P(None, "head"),
        P("head", None),
        P(),
        P(),
        P(),
        P(None, "head"),
        P("head"),
        P("head", None),
        P(),
        P(),
        P(),
    )
    return jax.shard_map(body, mesh=mesh, in_specs=in_specs, out_specs=out_specs, check_vma=False)
```
